256 devices in a mesh: dp: 8 (over y, x_hi), ctx: 32 (over x_lo, z, core).
Axes of the slice: x: 4 (x_hi: 2, x_lo: 2; x = x_hi * 2 + x_lo), y: 4, z: 8, core: 2. Of those that a mesh axis runs over, the one named last changes fastest.
Arguments:
- query_rows: bfloat16 [8, 4096, 2048], P('dp', 'ctx'), may hold values from -6 to 6
- key_rows: bfloat16 [8, 4096, 2048], P('dp', 'ctx'), may hold values from -6 to 6
- value_rows: bfloat16 [8, 4096, 2048], P('dp', 'ctx'), may hold values from -6 to 6
- norm_gain: float32 [2048], replicated, may hold values from 0.1 to 1.9
- out_weight: bfloat16 [2048, 2048], P('ctx'), may hold values from -0.125 to 0.125
- cotangent: bfloat16 [8, 4096, 2048], P('dp', 'ctx'), may hold values from -6 to 6
Outputs:
- mixed: bfloat16 [8, 4096, 2048], P('dp', 'ctx')
- grad_queries: bfloat16 [8, 4096, 2048], P('dp', 'ctx')
- grad_keys: bfloat16 [8, 4096, 2048], P('dp', 'ctx')
- grad_values: bfloat16 [8, 4096, 2048], P('dp', 'ctx')
- grad_weight: float32 [2048, 2048], P('ctx')
The draws below stay inside these ranges and needn't reach their ends.
All inputs are finite; a program needn't handle non-finite values.
Results may differ from the reference program's by a relative error of at most 0.025.
Values may be sent and summed in bfloat16 or wider, within the bound.
A program may use at most 192 MiB of HBM per device.

```python
import math
import jax
import jax.numpy as jnp
from jax import lax

HEADS = 16
HEAD = 128
D = 2048
SPAN = 128
SEQS = 8
LEN = 4096


def steps_of(key, extent, split, least, top_value):
    def one(axis_at, parts):
        heights = jax.random.uniform(jax.random.fold_in(jax.random.fold_in(key, 6), axis_at), (parts,), jnp.float32, least / len(split), top_value / len(split))
        return jnp.repeat(jnp.exp(heights), extent[axis_at] // parts).reshape((-1,) + (1,) * (len(extent) - axis_at - 1))

    factor_of = one(*split[0])
    for cut in split[1:]:
        factor_of = factor_of * one(*cut)
    return factor_of


def scatter_about(rng, shape, spread, reach, cuts=(), held_as=jnp.bfloat16):
    drawn = spread * jax.random.normal(rng, shape, jnp.float32)
    if cuts:
        drawn = drawn * steps_of(rng, shape, cuts, -0.22, 0.18)
    return jnp.clip(drawn, -reach, reach).astype(held_as)


def setup_inputs(seed: int = 0) -> dict:
    seeds = jax.random.split(jax.random.key(seed), 7)
    return {
        "query_rows": scatter_about(seeds[0], (SEQS, LEN, D), 1.0, 6.0, ((0, 8), (1, 32))),
        "key_rows": scatter_about(seeds[1], (SEQS, LEN, D), 1.0, 6.0, ((0, 8), (1, 32))),
        "value_rows": scatter_about(seeds[2], (SEQS, LEN, D), 1.0, 6.0, ((0, 8), (1, 32))),
        "norm_gain": jnp.clip(1.0 + 0.18 * jax.random.normal(seeds[3], (D,), jnp.float32), 0.1, 1.9),
        "out_weight": scatter_about(seeds[4], (D, D), D ** -0.5, 0.125, ((0, 32),)),
        "cotangent": scatter_about(seeds[5], (SEQS, LEN, D), 1.0, 6.0, ((0, 8), (1, 32))),
    }


epsilon = 1e-06
highest_precision = lax.Precision.HIGHEST

def feature(values):
    wide = values.astype(jnp.float32)
    return jnp.where(wide > 0, wide + 1.0, jnp.exp(jnp.minimum(wide, 0.0))).astype(jnp.bfloat16)

def feature_slope(values):
    wide = values.astype(jnp.float32)
    return jnp.where(wide > 0, 1.0, jnp.exp(jnp.minimum(wide, 0.0)))

def round_trip(values):
    return lax.optimization_barrier(values.astype(jnp.bfloat16)).astype(jnp.float32)

def one_sequence(query_seq, key_seq, value_seq, norm_gain, out_weight, upstream):
    length = query_seq.shape[0]
    blocks = length // SPAN
    shape4 = (blocks, SPAN, HEADS, HEAD)
    query_feat = feature(query_seq).astype(jnp.float32).reshape(shape4)
    key_feat = feature(key_seq).astype(jnp.float32).reshape(shape4)
    value_wide_rows = value_seq.astype(jnp.float32).reshape(shape4)
    local_state = jnp.einsum('cshk,cshv->chkv', key_feat, value_wide_rows, precision=highest_precision)
    running = jnp.cumsum(local_state, axis=0)
    prefix_state = jnp.concatenate([jnp.zeros_like(local_state[:1]), running[:-1]], axis=0)
    causal = jnp.tril(jnp.ones((SPAN, SPAN), dtype=bool))
    scores = jnp.einsum('cthd,cshd->chts', query_feat, key_feat, precision=highest_precision)
    probs = round_trip(jnp.where(causal, scores, 0.0))
    attended_output = jnp.einsum('chts,cshv->cthv', probs, value_wide_rows, precision=highest_precision)
    attended_output = attended_output + jnp.einsum('cthk,chkv->cthv', query_feat, prefix_state, precision=highest_precision)
    inverse = lax.rsqrt(lax.optimization_barrier(jnp.mean(attended_output * attended_output, axis=-1, keepdims=True)) + epsilon)
    gain_heads = norm_gain.astype(jnp.float32).reshape(HEADS, HEAD)
    normed = (attended_output * inverse * gain_heads).reshape(length, D).astype(jnp.bfloat16)
    mixed = jnp.dot(normed, out_weight, preferred_element_type=jnp.float32).astype(jnp.bfloat16)
    d_normed = lax.dot_general(upstream, out_weight, (((1,), (1,)), ((), ())), preferred_element_type=jnp.float32).reshape(shape4)
    scaled = d_normed * gain_heads
    attended_gradient = round_trip(inverse * (scaled - attended_output * inverse * inverse * lax.optimization_barrier(jnp.mean(scaled * attended_output, axis=-1, keepdims=True))))
    grad_local = jnp.einsum('cthk,cthv->chkv', query_feat, attended_gradient, precision=highest_precision)
    backward_run = jnp.cumsum(grad_local[::-1], axis=0)[::-1]
    suffix_state = jnp.concatenate([backward_run[1:], jnp.zeros_like(grad_local[:1])], axis=0)
    d_probs = round_trip(jnp.where(causal, jnp.einsum('cthv,cshv->chts', attended_gradient, value_wide_rows, precision=highest_precision), 0.0))
    query_gradient = jnp.einsum('chts,cshk->cthk', d_probs, key_feat, precision=highest_precision)
    query_gradient = query_gradient + jnp.einsum('cthv,chkv->cthk', attended_gradient, prefix_state, precision=highest_precision)
    key_gradient = jnp.einsum('chts,cthk->cshk', d_probs, query_feat, precision=highest_precision)
    key_gradient = key_gradient + jnp.einsum('cshv,chkv->cshk', value_wide_rows, suffix_state, precision=highest_precision)
    value_gradient = jnp.einsum('chts,cthv->cshv', probs, attended_gradient, precision=highest_precision)
    value_gradient = value_gradient + jnp.einsum('cshk,chkv->cshv', key_feat, suffix_state, precision=highest_precision)
    grad_queries = (query_gradient.reshape(length, D) * feature_slope(query_seq)).astype(jnp.bfloat16)
    grad_keys = (key_gradient.reshape(length, D) * feature_slope(key_seq)).astype(jnp.bfloat16)
    grad_values = value_gradient.reshape(length, D).astype(jnp.bfloat16)
    partial_grad = lax.dot_general(normed, upstream, (((0,), (0,)), ((), ())), preferred_element_type=jnp.float32)
    return (mixed, grad_queries, grad_keys, grad_values, partial_grad)

def reference(query_rows, key_rows, value_rows, norm_gain, out_weight, cotangent):

    def per_sequence(total, pieces):
        query_seq, key_seq, value_seq, upstream = pieces
        mixed, grad_queries, grad_keys, grad_values, partial_grad = one_sequence(query_seq, key_seq, value_seq, norm_gain, out_weight, upstream)
        return (total + partial_grad, (mixed, grad_queries, grad_keys, grad_values))
    total, stacked = lax.scan(per_sequence, jnp.zeros((D, D), jnp.float32), (query_rows, key_rows, value_rows, cotangent))
    grad_weight = total * (1.0 / math.sqrt(SEQS * LEN))
    return (stacked[0], stacked[1], stacked[2], stacked[3], grad_weight)
```

```python
import math

import jax
import jax.numpy as jnp
from jax import lax
from jax.experimental import pallas as pl
from jax.experimental.pallas import tpu as pltpu
from jax.sharding import PartitionSpec as P

MESH = pl.DeviceIdType.MESH
F32 = jnp.float32
BF16 = jnp.bfloat16
HEAD = 128
EPSILON = 1e-06
NZ = 8
NX = 4
NY = 4
CHIPS = 16
HALF = 1024


def dot(a, b, ca, cb):
    return lax.dot_general(a, b, (((ca,), (cb,)), ((), ())), preferred_element_type=F32)


def rcopy(src, dst, send, recv, device):
    return pltpu.make_async_remote_copy(
        src_ref=src, dst_ref=dst, send_sem=send, recv_sem=recv, device_id=device, device_id_type=MESH
    )


def exp_low(wide):
    return jnp.exp(jnp.minimum(wide, 0.0))


def feature(values):
    wide = values.astype(F32)
    return jnp.where(wide > 0, wide + 1.0, exp_low(wide)).astype(BF16)


def slope(values):
    wide = values.astype(F32)
    return jnp.where(wide > 0, 1.0, exp_low(wide))


def kernel(
    loss_scale,
    q_ref, k_ref, v_ref, gain_ref, w_ref, cot_ref,
    mixed_ref, gq_ref, gk_ref, gv_ref, gw_ref,
    fq, fk, probs, att, dnorm, normed, datt, dfk, dgv, local, state,
    xsend, xrecv, pieces, got, back_out, back_in, psend, prefix, suffix,
    wfull, cotg, normg, gwf, gwt, xh_in, x_out, x_in, z_out, z_in, f_out, f_in,
    sx_s, sx_r, s1_s, s1_r, s2_s, s2_r, sp_s, sp_r,
    up_s, up_r, dn_s, dn_r, wx_s, wx_r, wp_s, wp_r,
    cu_s, cu_r, cd_s, cd_r, cp_s, cp_r,
    n_s, n_r, xa_s, xa_r, xb_s, xb_r, z_s, z_r, f_s, f_r,
):
    d = lax.axis_index("dp")
    i = lax.axis_index("ctx")
    c = i % 2
    j = i // 2
    z = j % NZ
    xl = j // NZ
    y = d // 2
    xh = d % 2
    x = xh * 2 + xl
    o = 1 - c
    partner = (d, j * 2 + o)

    def chip(jj):
        return (d, jj * 2 + c)

    def at_x(xx):
        return (y * 2 + xx // 2, ((xx % 2) * NZ + z) * 2 + c)

    def at_z(zz):
        return (d, (xl * NZ + zz) * 2 + c)

    def at_y(yy, cc):
        return (yy * 2 + xh, j * 2 + cc)

    def final_to(t):
        return (t, 8 * y + 4 * c + x)

    from_x = i % 4
    from_c = (i // 4) % 2
    from_d = (i // 8) * 2 + from_x // 2

    def final_from(zz):
        return (from_d, ((from_x % 2) * NZ + zz) * 2 + from_c)

    def same(device):
        return jnp.logical_and(device[0] == d, device[1] == i)

    barrier = pltpu.get_barrier_semaphore()

    def greet(device):
        pl.semaphore_signal(barrier, inc=1, device_id=device, device_id_type=MESH)

    def greet_maybe_self(device):
        @pl.when(jnp.logical_not(same(device)))
        def _():
            greet(device)

    for t in range(1, CHIPS):
        greet(chip((j + t) % CHIPS))
    greet(partner)
    for t in range(1, NX):
        greet(at_x((x + t) % NX))
    for t in range(1, NY):
        greet(at_y((y + t) % NY, 0))
        greet(at_y((y + t) % NY, 1))
    for t in range(8):
        greet_maybe_self(final_to(t))
        greet_maybe_self(final_from(t))

    def head(h):
        return pl.ds(pl.multiple_of(h * HEAD, HEAD), HEAD)

    def loop_a(h, _):
        cols = head(h)
        fq[:, cols] = feature(q_ref[:, cols])
        kf = feature(k_ref[:, cols])
        fk[:, cols] = kf
        local[h] = dot(kf, v_ref[:, cols], 0, 0)
        return 0

    lax.fori_loop(0, 16, loop_a, 0, unroll=2)

    selves = jnp.where(8 * y + 4 * c + x == i, 2, 0)
    pl.semaphore_wait(barrier, 15 + 1 + 3 + 6 + 16 - selves)

    left = pl.ds(0, HALF)
    right = pl.ds(HALF, HALF)

    pending = []

    def begin(copy):
        copy.start()
        pending.append(copy)
        return copy

    def wslot(zz):
        return (xl * NZ + zz) * 2 + c

    def oslot(zz):
        return ((1 - xl) * NZ + zz) * 2 + c

    near_x = (y * 2 + xh, ((1 - xl) * NZ + z) * 2 + c)
    far_x = (y * 2 + (1 - xh), ((1 - xl) * NZ + z) * 2 + c)
    z_up = at_z((z + 1) % NZ)
    z_dn = at_z((z + NZ - 1) % NZ)

    def wsrc(r, cols=None):
        if r == 0:
            return w_ref if cols is None else w_ref.at[:, cols]
        slot = wslot((z + r) % NZ)
        return wfull.at[slot] if cols is None else wfull.at[slot, :, cols]

    def wdst(r, cols=None):
        slot = wslot((z + r) % NZ)
        return wfull.at[slot] if cols is None else wfull.at[slot, :, cols]

    def w_up(k):
        cols = left if k == 3 else None
        r = (-k) % NZ
        return rcopy(wsrc(r, cols), wdst(r, cols), up_s.at[k], up_r.at[k], z_up)

    def w_dn(k):
        cols = right if k == 3 else None
        return rcopy(wsrc(k, cols), wdst(k, cols), dn_s.at[k], dn_r.at[k], z_dn)

    def w_up_wait(k):
        r = (-k - 1) % NZ
        cols = left if k == 3 else None
        ref = wdst(r, cols)
        rcopy(ref, ref, up_s.at[k], up_r.at[k], z_up).wait_recv()

    def w_dn_wait(k):
        cols = right if k == 3 else None
        ref = wdst(k + 1, cols)
        rcopy(ref, ref, dn_s.at[k], dn_r.at[k], z_dn).wait_recv()

    def w_near(r):
        begin(rcopy(wsrc(r, left), wdst(r, left), wx_s.at[r, 0], wx_r.at[r, 0], near_x))

    def w_far(r):
        begin(rcopy(wsrc(r, right), wdst(r, right), wx_s.at[r, 1], wx_r.at[r, 1], far_x))

    def w_pair(r):
        begin(rcopy(wsrc(r), wdst(r), wp_s.at[r], wp_r.at[r], partner))

    def w_first():
        begin(w_up(0))
        begin(w_dn(0))
        w_near(0)
        w_far(0)
        w_pair(0)

    def w_step(k):
        w_up_wait(k - 1)
        begin(w_up(k))
        w_dn_wait(k - 1)
        begin(w_dn(k))
        for r in ((-k) % NZ, k):
            w_near(r)
            w_far(r)
            w_pair(r)

    def w_last():
        w_up_wait(3)
        w_near(4)
        w_dn_wait(3)
        w_far(4)
        w_pair(4)

    def w_other(r):
        slot = oslot((z + r) % NZ)
        for a, cols in ((0, left), (1, right)):
            ref = wfull.at[slot, :, cols]
            rcopy(ref, ref, wx_s.at[r, a], wx_r.at[r, a], near_x).wait_recv()
        begin(rcopy(wfull.at[slot], wfull.at[slot], wp_s.at[8 + r], wp_r.at[8 + r], partner))

    def w_pair_wait():
        for r in range(16):
            zz = (z + r) % NZ
            side = xl if r < 8 else 1 - xl
            ref = wfull.at[(side * NZ + zz) * 2 + o]
            rcopy(ref, ref, wp_s.at[r], wp_r.at[r], partner).wait_recv()

    y_up = at_y((y + 1) % NY, c)
    y_dn = at_y((y + NY - 1) % NY, c)

    def cslot(r):
        return ((y + r) % NY) * 2 + c

    def c_first():
        own = cotg.at[cslot(0)]
        begin(rcopy(cot_ref, own, cu_s.at[0], cu_r.at[0], y_up))
        begin(rcopy(cot_ref, own, cd_s.at[0], cd_r.at[0], y_dn))
        begin(rcopy(cot_ref, own, cp_s.at[0], cp_r.at[0], partner))

    def c_pair(r):
        ref = cotg.at[cslot(r)]
        begin(rcopy(ref, ref, cp_s.at[r], cp_r.at[r], partner))

    def c_second():
        below = cotg.at[cslot(3)]
        rcopy(below, below, cu_s.at[0], cu_r.at[0], y_up).wait_recv()
        part = cotg.at[cslot(3), :, left]
        begin(rcopy(part, part, cu_s.at[1], cu_r.at[1], y_up))
        above = cotg.at[cslot(1)]
        rcopy(above, above, cd_s.at[0], cd_r.at[0], y_dn).wait_recv()
        part = cotg.at[cslot(1), :, right]
        begin(rcopy(part, part, cd_s.at[1], cd_r.at[1], y_dn))
        c_pair(3)
        c_pair(1)

    def c_third():
        a = cotg.at[cslot(2), :, left]
        rcopy(a, a, cu_s.at[1], cu_r.at[1], y_up).wait_recv()
        b = cotg.at[cslot(2), :, right]
        rcopy(b, b, cd_s.at[1], cd_r.at[1], y_dn).wait_recv()
        c_pair(2)

    def c_wait():
        for r in range(4):
            ref = cotg.at[((y + r) % NY) * 2 + o]
            rcopy(ref, ref, cp_s.at[r], cp_r.at[r], partner).wait_recv()

    own_heads = pl.ds(8 * c, 8)
    other_heads = pl.ds(8 * o, 8)

    def scan_pair(n):
        xsend[n] = local[other_heads].astype(BF16)
        begin(rcopy(xsend.at[n], xrecv.at[n], sx_s.at[n], sx_r.at[n], partner))

    def scan_spread(n):
        rcopy(xrecv.at[n], xrecv.at[n], sx_s.at[n], sx_r.at[n], partner).wait_recv()
        total = (local[own_heads] + xrecv[n].astype(F32)).astype(BF16)
        pieces[n] = total.reshape(CHIPS, 64, HEAD)
        for t in range(1, CHIPS):
            jj = (j + t) % CHIPS
            begin(rcopy(pieces.at[n, jj], got.at[n, j], s1_s.at[n, jj], s1_r.at[n, j], chip(jj)))
        got[n, j] = pieces[n, j]

    def scan_return(n):
        for t in range(1, CHIPS):
            jj = (j + t) % CHIPS
            ref = got.at[n, jj]
            rcopy(ref, ref, s1_s.at[n, jj], s1_r.at[n, jj], partner).wait_recv()
        total = jnp.zeros((64, HEAD), F32)
        order = range(CHIPS) if n == 0 else range(CHIPS - 1, -1, -1)
        for jj in order:
            back_out[n, jj] = total.astype(BF16)
            total = total + got[n, jj].astype(F32)
        for t in range(1, CHIPS):
            jj = (j + t) % CHIPS
            begin(rcopy(back_out.at[n, jj], back_in.at[n, j], s2_s.at[n, jj], s2_r.at[n, j], chip(jj)))
        back_in[n, j] = back_out[n, j]

    def scan_share(n, out):
        for t in range(1, CHIPS):
            jj = (j + t) % CHIPS
            ref = back_in.at[n, jj]
            rcopy(ref, ref, s2_s.at[n, jj], s2_r.at[n, jj], partner).wait_recv()
        mine = back_in[n].astype(F32).reshape(8, HEAD, HEAD)
        last = (c if n == 0 else o).astype(F32)
        psend[n] = (mine + (1.0 - last) * local[own_heads]).astype(BF16)
        begin(rcopy(psend.at[n], out.at[own_heads], sp_s.at[n], sp_r.at[n], partner))
        out[own_heads] = (mine + last * xrecv[n].astype(F32)).astype(BF16)

    def scan_wait(n, out):
        ref = out.at[other_heads]
        rcopy(ref, ref, sp_s.at[n], sp_r.at[n], partner).wait_recv()

    scan_pair(0)
    w_first()
    c_first()
    scan_spread(0)

    rows_at = lax.broadcasted_iota(jnp.int32, (HEAD, HEAD), 0)
    cols_at = lax.broadcasted_iota(jnp.int32, (HEAD, HEAD), 1)
    causal = rows_at >= cols_at

    def loop_b(h, _):
        cols = head(h)
        scores = dot(fq[:, cols], fk[:, cols], 1, 1)
        p = jnp.where(causal, scores, 0.0).astype(BF16)
        probs[h] = p
        att[:, cols] = dot(p, v_ref[:, cols], 1, 0)
        return 0

    lax.fori_loop(0, 16, loop_b, 0, unroll=2)
    wfull[i] = w_ref[...]
    cotg[cslot(0)] = cot_ref[...]

    w_step(1)
    scan_return(0)
    w_other(0)
    w_step(2)
    c_second()
    scan_share(0, prefix)
    w_other(7)
    w_other(1)
    w_step(3)
    scan_wait(0, prefix)
    w_other(6)
    w_other(2)
    w_last()
    c_third()
    for r in (5, 3, 4):
        w_other(r)
    w_pair_wait()

    def loop_c(h2, _):
        cols = pl.ds(pl.multiple_of(h2 * 256, 256), 256)
        rows = wfull[pl.ds(h2 * 4, 4)].reshape(256, 2048)
        dnorm[:, cols] = dot(cot_ref[...], rows, 1, 1) * gain_ref[:, cols]
        return 0

    lax.fori_loop(0, 8, loop_c, 0)

    def loop_d(h, _):
        cols = head(h)
        fqh = fq[:, cols]
        a = att[:, cols] + dot(fqh, prefix[h], 1, 0)
        inverse = lax.rsqrt(jnp.mean(a * a, axis=-1, keepdims=True) + EPSILON)
        ai = a * inverse
        normed[:, cols] = (ai * gain_ref[:, cols]).astype(BF16)
        s = dnorm[:, cols]
        m = jnp.mean(s * a, axis=-1, keepdims=True)
        g = (inverse * (s - ai * inverse * m)).astype(BF16)
        datt[:, cols] = g
        local[h] = dot(fqh, g, 0, 0)
        return 0

    lax.fori_loop(0, 16, loop_d, 0, unroll=2)

    me8 = y * 2 + c

    def block8(b):
        return pl.ds(pl.multiple_of(b * 256, 256), 256)

    scan_pair(1)
    for t in range(1, 8):
        b = (me8 + t) % 8
        begin(
            rcopy(
                normed.at[:, block8(b)], normg.at[me8], n_s.at[b], n_r.at[me8], at_y(b // 2, b % 2)
            )
        )
    normg[me8] = normed[:, block8(me8)]
    scan_spread(1)

    def loop_e(h, _):
        cols = head(h)
        g = datt[:, cols]
        vh = v_ref[:, cols]
        fkh = fk[:, cols]
        fqh = fq[:, cols]
        dp = jnp.where(causal, dot(g, vh, 1, 1), 0.0).astype(BF16)
        dfq = dot(dp, fkh, 1, 0) + dot(g, prefix[h], 1, 1)
        gq_ref[:, cols] = (dfq * slope(q_ref[:, cols])).astype(BF16)
        dfk[:, cols] = dot(dp, fqh, 0, 0)
        dgv[:, cols] = dot(probs[h], g, 0, 0)
        return 0

    lax.fori_loop(0, 16, loop_e, 0, unroll=2)

    c_wait()
    for t in range(1, 8):
        b = (me8 + t) % 8
        ref = normg.at[b]
        rcopy(ref, ref, n_s.at[b], n_r.at[b], partner).wait_recv()

    def loop_g(n, _):
        cols = pl.ds(pl.multiple_of(n * 512, 512), 512)
        a = normg[...].reshape(1024, 256)
        b = cotg[:, :, cols].reshape(1024, 512)
        tile = dot(a, b, 0, 0)
        gwf[:, :, cols] = tile.reshape(4, 64, 512)
        gwt[:, :, cols] = tile.astype(BF16).reshape(4, 64, 512)
        return 0

    lax.fori_loop(0, 4, loop_g, 0)

    x_up = at_x((x + 1) % NX)
    x_dn = at_x((x + 3) % NX)
    two = (x + 2) % NX
    begin(rcopy(gwt.at[two, :, left], xh_in.at[0], xa_s.at[0], xa_r.at[0], x_up))
    begin(rcopy(gwt.at[two, :, right], xh_in.at[1], xa_s.at[1], xa_r.at[1], x_dn))
    scan_return(1)
    for a, to in ((0, x_up), (1, x_dn)):
        rcopy(xh_in.at[a], xh_in.at[a], xa_s.at[a], xa_r.at[a], to).wait_recv()
    one_up = (x + 1) % NX
    one_dn = (x + 3) % NX
    x_out[0, :, left] = (gwf[one_up, :, left] + xh_in[0].astype(F32)).astype(BF16)
    x_out[0, :, right] = gwt[one_up, :, right]
    x_out[1, :, left] = gwt[one_dn, :, left]
    x_out[1, :, right] = (gwf[one_dn, :, right] + xh_in[1].astype(F32)).astype(BF16)
    begin(rcopy(x_out.at[0], x_in.at[0], xb_s.at[0], xb_r.at[0], x_up))
    begin(rcopy(x_out.at[1], x_in.at[1], xb_s.at[1], xb_r.at[1], x_dn))

    def loop_m(n, _):
        cols = pl.ds(pl.multiple_of(n * 512, 512), 512)
        rows = wfull[:, :, cols].reshape(2048, 512)
        mixed_ref[:, cols] = dot(normed[...], rows, 1, 0).astype(BF16)
        return 0

    lax.fori_loop(0, 4, loop_m, 0)

    scan_share(1, suffix)
    for a, to in ((0, x_up), (1, x_dn)):
        rcopy(x_in.at[a], x_in.at[a], xb_s.at[a], xb_r.at[a], to).wait_recv()
    total = gwf[x] + x_in[0].astype(F32) + x_in[1].astype(F32)
    for zz in range(NZ):
        z_out[zz] = total[:, zz * 256 : (zz + 1) * 256].astype(BF16)
    for t in range(1, NZ):
        zz = (z + t) % NZ
        begin(rcopy(z_out.at[zz], z_in.at[z], z_s.at[zz], z_r.at[z], at_z(zz)))
    z_in[z] = z_out[z]

    scan_wait(1, suffix)

    def loop_f(h, _):
        cols = head(h)
        s = suffix[h]
        gk = dfk[:, cols] + dot(v_ref[:, cols], s, 1, 1)
        gk_ref[:, cols] = (gk * slope(k_ref[:, cols])).astype(BF16)
        gv_ref[:, cols] = (dgv[:, cols] + dot(fk[:, cols], s, 1, 0)).astype(BF16)
        return 0

    lax.fori_loop(0, 16, loop_f, 0, unroll=2)

    for t in range(1, NZ):
        zz = (z + t) % NZ
        rcopy(z_in.at[zz], z_in.at[zz], z_s.at[zz], z_r.at[zz], partner).wait_recv()
    whole = z_in[0].astype(F32)
    for zz in range(1, NZ):
        whole = whole + z_in[zz].astype(F32)
    f_out[...] = whole.astype(BF16)
    for t in range(8):
        to = final_to(t)

        @pl.when(jnp.logical_not(same(to)))
        def _(to=to, t=t):
            rcopy(f_out, f_in.at[z], f_s.at[t], f_r.at[z], to).start()

        @pl.when(same(to))
        def _():
            f_in[z] = f_out[...]

    for copy in pending:
        copy.wait_send()
    for t in range(8):
        to = final_to(t)

        @pl.when(jnp.logical_not(same(to)))
        def _(to=to, t=t):
            rcopy(f_out, f_in.at[z], f_s.at[t], f_r.at[z], to).wait_send()

    for zz in range(NZ):
        source = final_from(zz)

        @pl.when(jnp.logical_not(same(source)))
        def _(source=source, zz=zz):
            rcopy(f_in.at[zz], f_in.at[zz], f_s.at[zz], f_r.at[zz], source).wait_recv()

        gw_ref[:, zz * 256 : (zz + 1) * 256] = f_in[zz].astype(F32) * loss_scale


def on_device(loss_scale, query_rows, key_rows, value_rows, norm_gain, out_weight, cotangent):
    length, width = query_rows.shape[1:]
    rows = out_weight.shape[0]
    vmem = pl.BlockSpec(memory_space=pltpu.VMEM)
    block = jax.ShapeDtypeStruct((length, width), BF16)
    dma = pltpu.SemaphoreType.DMA
    states = (16, HEAD, HEAD)
    scratch = [
        pltpu.VMEM((length, width), BF16),
        pltpu.VMEM((length, width), BF16),
        pltpu.VMEM(states, BF16),
        pltpu.VMEM((length, width), F32),
        pltpu.VMEM((length, width), F32),
        pltpu.VMEM((length, width), BF16),
        pltpu.VMEM((length, width), BF16),
        pltpu.VMEM((length, width), F32),
        pltpu.VMEM((length, width), F32),
        pltpu.VMEM(states, F32),
        pltpu.VMEM((8, HEAD), F32),
        pltpu.VMEM((2, 8, HEAD, HEAD), BF16),
        pltpu.VMEM((2, 8, HEAD, HEAD), BF16),
        pltpu.VMEM((2, CHIPS, 64, HEAD), BF16),
        pltpu.VMEM((2, CHIPS, 64, HEAD), BF16),
        pltpu.VMEM((2, CHIPS, 64, HEAD), BF16),
        pltpu.VMEM((2, CHIPS, 64, HEAD), BF16),
        pltpu.VMEM((2, 8, HEAD, HEAD), BF16),
        pltpu.VMEM(states, BF16),
        pltpu.VMEM(states, BF16),
        pltpu.VMEM((32, 64, width), BF16),
        pltpu.VMEM((8, length, width), BF16),
        pltpu.VMEM((8, length, 256), BF16),
        pltpu.VMEM((4, 64, width), F32),
        pltpu.VMEM((4, 64, width), BF16),
        pltpu.VMEM((2, 64, HALF), BF16),
        pltpu.VMEM((2, 64, width), BF16),
        pltpu.VMEM((2, 64, width), BF16),
        pltpu.VMEM((8, 64, 256), BF16),
        pltpu.VMEM((8, 64, 256), BF16),
        pltpu.VMEM((64, 256), BF16),
        pltpu.VMEM((8, 64, 256), BF16),
        dma((2,)), dma((2,)), dma((2, 16)), dma((2, 16)), dma((2, 16)), dma((2, 16)), dma((2,)), dma((2,)),
        dma((4,)), dma((4,)), dma((4,)), dma((4,)), dma((8, 2)), dma((8, 2)), dma((16,)), dma((16,)),
        dma((2,)), dma((2,)), dma((2,)), dma((2,)), dma((4,)), dma((4,)),
        dma((8,)), dma((8,)), dma((2,)), dma((2,)), dma((2,)), dma((2,)), dma((8,)), dma((8,)), dma((8,)), dma((8,)),
    ]

    def body(*refs):
        kernel(loss_scale, *refs)

    mixed, gq, gk, gv, gw = pl.pallas_call(
        body,
        out_shape=(block, block, block, block, jax.ShapeDtypeStruct((rows, width), F32)),
        in_specs=[vmem] * 6,
        out_specs=(vmem,) * 5,
        scratch_shapes=scratch,
        compiler_params=pltpu.CompilerParams(
            collective_id=0, has_side_effects=True, vmem_limit_bytes=60 * 1024 * 1024
        ),
        name="layer",
    )(query_rows[0], key_rows[0], value_rows[0], norm_gain.reshape(1, width), out_weight, cotangent[0])
    return mixed[None], gq[None], gk[None], gv[None], gw


def solution(mesh):
    positions = mesh.shape["dp"] * mesh.shape["ctx"] * HEAD
    loss_scale = 1.0 / math.sqrt(positions)

    def run(*args):
        return on_device(loss_scale, *args)

    split = P("dp", "ctx", None)
    return jax.shard_map(
        run,
        mesh=mesh,
        in_specs=(split, split, split, P(), P("ctx", None), split),
        out_specs=(split, split, split, split, P("ctx", None)),
        check_vma=False,
    )
```

```python
import math

import jax
import jax.numpy as jnp
from jax import lax
from jax.experimental import pallas as pl
from jax.experimental.pallas import tpu as pltpu
from jax.sharding import PartitionSpec as P

MESH = pl.DeviceIdType.MESH
F32 = jnp.float32
BF16 = jnp.bfloat16
HEAD = 128
EPSILON = 1e-06
NZ = 8
NX = 4
NY = 4
CHIPS = 16
HALF = 1024
CHUNKS = 2
CHUNK = 2048 // CHUNKS
PIECE = CHUNK // NZ


def dot(a, b, ca, cb):
    return lax.dot_general(a, b, (((ca,), (cb,)), ((), ())), preferred_element_type=F32)


def rcopy(src, dst, send, recv, device):
    return pltpu.make_async_remote_copy(
        src_ref=src, dst_ref=dst, send_sem=send, recv_sem=recv, device_id=device, device_id_type=MESH
    )


def exp_low(wide):
    return jnp.exp(jnp.minimum(wide, 0.0))


def feature(values):
    wide = values.astype(F32)
    return jnp.where(wide > 0, wide + 1.0, exp_low(wide)).astype(BF16)


def slope(values):
    wide = values.astype(F32)
    return jnp.where(wide > 0, 1.0, exp_low(wide))


def kernel(
    loss_scale,
    q_hbm, k_hbm, v_hbm, gain_ref, w_hbm, cot_hbm,
    mixed_ref, gq_ref, gk_ref, gv_ref, gw_ref,
    q_ref, k_ref, v_ref, w_ref, cot_ref, in_s,
    fq, fk, probs, att, dnorm, normed, datt, dfk, dgv, local, inverse,
    xsend, xrecv, pieces, got, back_out, back_in, psend, prefix, suffix,
    wfull, cotg, normg, gwf, gwt, xh_in, x_out, x_in, z_out, z_in, f_out, f_in,
    sx_s, sx_r, s1_s, s1_r, s2_s, s2_r, sp_s, sp_r,
    up_s, up_r, dn_s, dn_r, wx_s, wx_r, wp_s, wp_r,
    cu_s, cu_r, cd_s, cd_r, cp_s, cp_r,
    n_s, n_r, xa_s, xa_r, xb_s, xb_r, z_s, z_r, f_s, f_r,
):
    d = lax.axis_index("dp")
    i = lax.axis_index("ctx")
    c = i % 2
    j = i // 2
    z = j % NZ
    xl = j // NZ
    y = d // 2
    xh = d % 2
    x = xh * 2 + xl
    o = 1 - c
    partner = (d, j * 2 + o)

    def chip(jj):
        return (d, jj * 2 + c)

    def at_x(xx):
        return (y * 2 + xx // 2, ((xx % 2) * NZ + z) * 2 + c)

    def at_z(zz):
        return (d, (xl * NZ + zz) * 2 + c)

    def at_y(yy, cc):
        return (yy * 2 + xh, j * 2 + cc)

    def final_to(t):
        return (t, 8 * y + 4 * c + x)

    from_x = i % 4
    from_c = (i // 4) % 2
    from_d = (i // 8) * 2 + from_x // 2

    def final_from(zz):
        return (from_d, ((from_x % 2) * NZ + zz) * 2 + from_c)

    def same(device):
        return jnp.logical_and(device[0] == d, device[1] == i)

    inputs = ((k_hbm, k_ref), (v_hbm, v_ref), (q_hbm, q_ref), (w_hbm, w_ref), (cot_hbm, cot_ref))
    loads = [pltpu.make_async_copy(a, b, in_s.at[n]) for n, (a, b) in enumerate(inputs)]
    for load in loads:
        load.start()

    barrier = pltpu.get_barrier_semaphore()

    def greet(device):
        pl.semaphore_signal(barrier, inc=1, device_id=device, device_id_type=MESH)

    def greet_maybe_self(device):
        @pl.when(jnp.logical_not(same(device)))
        def _():
            greet(device)

    for t in range(1, CHIPS):
        greet(chip((j + t) % CHIPS))
    greet(partner)
    for t in range(1, NX):
        greet(at_x((x + t) % NX))
    for t in range(1, NY):
        greet(at_y((y + t) % NY, 0))
        greet(at_y((y + t) % NY, 1))
    for t in range(8):
        greet_maybe_self(final_to(t))
        greet_maybe_self(final_from(t))

    def head(h):
        return pl.ds(pl.multiple_of(h * HEAD, HEAD), HEAD)

    def loop_a(h, _):
        cols = head(h)
        fq[:, cols] = feature(q_ref[:, cols])
        kf = feature(k_ref[:, cols])
        fk[:, cols] = kf
        local[h] = dot(kf, v_ref[:, cols], 0, 0)
        return 0

    for load in loads[:3]:
        load.wait()
    lax.fori_loop(0, 16, loop_a, 0, unroll=2)
    for load in loads[3:]:
        load.wait()

    selves = jnp.where(8 * y + 4 * c + x == i, 2, 0)
    pl.semaphore_wait(barrier, 15 + 1 + 3 + 6 + 16 - selves)

    left = pl.ds(0, HALF)
    right = pl.ds(HALF, HALF)

    pending = []

    def begin(copy):
        copy.start()
        pending.append(copy)
        return copy

    def wslot(zz):
        return (xl * NZ + zz) * 2 + c

    def oslot(zz):
        return ((1 - xl) * NZ + zz) * 2 + c

    near_x = (y * 2 + xh, ((1 - xl) * NZ + z) * 2 + c)
    far_x = (y * 2 + (1 - xh), ((1 - xl) * NZ + z) * 2 + c)
    z_up = at_z((z + 1) % NZ)
    z_dn = at_z((z + NZ - 1) % NZ)

    def wsrc(r, cols=None):
        if r == 0:
            return w_ref if cols is None else w_ref.at[:, cols]
        slot = wslot((z + r) % NZ)
        return wfull.at[slot] if cols is None else wfull.at[slot, :, cols]

    def wdst(r, cols=None):
        slot = wslot((z + r) % NZ)
        return wfull.at[slot] if cols is None else wfull.at[slot, :, cols]

    def w_up(k):
        cols = left if k == 3 else None
        r = (-k) % NZ
        return rcopy(wsrc(r, cols), wdst(r, cols), up_s.at[k], up_r.at[k], z_up)

    def w_dn(k):
        cols = right if k == 3 else None
        return rcopy(wsrc(k, cols), wdst(k, cols), dn_s.at[k], dn_r.at[k], z_dn)

    def w_up_wait(k):
        r = (-k - 1) % NZ
        cols = left if k == 3 else None
        ref = wdst(r, cols)
        rcopy(ref, ref, up_s.at[k], up_r.at[k], z_up).wait_recv()

    def w_dn_wait(k):
        cols = right if k == 3 else None
        ref = wdst(k + 1, cols)
        rcopy(ref, ref, dn_s.at[k], dn_r.at[k], z_dn).wait_recv()

    def w_near(r):
        begin(rcopy(wsrc(r, left), wdst(r, left), wx_s.at[r, 0], wx_r.at[r, 0], near_x))

    def w_far(r):
        begin(rcopy(wsrc(r, right), wdst(r, right), wx_s.at[r, 1], wx_r.at[r, 1], far_x))

    def w_pair(r):
        begin(rcopy(wsrc(r), wdst(r), wp_s.at[r], wp_r.at[r], partner))

    def w_first():
        begin(w_up(0))
        begin(w_dn(0))
        w_near(0)
        w_far(0)
        w_pair(0)

    def w_step(k):
        w_up_wait(k - 1)
        begin(w_up(k))
        w_dn_wait(k - 1)
        begin(w_dn(k))
        for r in ((-k) % NZ, k):
            w_near(r)
            w_far(r)
            w_pair(r)

    def w_last():
        w_up_wait(3)
        w_near(4)
        w_dn_wait(3)
        w_far(4)
        w_pair(4)

    def w_other(r):
        slot = oslot((z + r) % NZ)
        for a, cols in ((0, left), (1, right)):
            ref = wfull.at[slot, :, cols]
            rcopy(ref, ref, wx_s.at[r, a], wx_r.at[r, a], near_x).wait_recv()
        begin(rcopy(wfull.at[slot], wfull.at[slot], wp_s.at[8 + r], wp_r.at[8 + r], partner))

    def w_pair_wait():
        for r in range(16):
            zz = (z + r) % NZ
            side = xl if r < 8 else 1 - xl
            ref = wfull.at[(side * NZ + zz) * 2 + o]
            rcopy(ref, ref, wp_s.at[r], wp_r.at[r], partner).wait_recv()

    y_up = at_y((y + 1) % NY, c)
    y_dn = at_y((y + NY - 1) % NY, c)

    def cslot(r):
        return ((y + r) % NY) * 2 + c

    def c_first():
        own = cotg.at[cslot(0)]
        begin(rcopy(cot_ref, own, cu_s.at[0], cu_r.at[0], y_up))
        begin(rcopy(cot_ref, own, cd_s.at[0], cd_r.at[0], y_dn))
        begin(rcopy(cot_ref, own, cp_s.at[0], cp_r.at[0], partner))

    def c_pair(r):
        ref = cotg.at[cslot(r)]
        begin(rcopy(ref, ref, cp_s.at[r], cp_r.at[r], partner))

    def c_second():
        below = cotg.at[cslot(3)]
        rcopy(below, below, cu_s.at[0], cu_r.at[0], y_up).wait_recv()
        part = cotg.at[cslot(3), :, left]
        begin(rcopy(part, part, cu_s.at[1], cu_r.at[1], y_up))
        above = cotg.at[cslot(1)]
        rcopy(above, above, cd_s.at[0], cd_r.at[0], y_dn).wait_recv()
        part = cotg.at[cslot(1), :, right]
        begin(rcopy(part, part, cd_s.at[1], cd_r.at[1], y_dn))
        c_pair(3)
        c_pair(1)

    def c_third():
        a = cotg.at[cslot(2), :, left]
        rcopy(a, a, cu_s.at[1], cu_r.at[1], y_up).wait_recv()
        b = cotg.at[cslot(2), :, right]
        rcopy(b, b, cd_s.at[1], cd_r.at[1], y_dn).wait_recv()
        c_pair(2)

    def c_wait():
        for r in range(4):
            ref = cotg.at[((y + r) % NY) * 2 + o]
            rcopy(ref, ref, cp_s.at[r], cp_r.at[r], partner).wait_recv()

    own_heads = pl.ds(8 * c, 8)
    other_heads = pl.ds(8 * o, 8)

    def scan_pair(n):
        xsend[n] = local[other_heads].astype(BF16)
        begin(rcopy(xsend.at[n], xrecv.at[n], sx_s.at[n], sx_r.at[n], partner))

    def scan_spread(n):
        rcopy(xrecv.at[n], xrecv.at[n], sx_s.at[n], sx_r.at[n], partner).wait_recv()
        total = (local[own_heads] + xrecv[n].astype(F32)).astype(BF16)
        pieces[n] = total.reshape(CHIPS, 64, HEAD)
        for t in range(1, CHIPS):
            jj = (j + t) % CHIPS
            begin(rcopy(pieces.at[n, jj], got.at[n, j], s1_s.at[n, jj], s1_r.at[n, j], chip(jj)))
        got[n, j] = pieces[n, j]

    def scan_return(n):
        for t in range(1, CHIPS):
            jj = (j + t) % CHIPS
            ref = got.at[n, jj]
            rcopy(ref, ref, s1_s.at[n, jj], s1_r.at[n, jj], partner).wait_recv()
        total = jnp.zeros((64, HEAD), F32)
        order = range(CHIPS) if n == 0 else range(CHIPS - 1, -1, -1)
        for jj in order:
            back_out[n, jj] = total.astype(BF16)
            total = total + got[n, jj].astype(F32)
        for t in range(1, CHIPS):
            jj = (j + t) % CHIPS
            begin(rcopy(back_out.at[n, jj], back_in.at[n, j], s2_s.at[n, jj], s2_r.at[n, j], chip(jj)))
        back_in[n, j] = back_out[n, j]

    def scan_share(n, out):
        for t in range(1, CHIPS):
            jj = (j + t) % CHIPS
            ref = back_in.at[n, jj]
            rcopy(ref, ref, s2_s.at[n, jj], s2_r.at[n, jj], partner).wait_recv()
        mine = back_in[n].astype(F32).reshape(8, HEAD, HEAD)
        last = (c if n == 0 else o).astype(F32)
        psend[n] = (mine + (1.0 - last) * local[own_heads]).astype(BF16)
        begin(rcopy(psend.at[n], out.at[own_heads], sp_s.at[n], sp_r.at[n], partner))
        out[own_heads] = (mine + last * xrecv[n].astype(F32)).astype(BF16)

    def scan_wait(n, out):
        ref = out.at[other_heads]
        rcopy(ref, ref, sp_s.at[n], sp_r.at[n], partner).wait_recv()

    me8 = y * 2 + c

    def block8(b):
        return pl.ds(pl.multiple_of(b * 256, 256), 256)

    def n_send():
        for t in range(1, 8):
            b = (me8 + t) % 8
            begin(
                rcopy(
                    normed.at[:, block8(b)], normg.at[me8], n_s.at[b], n_r.at[me8], at_y(b // 2, b % 2)
                )
            )
        normg[me8] = normed[:, block8(me8)]

    def n_wait():
        for t in range(1, 8):
            b = (me8 + t) % 8
            ref = normg.at[b]
            rcopy(ref, ref, n_s.at[b], n_r.at[b], partner).wait_recv()

    x_up = at_x((x + 1) % NX)
    x_dn = at_x((x + 3) % NX)
    two = (x + 2) % NX
    one_up = (x + 1) % NX
    one_dn = (x + 3) % NX

    def part(h, lo, size):
        return pl.ds(h * CHUNK + lo, size)

    def g_tile(h):
        def loop_g(n, _):
            cols = pl.ds(pl.multiple_of(h * CHUNK + n * 512, 512), 512)
            tile = dot(normg[...].reshape(1024, 256), cotg[:, :, cols].reshape(1024, 512), 0, 0)
            gwf[:, :, cols] = tile.reshape(4, 64, 512)
            gwt[:, :, cols] = tile.astype(BF16).reshape(4, 64, 512)
            return 0

        lax.fori_loop(0, CHUNK // 512, loop_g, 0)

    def g_first(h):
        low, high = part(h, 0, CHUNK // 2), part(h, CHUNK // 2, CHUNK // 2)
        begin(rcopy(gwt.at[two, :, low], xh_in.at[h, 0], xa_s.at[h, 0], xa_r.at[h, 0], x_up))
        begin(rcopy(gwt.at[two, :, high], xh_in.at[h, 1], xa_s.at[h, 1], xa_r.at[h, 1], x_dn))

    def g_second(h):
        low, high = part(h, 0, CHUNK // 2), part(h, CHUNK // 2, CHUNK // 2)
        lows, highs = pl.ds(0, CHUNK // 2), pl.ds(CHUNK // 2, CHUNK // 2)
        for a, to in ((0, x_up), (1, x_dn)):
            rcopy(xh_in.at[h, a], xh_in.at[h, a], xa_s.at[h, a], xa_r.at[h, a], to).wait_recv()
        x_out[h, 0, :, lows] = (gwf[one_up, :, low] + xh_in[h, 0].astype(F32)).astype(BF16)
        x_out[h, 0, :, highs] = gwt[one_up, :, high]
        x_out[h, 1, :, lows] = gwt[one_dn, :, low]
        x_out[h, 1, :, highs] = (gwf[one_dn, :, high] + xh_in[h, 1].astype(F32)).astype(BF16)
        begin(rcopy(x_out.at[h, 0], x_in.at[h, 0], xb_s.at[h, 0], xb_r.at[h, 0], x_up))
        begin(rcopy(x_out.at[h, 1], x_in.at[h, 1], xb_s.at[h, 1], xb_r.at[h, 1], x_dn))

    def g_third(h):
        for a, to in ((0, x_up), (1, x_dn)):
            rcopy(x_in.at[h, a], x_in.at[h, a], xb_s.at[h, a], xb_r.at[h, a], to).wait_recv()
        total = gwf[x, :, part(h, 0, CHUNK)] + x_in[h, 0].astype(F32) + x_in[h, 1].astype(F32)
        for zz in range(NZ):
            z_out[h, zz] = total[:, zz * PIECE : (zz + 1) * PIECE].astype(BF16)
        for t in range(1, NZ):
            zz = (z + t) % NZ
            begin(rcopy(z_out.at[h, zz], z_in.at[h, z], z_s.at[h, zz], z_r.at[h, z], at_z(zz)))
        z_in[h, z] = z_out[h, z]

    def f_copy(h, t):
        return rcopy(f_out.at[h], f_in.at[h, z], f_s.at[h, t], f_r.at[h, z], final_to(t))

    def g_fourth(h):
        for t in range(1, NZ):
            zz = (z + t) % NZ
            ref = z_in.at[h, zz]
            rcopy(ref, ref, z_s.at[h, zz], z_r.at[h, zz], partner).wait_recv()
        whole = z_in[h, 0].astype(F32)
        for zz in range(1, NZ):
            whole = whole + z_in[h, zz].astype(F32)
        f_out[h] = whole.astype(BF16)
        for t in range(8):
            to = final_to(t)

            @pl.when(jnp.logical_not(same(to)))
            def _(t=t):
                f_copy(h, t).start()

            @pl.when(same(to))
            def _():
                f_in[h, z] = f_out[h]

    def g_end(h):
        for zz in range(NZ):
            source = final_from(zz)

            @pl.when(jnp.logical_not(same(source)))
            def _(source=source, zz=zz):
                ref = f_in.at[h, zz]
                rcopy(ref, ref, f_s.at[h, zz], f_r.at[h, zz], source).wait_recv()

            gw_ref[:, h * CHUNK + zz * PIECE : h * CHUNK + (zz + 1) * PIECE] = f_in[h, zz].astype(F32) * loss_scale
        for t in range(8):
            to = final_to(t)

            @pl.when(jnp.logical_not(same(to)))
            def _(t=t):
                f_copy(h, t).wait_send()

    rows_at = lax.broadcasted_iota(jnp.int32, (HEAD, HEAD), 0)
    cols_at = lax.broadcasted_iota(jnp.int32, (HEAD, HEAD), 1)
    causal = rows_at >= cols_at

    def loop_b(h, _):
        cols = head(h)
        scores = dot(fq[:, cols], fk[:, cols], 1, 1)
        p = jnp.where(causal, scores, 0.0).astype(BF16)
        probs[h] = p
        att[:, cols] = dot(p, v_ref[:, cols], 1, 0)
        return 0

    def loop_c(h2, _):
        cols = pl.ds(pl.multiple_of(h2 * 256, 256), 256)
        rows = wfull[pl.ds(h2 * 4, 4)].reshape(256, 2048)
        dnorm[:, cols] = dot(cot_ref[...], rows, 1, 1) * gain_ref[:, cols]
        return 0

    def loop_n(h, _):
        cols = head(h)
        a = att[:, cols] + dot(fq[:, cols], prefix[h], 1, 0)
        inv = lax.rsqrt(jnp.mean(a * a, axis=-1, keepdims=True) + EPSILON)
        att[:, cols] = a
        inverse[h] = inv
        normed[:, cols] = (a * inv * gain_ref[:, cols]).astype(BF16)
        return 0

    def loop_d(h, _):
        cols = head(h)
        a = att[:, cols]
        inv = inverse[h]
        s = dnorm[:, cols]
        m = jnp.mean(s * a, axis=-1, keepdims=True)
        g = (inv * (s - a * inv * inv * m)).astype(BF16)
        datt[:, cols] = g
        local[h] = dot(fq[:, cols], g, 0, 0)
        return 0

    def loop_e(h, _):
        cols = head(h)
        g = datt[:, cols]
        fkh = fk[:, cols]
        dp = jnp.where(causal, dot(g, v_ref[:, cols], 1, 1), 0.0).astype(BF16)
        dfq = dot(dp, fkh, 1, 0) + dot(g, prefix[h], 1, 1)
        gq_ref[:, cols] = (dfq * slope(q_ref[:, cols])).astype(BF16)
        dfk[:, cols] = dot(dp, fq[:, cols], 0, 0)
        dgv[:, cols] = dot(probs[h], g, 0, 0)
        return 0

    def loop_m(n, _):
        cols = pl.ds(pl.multiple_of(n * 512, 512), 512)
        rows = wfull[:, :, cols].reshape(2048, 512)
        mixed_ref[:, cols] = dot(normed[...], rows, 1, 0).astype(BF16)
        return 0

    def loop_f(h, _):
        cols = head(h)
        s = suffix[h]
        gk = dfk[:, cols] + dot(v_ref[:, cols], s, 1, 1)
        gk_ref[:, cols] = (gk * slope(k_ref[:, cols])).astype(BF16)
        gv_ref[:, cols] = (dgv[:, cols] + dot(fk[:, cols], s, 1, 0)).astype(BF16)
        return 0

    scan_pair(0)
    w_first()
    c_first()
    scan_spread(0)
    lax.fori_loop(0, 16, loop_b, 0, unroll=2)
    wfull[i] = w_ref[...]
    cotg[cslot(0)] = cot_ref[...]
    scan_return(0)
    w_step(1)
    w_other(0)
    c_second()
    scan_share(0, prefix)
    scan_wait(0, prefix)
    w_step(2)
    lax.fori_loop(0, 16, loop_n, 0, unroll=2)
    n_send()
    w_other(7)
    w_other(1)
    c_third()
    w_step(3)
    c_wait()
    n_wait()
    for h in range(CHUNKS):
        g_tile(h)
        g_first(h)
    w_other(6)
    w_other(2)
    w_last()
    for h in range(CHUNKS):
        g_second(h)
    for r in (5, 3, 4):
        w_other(r)
    w_pair_wait()
    lax.fori_loop(0, 8, loop_c, 0)
    lax.fori_loop(0, 16, loop_d, 0, unroll=2)
    scan_pair(1)
    g_third(0)
    scan_spread(1)
    for h in range(1, CHUNKS):
        g_third(h)
    lax.fori_loop(0, 16, loop_e, 0, unroll=2)
    scan_return(1)
    for h in range(CHUNKS):
        g_fourth(h)
    lax.fori_loop(0, 4, loop_m, 0)
    scan_share(1, suffix)
    scan_wait(1, suffix)
    lax.fori_loop(0, 16, loop_f, 0, unroll=2)
    for copy in pending:
        copy.wait_send()
    for h in range(CHUNKS):
        g_end(h)


def finish(*refs):
    copies = [pltpu.make_async_copy(refs[n], refs[5 + n], refs[10].at[n]) for n in range(5)]
    for copy in copies:
        copy.start()
    for copy in copies:
        copy.wait()


def on_device(loss_scale, query_rows, key_rows, value_rows, norm_gain, out_weight, cotangent):
    length, width = query_rows.shape[1:]
    rows = out_weight.shape[0]
    vmem = pl.BlockSpec(memory_space=pltpu.VMEM)
    hbm = pl.BlockSpec(memory_space=pltpu.HBM)
    block = jax.ShapeDtypeStruct((length, width), BF16)
    dma = pltpu.SemaphoreType.DMA
    states = (16, HEAD, HEAD)
    scratch = [
        pltpu.VMEM((length, width), BF16),
        pltpu.VMEM((length, width), BF16),
        pltpu.VMEM((length, width), BF16),
        pltpu.VMEM((rows, width), BF16),
        pltpu.VMEM((length, width), BF16),
        dma((5,)),
        pltpu.VMEM((length, width), BF16),
        pltpu.VMEM((length, width), BF16),
        pltpu.VMEM(states, BF16),
        pltpu.VMEM((length, width), F32),
        pltpu.VMEM((length, width), F32),
        pltpu.VMEM((length, width), BF16),
        pltpu.VMEM((length, width), BF16),
        pltpu.VMEM((length, width), F32),
        pltpu.VMEM((length, width), F32),
        pltpu.VMEM(states, F32),
        pltpu.VMEM((16, length, 1), F32),
        pltpu.VMEM((2, 8, HEAD, HEAD), BF16),
        pltpu.VMEM((2, 8, HEAD, HEAD), BF16),
        pltpu.VMEM((2, CHIPS, 64, HEAD), BF16),
        pltpu.VMEM((2, CHIPS, 64, HEAD), BF16),
        pltpu.VMEM((2, CHIPS, 64, HEAD), BF16),
        pltpu.VMEM((2, CHIPS, 64, HEAD), BF16),
        pltpu.VMEM((2, 8, HEAD, HEAD), BF16),
        pltpu.VMEM(states, BF16),
        pltpu.VMEM(states, BF16),
        pltpu.VMEM((32, 64, width), BF16),
        pltpu.VMEM((8, length, width), BF16),
        pltpu.VMEM((8, length, 256), BF16),
        pltpu.VMEM((4, 64, width), F32),
        pltpu.VMEM((4, 64, width), BF16),
        pltpu.VMEM((CHUNKS, 2, 64, CHUNK // 2), BF16),
        pltpu.VMEM((CHUNKS, 2, 64, CHUNK), BF16),
        pltpu.VMEM((CHUNKS, 2, 64, CHUNK), BF16),
        pltpu.VMEM((CHUNKS, 8, 64, PIECE), BF16),
        pltpu.VMEM((CHUNKS, 8, 64, PIECE), BF16),
        pltpu.VMEM((CHUNKS, 64, PIECE), BF16),
        pltpu.VMEM((CHUNKS, 8, 64, PIECE), BF16),
        dma((2,)), dma((2,)), dma((2, 16)), dma((2, 16)), dma((2, 16)), dma((2, 16)), dma((2,)), dma((2,)),
        dma((4,)), dma((4,)), dma((4,)), dma((4,)), dma((8, 2)), dma((8, 2)), dma((16,)), dma((16,)),
        dma((2,)), dma((2,)), dma((2,)), dma((2,)), dma((4,)), dma((4,)),
        dma((8,)), dma((8,)),
        dma((CHUNKS, 2)), dma((CHUNKS, 2)), dma((CHUNKS, 2)), dma((CHUNKS, 2)),
        dma((CHUNKS, 8)), dma((CHUNKS, 8)), dma((CHUNKS, 8)), dma((CHUNKS, 8)),
    ]

    def body(*refs):
        kernel(loss_scale, *refs)

    shapes = (block, block, block, block, jax.ShapeDtypeStruct((rows, width), F32))
    results = pl.pallas_call(
        body,
        out_shape=shapes,
        in_specs=[hbm, hbm, hbm, vmem, hbm, hbm],
        out_specs=(vmem,) * 5,
        scratch_shapes=scratch,
        compiler_params=pltpu.CompilerParams(
            collective_id=0, has_side_effects=True, vmem_limit_bytes=44 * 1024 * 1024
        ),
        name="layer",
    )(query_rows[0], key_rows[0], value_rows[0], norm_gain.reshape(1, width), out_weight, cotangent[0])
    anywhere = pl.BlockSpec(memory_space=pl.ANY)
    mixed, gq, gk, gv, gw = pl.pallas_call(
        finish,
        out_shape=shapes,
        in_specs=[anywhere] * 5,
        out_specs=(hbm,) * 5,
        scratch_shapes=[dma((5,))],
        compiler_params=pltpu.CompilerParams(vmem_limit_bytes=8 * 1024 * 1024),
        name="finish",
    )(*results)
    return mixed[None], gq[None], gk[None], gv[None], gw


def solution(mesh):
    positions = mesh.shape["dp"] * mesh.shape["ctx"] * HEAD
    loss_scale = 1.0 / math.sqrt(positions)

    def run(*args):
        return on_device(loss_scale, *args)

    split = P("dp", "ctx", None)
    return jax.shard_map(
        run,
        mesh=mesh,
        in_specs=(split, split, split, P(), P("ctx", None), split),
        out_specs=(split, split, split, split, P("ctx", None)),
        check_vma=False,
    )
```

```python
import math

import jax
import jax.numpy as jnp
from jax import lax
from jax.experimental import pallas as pl
from jax.experimental.pallas import tpu as pltpu
from jax.sharding import PartitionSpec as P

MESH = pl.DeviceIdType.MESH
F32 = jnp.float32
BF16 = jnp.bfloat16
HEAD = 128
EPSILON = 1e-06
NZ = 8
NX = 4
NY = 4
CHIPS = 16
HALF = 1024
CHUNKS = 2
CHUNK = 2048 // CHUNKS
WIDE = CHUNK // 2


def dot(a, b, ca, cb):
    return lax.dot_general(a, b, (((ca,), (cb,)), ((), ())), preferred_element_type=F32)


def rcopy(src, dst, send, recv, device):
    return pltpu.make_async_remote_copy(
        src_ref=src, dst_ref=dst, send_sem=send, recv_sem=recv, device_id=device, device_id_type=MESH
    )


def exp_low(wide):
    return jnp.exp(jnp.minimum(wide, 0.0))


def feature(values):
    wide = values.astype(F32)
    return jnp.where(wide > 0, wide + 1.0, exp_low(wide)).astype(BF16)


def slope(values):
    wide = values.astype(F32)
    return jnp.where(wide > 0, 1.0, exp_low(wide))


def kernel(
    loss_scale,
    q_hbm, k_hbm, v_hbm, gain_hbm, w_hbm, cot_hbm,
    mixed_ref, gq_ref, gk_ref, gv_ref, gw_ref,
    q_ref, k_ref, v_ref, gain_ref, w_ref, cot_ref, in_s,
    fq, fk, probs, att, dnorm, normed, datt, dfk, dgv, local, inverse,
    xsend, xrecv, pieces, got, back_out, back_in, psend, prefix, suffix,
    wfull, cotg, flipped, normg, gwf, gwt, xh_in, x_out, x_in, z_out, z_in, f_out, f_in,
    sx_s, sx_r, s1_s, s1_r, s2_s, s2_r, sp_s, sp_r,
    up_s, up_r, dn_s, dn_r, wx_s, wx_r, wy_s, wy_r, wp_s, wp_r,
    cu_s, cu_r, cd_s, cd_r, cp_s, cp_r,
    n_s, n_r, xa_s, xa_r, xb_s, xb_r, z_s, z_r, f_s, f_r,
):
    d = lax.axis_index("dp")
    i = lax.axis_index("ctx")
    c = i % 2
    j = i // 2
    z = j % NZ
    xl = j // NZ
    y = d // 2
    xh = d % 2
    x = xh * 2 + xl
    o = 1 - c
    partner = (d, j * 2 + o)

    def chip(jj):
        return (d, jj * 2 + c)

    def at_x(xx):
        return (y * 2 + xx // 2, ((xx % 2) * NZ + z) * 2 + c)

    def at_z(zz):
        return (d, (xl * NZ + zz) * 2 + c)

    def at_y(yy, cc):
        return (yy * 2 + xh, j * 2 + cc)

    def final_to(t):
        return (t, (xl * NZ + z) * 2 + y // 2)

    def final_from(t):
        return ((2 * c + t // 4) * 2 + t % 2, (xl * NZ + z) * 2 + (t // 2) % 2)

    def same(device):
        return jnp.logical_and(device[0] == d, device[1] == i)

    inputs = ((k_hbm, k_ref), (v_hbm, v_ref), (q_hbm, q_ref), (w_hbm, w_ref), (cot_hbm, cot_ref), (gain_hbm, gain_ref))
    loads = [pltpu.make_async_copy(a, b, in_s.at[n]) for n, (a, b) in enumerate(inputs)]
    for load in loads:
        load.start()

    barrier = pltpu.get_barrier_semaphore()

    def greet(device):
        pl.semaphore_signal(barrier, inc=1, device_id=device, device_id_type=MESH)

    def greet_maybe_self(device):
        @pl.when(jnp.logical_not(same(device)))
        def _():
            greet(device)

    for t in range(1, CHIPS):
        greet(chip((j + t) % CHIPS))
    greet(partner)
    for t in range(1, NX):
        greet(at_x((x + t) % NX))
    for t in range(1, NY):
        greet(at_y((y + t) % NY, 0))
        greet(at_y((y + t) % NY, 1))
    for t in range(8):
        greet_maybe_self(final_to(t))
        greet_maybe_self(final_from(t))

    def head(h):
        return pl.ds(pl.multiple_of(h * HEAD, HEAD), HEAD)

    def loop_a(h, _):
        cols = head(h)
        fq[:, cols] = feature(q_ref[:, cols])
        kf = feature(k_ref[:, cols])
        fk[:, cols] = kf
        local[h] = dot(kf, v_ref[:, cols], 0, 0)
        return 0

    for load in loads[:3]:
        load.wait()
    lax.fori_loop(0, 16, loop_a, 0, unroll=2)
    for load in loads[3:]:
        load.wait()

    selves = jnp.where(y // 2 == c, 2, 0)
    pl.semaphore_wait(barrier, 15 + 1 + 3 + 6 + 16 - selves)

    left = pl.ds(0, HALF)
    right = pl.ds(HALF, HALF)

    pending = []

    def begin(copy):
        copy.start()
        pending.append(copy)
        return copy

    def wslot(zz):
        return (xl * NZ + zz) * 2 + c

    def oslot(zz):
        return ((1 - xl) * NZ + zz) * 2 + c

    near_x = (y * 2 + xh, ((1 - xl) * NZ + z) * 2 + c)
    far_x = (y * 2 + (1 - xh), ((1 - xl) * NZ + z) * 2 + c)
    z_up = at_z((z + 1) % NZ)
    z_dn = at_z((z + NZ - 1) % NZ)

    p = y % 2
    mine_w = pl.ds(pl.multiple_of(p * HALF, HALF), HALF)
    rest_w = pl.ds(pl.multiple_of((1 - p) * HALF, HALF), HALF)

    def quarter(side, a):
        return pl.ds(pl.multiple_of(side * HALF + a * 512, 512), 512)

    y_up = at_y((y + 1) % NY, c)
    y_dn = at_y((y + NY - 1) % NY, c)

    def wcols(r, cols, own=False):
        if r == 0 and not own:
            return w_ref.at[:, cols]
        return wfull.at[wslot((z + r) % NZ), :, cols]

    def z_cols(k, a):
        return quarter(p, a) if k == 3 else mine_w

    def w_up(k):
        r = (-k) % NZ
        cols = z_cols(k, 0)
        begin(rcopy(wcols(r, cols), wcols(r, cols, True), up_s.at[k], up_r.at[k], z_up))

    def w_dn(k):
        cols = z_cols(k, 1)
        begin(rcopy(wcols(k, cols), wcols(k, cols, True), dn_s.at[k], dn_r.at[k], z_dn))

    def w_up_wait(k):
        ref = wcols((-k - 1) % NZ, z_cols(k, 0), True)
        rcopy(ref, ref, up_s.at[k], up_r.at[k], z_up).wait_recv()

    def w_dn_wait(k):
        ref = wcols(k + 1, z_cols(k, 1), True)
        rcopy(ref, ref, dn_s.at[k], dn_r.at[k], z_dn).wait_recv()

    def w_near(r):
        begin(rcopy(wcols(r, mine_w), wcols(r, mine_w, True), wx_s.at[r, 0], wx_r.at[r, 0], near_x))

    def w_far(r):
        begin(rcopy(wcols(r, rest_w), wcols(r, rest_w, True), wx_s.at[r, 1], wx_r.at[r, 1], far_x))

    def w_pair(r):
        dst = wfull.at[wslot((z + r) % NZ)]
        begin(rcopy(w_ref if r == 0 else dst, dst, wp_s.at[r], wp_r.at[r], partner))

    def w_side(r, a):
        ref = wcols(r, quarter(p, a))
        begin(rcopy(ref, ref, wy_s.at[r, a], wy_r.at[r, a], y_dn if a else y_up))

    def w_first():
        w_up(0)
        w_dn(0)
        w_near(0)
        w_far(0)
        w_pair(0)

    def w_step(k):
        w_up_wait(k - 1)
        w_up(k)
        w_dn_wait(k - 1)
        w_dn(k)
        for r in ((-k) % NZ, k):
            w_near(r)
            w_side(r, 0)
            w_side(r, 1)

    def w_last():
        w_up_wait(3)
        w_side(4, 0)
        w_dn_wait(3)
        w_side(4, 1)
        w_near(4)

    def w_rest(r):
        for a in (0, 1):
            ref = wcols(r, quarter(1 - p, a))
            rcopy(ref, ref, wy_s.at[r, a], wy_r.at[r, a], y_up).wait_recv()
        w_far(r)
        w_pair(r)

    def w_other(r):
        slot = oslot((z + r) % NZ)
        for a, cols in ((0, mine_w), (1, rest_w)):
            ref = wfull.at[slot, :, cols]
            rcopy(ref, ref, wx_s.at[r, a], wx_r.at[r, a], near_x).wait_recv()
        begin(rcopy(wfull.at[slot], wfull.at[slot], wp_s.at[8 + r], wp_r.at[8 + r], partner))

    def w_pair_wait():
        for r in range(16):
            zz = (z + r) % NZ
            side = xl if r < 8 else 1 - xl
            ref = wfull.at[(side * NZ + zz) * 2 + o]
            rcopy(ref, ref, wp_s.at[r], wp_r.at[r], partner).wait_recv()

    def cslot(r):
        return ((y + r) % NY) * 2 + c

    def c_first():
        own = cotg.at[cslot(0)]
        begin(rcopy(cot_ref, own, cu_s.at[0], cu_r.at[0], y_up))
        begin(rcopy(cot_ref, own, cd_s.at[0], cd_r.at[0], y_dn))
        begin(rcopy(cot_ref, own, cp_s.at[0], cp_r.at[0], partner))

    def c_pair(r):
        ref = cotg.at[cslot(r)]
        begin(rcopy(ref, ref, cp_s.at[r], cp_r.at[r], partner))

    def c_second():
        below = cotg.at[cslot(3)]
        rcopy(below, below, cu_s.at[0], cu_r.at[0], y_up).wait_recv()
        part = cotg.at[cslot(3), :, left]
        begin(rcopy(part, part, cu_s.at[1], cu_r.at[1], y_up))
        above = cotg.at[cslot(1)]
        rcopy(above, above, cd_s.at[0], cd_r.at[0], y_dn).wait_recv()
        part = cotg.at[cslot(1), :, right]
        begin(rcopy(part, part, cd_s.at[1], cd_r.at[1], y_dn))
        c_pair(3)
        c_pair(1)

    def c_third():
        a = cotg.at[cslot(2), :, left]
        rcopy(a, a, cu_s.at[1], cu_r.at[1], y_up).wait_recv()
        b = cotg.at[cslot(2), :, right]
        rcopy(b, b, cd_s.at[1], cd_r.at[1], y_dn).wait_recv()
        c_pair(2)

    def c_wait():
        for r in range(4):
            ref = cotg.at[((y + r) % NY) * 2 + o]
            rcopy(ref, ref, cp_s.at[r], cp_r.at[r], partner).wait_recv()

    own_heads = pl.ds(8 * c, 8)
    other_heads = pl.ds(8 * o, 8)

    def scan_pair(n):
        xsend[n] = local[other_heads].astype(BF16)
        begin(rcopy(xsend.at[n], xrecv.at[n], sx_s.at[n], sx_r.at[n], partner))

    def scan_spread(n):
        rcopy(xrecv.at[n], xrecv.at[n], sx_s.at[n], sx_r.at[n], partner).wait_recv()
        total = (local[own_heads] + xrecv[n].astype(F32)).astype(BF16)
        pieces[n] = total.reshape(CHIPS, 64, HEAD)
        for t in range(1, CHIPS):
            jj = (j + t) % CHIPS
            begin(rcopy(pieces.at[n, jj], got.at[n, j], s1_s.at[n, jj], s1_r.at[n, j], chip(jj)))
        got[n, j] = pieces[n, j]

    def scan_return(n):
        for t in range(1, CHIPS):
            jj = (j + t) % CHIPS
            ref = got.at[n, jj]
            rcopy(ref, ref, s1_s.at[n, jj], s1_r.at[n, jj], partner).wait_recv()
        total = jnp.zeros((64, HEAD), F32)
        order = range(CHIPS) if n == 0 else range(CHIPS - 1, -1, -1)
        for jj in order:
            back_out[n, jj] = total.astype(BF16)
            total = total + got[n, jj].astype(F32)
        for t in range(1, CHIPS):
            jj = (j + t) % CHIPS
            begin(rcopy(back_out.at[n, jj], back_in.at[n, j], s2_s.at[n, jj], s2_r.at[n, j], chip(jj)))
        back_in[n, j] = back_out[n, j]

    def scan_share(n, out):
        for t in range(1, CHIPS):
            jj = (j + t) % CHIPS
            ref = back_in.at[n, jj]
            rcopy(ref, ref, s2_s.at[n, jj], s2_r.at[n, jj], partner).wait_recv()
        mine = back_in[n].astype(F32).reshape(8, HEAD, HEAD)
        last = (c if n == 0 else o).astype(F32)
        psend[n] = (mine + (1.0 - last) * local[own_heads]).astype(BF16)
        begin(rcopy(psend.at[n], out.at[own_heads], sp_s.at[n], sp_r.at[n], partner))
        out[own_heads] = (mine + last * xrecv[n].astype(F32)).astype(BF16)

    def scan_wait(n, out):
        ref = out.at[other_heads]
        rcopy(ref, ref, sp_s.at[n], sp_r.at[n], partner).wait_recv()

    me8 = y * 2 + c

    def positions(b):
        return pl.ds(pl.multiple_of(b * HEAD, HEAD), HEAD)

    def n_send():
        for t in range(1, 8):
            b = (me8 + t) % 8
            begin(
                rcopy(
                    flipped.at[:, b],
                    normg.at[:, :, positions(me8)],
                    n_s.at[b],
                    n_r.at[me8],
                    at_y(b // 2, b % 2),
                )
            )
        normg[:, :, positions(me8)] = flipped[:, me8]

    def n_wait():
        for t in range(1, 8):
            b = (me8 + t) % 8
            ref = normg.at[:, :, positions(b)]
            rcopy(ref, ref, n_s.at[b], n_r.at[b], partner).wait_recv()

    x_up = at_x((x + 1) % NX)
    x_dn = at_x((x + 3) % NX)
    two = (x + 2) % NX
    one_up = (x + 1) % NX
    one_dn = (x + 3) % NX

    def piece(k, h, lo, size):
        cols = pl.ds(pl.multiple_of(h * CHUNK + (k // 2) * WIDE + lo, HEAD), size)
        return pl.ds(8 * (k % 2), 8), slice(None), cols

    lows, highs = pl.ds(0, WIDE // 2), pl.ds(WIDE // 2, WIDE // 2)

    def low(k, h):
        return piece(k, h, 0, WIDE // 2)

    def high(k, h):
        return piece(k, h, WIDE // 2, WIDE // 2)

    def g_tile(h):
        def loop_g(n, _):
            cols = pl.ds(pl.multiple_of(h * CHUNK + n * 512, 512), 512)
            tile = dot(normg[...].reshape(256, 1024), cotg[:, :, cols].reshape(1024, 512), 1, 0)
            gwf[:, :, cols] = tile.reshape(16, 16, 512)
            gwt[:, :, cols] = tile.astype(BF16).reshape(16, 16, 512)
            return 0

        lax.fori_loop(0, CHUNK // 512, loop_g, 0)

    def g_first(h):
        begin(rcopy(gwt.at[low(two, h)], xh_in.at[h, 0], xa_s.at[h, 0], xa_r.at[h, 0], x_up))
        begin(rcopy(gwt.at[high(two, h)], xh_in.at[h, 1], xa_s.at[h, 1], xa_r.at[h, 1], x_dn))

    def g_second(h):
        for a, to in ((0, x_up), (1, x_dn)):
            rcopy(xh_in.at[h, a], xh_in.at[h, a], xa_s.at[h, a], xa_r.at[h, a], to).wait_recv()
        x_out[h, 0, :, :, lows] = (gwf[low(one_up, h)] + xh_in[h, 0].astype(F32)).astype(BF16)
        x_out[h, 0, :, :, highs] = gwt[high(one_up, h)]
        x_out[h, 1, :, :, lows] = gwt[low(one_dn, h)]
        x_out[h, 1, :, :, highs] = (gwf[high(one_dn, h)] + xh_in[h, 1].astype(F32)).astype(BF16)
        begin(rcopy(x_out.at[h, 0], x_in.at[h, 0], xb_s.at[h, 0], xb_r.at[h, 0], x_up))
        begin(rcopy(x_out.at[h, 1], x_in.at[h, 1], xb_s.at[h, 1], xb_r.at[h, 1], x_dn))

    def g_third(h):
        for a, to in ((0, x_up), (1, x_dn)):
            rcopy(x_in.at[h, a], x_in.at[h, a], xb_s.at[h, a], xb_r.at[h, a], to).wait_recv()
        total = gwf[piece(x, h, 0, WIDE)] + x_in[h, 0].astype(F32) + x_in[h, 1].astype(F32)
        z_out[h] = total.astype(BF16)
        for t in range(1, NZ):
            zz = (z + t) % NZ
            begin(rcopy(z_out.at[h, zz], z_in.at[h, z], z_s.at[h, zz], z_r.at[h, z], at_z(zz)))
        z_in[h, z] = z_out[h, z]

    me_f = (2 * (y % 2) + c) * 2 + xh

    def f_copy(h, t):
        return rcopy(f_out.at[h], f_in.at[h, me_f], f_s.at[h, t], f_r.at[h, me_f], final_to(t))

    def g_fourth(h):
        for t in range(1, NZ):
            zz = (z + t) % NZ
            ref = z_in.at[h, zz]
            rcopy(ref, ref, z_s.at[h, zz], z_r.at[h, zz], partner).wait_recv()
        whole = z_in[h, 0].astype(F32)
        for zz in range(1, NZ):
            whole = whole + z_in[h, zz].astype(F32)
        f_out[h] = whole.astype(BF16)
        for t in range(8):
            to = final_to(t)

            @pl.when(jnp.logical_not(same(to)))
            def _(t=t):
                f_copy(h, t).start()

            @pl.when(same(to))
            def _():
                f_in[h, me_f] = f_out[h]

    def g_end(h):
        for t in range(8):
            source = final_from(t)

            @pl.when(jnp.logical_not(same(source)))
            def _(source=source, t=t):
                ref = f_in.at[h, t]
                rcopy(ref, ref, f_s.at[h, t], f_r.at[h, t], source).wait_recv()

            row, col = 16 * (t // 2), h * CHUNK + WIDE * (t % 2)
            gw_ref[row : row + 16, col : col + WIDE] = f_in[h, t].astype(F32) * loss_scale
        for t in range(8):
            to = final_to(t)

            @pl.when(jnp.logical_not(same(to)))
            def _(t=t):
                f_copy(h, t).wait_send()

    rows_at = lax.broadcasted_iota(jnp.int32, (HEAD, HEAD), 0)
    cols_at = lax.broadcasted_iota(jnp.int32, (HEAD, HEAD), 1)
    causal = rows_at >= cols_at

    def loop_b(h, _):
        cols = head(h)
        scores = dot(fq[:, cols], fk[:, cols], 1, 1)
        p = jnp.where(causal, scores, 0.0).astype(BF16)
        probs[h] = p
        att[:, cols] = dot(p, v_ref[:, cols], 1, 0)
        return 0

    def loop_c(h2, _):
        cols = pl.ds(pl.multiple_of(h2 * 256, 256), 256)
        rows = wfull[pl.ds(h2 * 4, 4)].reshape(256, 2048)
        dnorm[:, cols] = dot(cot_ref[...], rows, 1, 1) * gain_ref[:, cols]
        return 0

    def loop_n(h, _):
        cols = head(h)
        a = att[:, cols] + dot(fq[:, cols], prefix[h], 1, 0)
        inv = lax.rsqrt(jnp.mean(a * a, axis=-1, keepdims=True) + EPSILON)
        att[:, cols] = a
        inverse[h] = inv
        out = a * inv * gain_ref[:, cols]
        normed[:, cols] = out.astype(BF16)
        flipped[h] = jnp.transpose(out).astype(BF16).reshape(8, 16, HEAD)
        return 0

    def loop_d(h, _):
        cols = head(h)
        a = att[:, cols]
        inv = inverse[h]
        s = dnorm[:, cols]
        m = jnp.mean(s * a, axis=-1, keepdims=True)
        g = (inv * (s - a * inv * inv * m)).astype(BF16)
        datt[:, cols] = g
        local[h] = dot(fq[:, cols], g, 0, 0)
        return 0

    def loop_e(h, _):
        cols = head(h)
        g = datt[:, cols]
        fkh = fk[:, cols]
        dp = jnp.where(causal, dot(g, v_ref[:, cols], 1, 1), 0.0).astype(BF16)
        dfq = dot(dp, fkh, 1, 0) + dot(g, prefix[h], 1, 1)
        gq_ref[:, cols] = (dfq * slope(q_ref[:, cols])).astype(BF16)
        dfk[:, cols] = dot(dp, fq[:, cols], 0, 0)
        dgv[:, cols] = dot(probs[h], g, 0, 0)
        return 0

    def loop_m(n, _):
        cols = pl.ds(pl.multiple_of(n * 512, 512), 512)
        rows = wfull[:, :, cols].reshape(2048, 512)
        mixed_ref[:, cols] = dot(normed[...], rows, 1, 0).astype(BF16)
        return 0

    def loop_f(h, _):
        cols = head(h)
        s = suffix[h]
        gk = dfk[:, cols] + dot(v_ref[:, cols], s, 1, 1)
        gk_ref[:, cols] = (gk * slope(k_ref[:, cols])).astype(BF16)
        gv_ref[:, cols] = (dgv[:, cols] + dot(fk[:, cols], s, 1, 0)).astype(BF16)
        return 0

    scan_pair(0)
    w_first()
    c_first()
    scan_spread(0)
    wfull[i] = w_ref[...]
    cotg[cslot(0)] = cot_ref[...]
    w_step(1)
    lax.fori_loop(0, 16, loop_b, 0, unroll=2)
    scan_return(0)
    w_step(2)
    c_second()
    w_rest(1)
    w_rest(7)
    w_rest(2)
    w_rest(6)
    scan_share(0, prefix)
    w_step(3)
    scan_wait(0, prefix)
    lax.fori_loop(0, 16, loop_n, 0, unroll=2)
    n_send()
    c_third()
    w_last()
    for r in (0, 1, 7):
        w_other(r)
    for r in (3, 5):
        w_rest(r)
    for r in (2, 6):
        w_other(r)
    w_rest(4)
    c_wait()
    for r in (3, 5, 4):
        w_other(r)
    w_pair_wait()
    lax.fori_loop(0, 8, loop_c, 0)
    n_wait()
    for h in range(CHUNKS):
        g_tile(h)
        g_first(h)
    lax.fori_loop(0, 16, loop_d, 0, unroll=2)
    scan_pair(1)
    g_second(0)
    scan_spread(1)
    for h in range(1, CHUNKS):
        g_second(h)
    lax.fori_loop(0, 8, loop_e, 0, unroll=2)
    g_third(0)
    lax.fori_loop(8, 16, loop_e, 0, unroll=2)
    for h in range(1, CHUNKS):
        g_third(h)
    scan_return(1)
    g_fourth(0)
    lax.fori_loop(0, 4, loop_m, 0)
    for h in range(1, CHUNKS):
        g_fourth(h)
    scan_share(1, suffix)
    scan_wait(1, suffix)
    lax.fori_loop(0, 16, loop_f, 0, unroll=2)
    for copy in pending:
        copy.wait_send()
    for h in range(CHUNKS):
        g_end(h)


def finish(*refs):
    copies = [pltpu.make_async_copy(refs[n], refs[5 + n], refs[10].at[n]) for n in range(5)]
    for copy in copies:
        copy.start()
    for copy in copies:
        copy.wait()


def on_device(loss_scale, query_rows, key_rows, value_rows, norm_gain, out_weight, cotangent):
    length, width = query_rows.shape[1:]
    rows = out_weight.shape[0]
    vmem = pl.BlockSpec(memory_space=pltpu.VMEM)
    hbm = pl.BlockSpec(memory_space=pltpu.HBM)
    block = jax.ShapeDtypeStruct((length, width), BF16)
    dma = pltpu.SemaphoreType.DMA
    states = (16, HEAD, HEAD)
    scratch = [
        pltpu.VMEM((length, width), BF16),
        pltpu.VMEM((length, width), BF16),
        pltpu.VMEM((length, width), BF16),
        pltpu.VMEM((1, width), F32),
        pltpu.VMEM((rows, width), BF16),
        pltpu.VMEM((length, width), BF16),
        dma((6,)),
        pltpu.VMEM((length, width), BF16),
        pltpu.VMEM((length, width), BF16),
        pltpu.VMEM(states, BF16),
        pltpu.VMEM((length, width), F32),
        pltpu.VMEM((length, width), F32),
        pltpu.VMEM((length, width), BF16),
        pltpu.VMEM((length, width), BF16),
        pltpu.VMEM((length, width), F32),
        pltpu.VMEM((length, width), F32),
        pltpu.VMEM(states, F32),
        pltpu.VMEM((16, length, 1), F32),
        pltpu.VMEM((2, 8, HEAD, HEAD), BF16),
        pltpu.VMEM((2, 8, HEAD, HEAD), BF16),
        pltpu.VMEM((2, CHIPS, 64, HEAD), BF16),
        pltpu.VMEM((2, CHIPS, 64, HEAD), BF16),
        pltpu.VMEM((2, CHIPS, 64, HEAD), BF16),
        pltpu.VMEM((2, CHIPS, 64, HEAD), BF16),
        pltpu.VMEM((2, 8, HEAD, HEAD), BF16),
        pltpu.VMEM(states, BF16),
        pltpu.VMEM(states, BF16),
        pltpu.VMEM((32, 64, width), BF16),
        pltpu.VMEM((8, length, width), BF16),
        pltpu.VMEM((16, 8, 16, length), BF16),
        pltpu.VMEM((16, 16, 8 * length), BF16),
        pltpu.VMEM((16, 16, width), F32),
        pltpu.VMEM((16, 16, width), BF16),
        pltpu.VMEM((CHUNKS, 2, 8, 16, WIDE // 2), BF16),
        pltpu.VMEM((CHUNKS, 2, 8, 16, WIDE), BF16),
        pltpu.VMEM((CHUNKS, 2, 8, 16, WIDE), BF16),
        pltpu.VMEM((CHUNKS, 8, 16, WIDE), BF16),
        pltpu.VMEM((CHUNKS, 8, 16, WIDE), BF16),
        pltpu.VMEM((CHUNKS, 16, WIDE), BF16),
        pltpu.VMEM((CHUNKS, 8, 16, WIDE), BF16),
        dma((2,)), dma((2,)), dma((2, 16)), dma((2, 16)), dma((2, 16)), dma((2, 16)), dma((2,)), dma((2,)),
        dma((4,)), dma((4,)), dma((4,)), dma((4,)), dma((8, 2)), dma((8, 2)), dma((8, 2)), dma((8, 2)), dma((16,)), dma((16,)),
        dma((2,)), dma((2,)), dma((2,)), dma((2,)), dma((4,)), dma((4,)),
        dma((8,)), dma((8,)),
        dma((CHUNKS, 2)), dma((CHUNKS, 2)), dma((CHUNKS, 2)), dma((CHUNKS, 2)),
        dma((CHUNKS, 8)), dma((CHUNKS, 8)), dma((CHUNKS, 8)), dma((CHUNKS, 8)),
    ]

    def body(*refs):
        kernel(loss_scale, *refs)

    shapes = (block, block, block, block, jax.ShapeDtypeStruct((rows, width), F32))
    results = pl.pallas_call(
        body,
        out_shape=shapes,
        in_specs=[hbm] * 6,
        out_specs=(vmem,) * 5,
        scratch_shapes=scratch,
        compiler_params=pltpu.CompilerParams(
            collective_id=0, has_side_effects=True, vmem_limit_bytes=44 * 1024 * 1024
        ),
        name="layer",
    )(
        *(pltpu.with_memory_space_constraint(a, pltpu.HBM) for a in (query_rows[0], key_rows[0], value_rows[0])),
        pltpu.with_memory_space_constraint(norm_gain.reshape(1, width), pltpu.HBM),
        *(pltpu.with_memory_space_constraint(a, pltpu.HBM) for a in (out_weight, cotangent[0])),
    )
    anywhere = pl.BlockSpec(memory_space=pl.ANY)
    mixed, gq, gk, gv, gw = pl.pallas_call(
        finish,
        out_shape=shapes,
        in_specs=[anywhere] * 5,
        out_specs=(hbm,) * 5,
        scratch_shapes=[dma((5,))],
        compiler_params=pltpu.CompilerParams(vmem_limit_bytes=8 * 1024 * 1024),
        name="finish",
    )(*results)
    return mixed[None], gq[None], gk[None], gv[None], gw


def solution(mesh):
    positions = mesh.shape["dp"] * mesh.shape["ctx"] * HEAD
    loss_scale = 1.0 / math.sqrt(positions)

    def run(*args):
        return on_device(loss_scale, *args)

    split = P("dp", "ctx", None)
    return jax.shard_map(
        run,
        mesh=mesh,
        in_specs=(split, split, split, P(), P("ctx", None), split),
        out_specs=(split, split, split, split, P("ctx", None)),
        check_vma=False,
    )
```

```python
import math

import jax
import jax.numpy as jnp
from jax import lax
from jax.experimental import pallas as pl
from jax.experimental.pallas import tpu as pltpu
from jax.sharding import PartitionSpec as P

MESH = pl.DeviceIdType.MESH
F32 = jnp.float32
BF16 = jnp.bfloat16
HEAD = 128
EPSILON = 1e-06
NZ = 8
NX = 4
NY = 4
CHIPS = 16
HALF = 1024
CHUNKS = 2
CHUNK = 2048 // CHUNKS
WIDE = CHUNK // 2


def dot(a, b, ca, cb):
    return lax.dot_general(a, b, (((ca,), (cb,)), ((), ())), preferred_element_type=F32)


def rcopy(src, dst, send, recv, device):
    return pltpu.make_async_remote_copy(
        src_ref=src, dst_ref=dst, send_sem=send, recv_sem=recv, device_id=device, device_id_type=MESH
    )


def exp_low(wide):
    return jnp.exp(jnp.minimum(wide, 0.0))


def feature(values):
    wide = values.astype(F32)
    return jnp.where(wide > 0, wide + 1.0, exp_low(wide)).astype(BF16)


def slope(values):
    wide = values.astype(F32)
    return jnp.where(wide > 0, 1.0, exp_low(wide))


def kernel(
    loss_scale,
    q_hbm, k_hbm, v_hbm, gain_hbm, w_hbm, cot_hbm,
    mixed_ref, gq_ref, gk_ref, gv_ref, gw_ref,
    q_ref, k_ref, v_ref, gain_ref, w_ref, cot_ref, in_s,
    fq, fk, probs, att, dnorm, normed, datt, dfk, dgv, local, inverse,
    xsend, xrecv, pieces, got, back_out, back_in, psend, prefix, suffix,
    wfull, cotg, flipped, normg, gwf, gwt, xh_in, x_out, x_in, z_out, z_in, f_out, f_in,
    sx_s, sx_r, s1_s, s1_r, s2_s, s2_r, sp_s, sp_r,
    up_s, up_r, dn_s, dn_r, wx_s, wx_r, wy_s, wy_r, wp_s, wp_r,
    cu_s, cu_r, cd_s, cd_r, cp_s, cp_r,
    n_s, n_r, xa_s, xa_r, xb_s, xb_r, z_s, z_r, f_s, f_r,
):
    d = lax.axis_index("dp")
    i = lax.axis_index("ctx")
    c = i % 2
    j = i // 2
    z = j % NZ
    xl = j // NZ
    y = d // 2
    xh = d % 2
    x = xh * 2 + xl
    o = 1 - c
    partner = (d, j * 2 + o)

    def chip(jj):
        return (d, jj * 2 + c)

    def at_x(xx):
        return (y * 2 + xx // 2, ((xx % 2) * NZ + z) * 2 + c)

    def at_z(zz):
        return (d, (xl * NZ + zz) * 2 + c)

    def at_y(yy, cc):
        return (yy * 2 + xh, j * 2 + cc)

    def final_to(t):
        return (t, (xl * NZ + z) * 2 + y // 2)

    def final_from(t):
        return ((2 * c + t // 4) * 2 + t % 2, (xl * NZ + z) * 2 + (t // 2) % 2)

    def same(device):
        return jnp.logical_and(device[0] == d, device[1] == i)

    inputs = ((k_hbm, k_ref), (v_hbm, v_ref), (q_hbm, q_ref), (w_hbm, w_ref), (cot_hbm, cot_ref), (gain_hbm, gain_ref))
    loads = [pltpu.make_async_copy(a, b, in_s.at[n]) for n, (a, b) in enumerate(inputs)]
    for load in loads:
        load.start()

    barrier = pltpu.get_barrier_semaphore()

    def greet(device):
        pl.semaphore_signal(barrier, inc=1, device_id=device, device_id_type=MESH)

    def greet_maybe_self(device):
        @pl.when(jnp.logical_not(same(device)))
        def _():
            greet(device)

    for t in range(1, CHIPS):
        greet(chip((j + t) % CHIPS))
    greet(partner)
    for t in range(1, NX):
        greet(at_x((x + t) % NX))
    for t in range(1, NY):
        greet(at_y((y + t) % NY, 0))
        greet(at_y((y + t) % NY, 1))
    for t in range(8):
        greet_maybe_self(final_to(t))
        greet_maybe_self(final_from(t))

    def head(h):
        return pl.ds(pl.multiple_of(h * HEAD, HEAD), HEAD)

    def loop_a(h, _):
        cols = head(h)
        fq[:, cols] = feature(q_ref[:, cols])
        kf = feature(k_ref[:, cols])
        fk[:, cols] = kf
        local[h] = dot(kf, v_ref[:, cols], 0, 0)
        return 0

    for load in loads[:3]:
        load.wait()
    lax.fori_loop(0, 16, loop_a, 0, unroll=4)
    for load in loads[3:]:
        load.wait()

    selves = jnp.where(y // 2 == c, 2, 0)
    pl.semaphore_wait(barrier, 15 + 1 + 3 + 6 + 16 - selves)

    left = pl.ds(0, HALF)
    right = pl.ds(HALF, HALF)

    pending = []

    def begin(copy):
        copy.start()
        pending.append(copy)
        return copy

    def wslot(zz):
        return (xl * NZ + zz) * 2 + c

    def oslot(zz):
        return ((1 - xl) * NZ + zz) * 2 + c

    near_x = (y * 2 + xh, ((1 - xl) * NZ + z) * 2 + c)
    far_x = (y * 2 + (1 - xh), ((1 - xl) * NZ + z) * 2 + c)
    z_up = at_z((z + 1) % NZ)
    z_dn = at_z((z + NZ - 1) % NZ)

    p = y % 2
    mine_w = pl.ds(pl.multiple_of(p * HALF, HALF), HALF)
    rest_w = pl.ds(pl.multiple_of((1 - p) * HALF, HALF), HALF)

    def quarter(side, a):
        return pl.ds(pl.multiple_of(side * HALF + a * 512, 512), 512)

    y_up = at_y((y + 1) % NY, c)
    y_dn = at_y((y + NY - 1) % NY, c)

    def wcols(r, cols, own=False):
        if r == 0 and not own:
            return w_ref.at[:, cols]
        return wfull.at[wslot((z + r) % NZ), :, cols]

    def z_cols(k, a):
        return quarter(p, a) if k == 3 else mine_w

    def w_up(k):
        r = (-k) % NZ
        cols = z_cols(k, 0)
        begin(rcopy(wcols(r, cols), wcols(r, cols, True), up_s.at[k], up_r.at[k], z_up))

    def w_dn(k):
        cols = z_cols(k, 1)
        begin(rcopy(wcols(k, cols), wcols(k, cols, True), dn_s.at[k], dn_r.at[k], z_dn))

    def w_up_wait(k):
        ref = wcols((-k - 1) % NZ, z_cols(k, 0), True)
        rcopy(ref, ref, up_s.at[k], up_r.at[k], z_up).wait_recv()

    def w_dn_wait(k):
        ref = wcols(k + 1, z_cols(k, 1), True)
        rcopy(ref, ref, dn_s.at[k], dn_r.at[k], z_dn).wait_recv()

    def w_near(r):
        begin(rcopy(wcols(r, mine_w), wcols(r, mine_w, True), wx_s.at[r, 0], wx_r.at[r, 0], near_x))

    def w_far(r):
        begin(rcopy(wcols(r, rest_w), wcols(r, rest_w, True), wx_s.at[r, 1], wx_r.at[r, 1], far_x))

    def w_pair(r):
        dst = wfull.at[wslot((z + r) % NZ)]
        begin(rcopy(w_ref if r == 0 else dst, dst, wp_s.at[r], wp_r.at[r], partner))

    def w_side(r, a):
        ref = wcols(r, quarter(p, a))
        begin(rcopy(ref, ref, wy_s.at[r, a], wy_r.at[r, a], y_dn if a else y_up))

    def w_first():
        w_up(0)
        w_dn(0)
        w_near(0)
        w_far(0)
        w_pair(0)

    def w_step(k):
        w_up_wait(k - 1)
        w_up(k)
        w_dn_wait(k - 1)
        w_dn(k)
        for r in ((-k) % NZ, k):
            w_near(r)
            w_side(r, 0)
            w_side(r, 1)

    def w_last():
        w_up_wait(3)
        w_side(4, 0)
        w_dn_wait(3)
        w_side(4, 1)
        w_near(4)

    def w_rest(r):
        for a in (0, 1):
            ref = wcols(r, quarter(1 - p, a))
            rcopy(ref, ref, wy_s.at[r, a], wy_r.at[r, a], y_up).wait_recv()
        w_far(r)
        w_pair(r)

    def w_other(r):
        slot = oslot((z + r) % NZ)
        for a, cols in ((0, mine_w), (1, rest_w)):
            ref = wfull.at[slot, :, cols]
            rcopy(ref, ref, wx_s.at[r, a], wx_r.at[r, a], near_x).wait_recv()
        begin(rcopy(wfull.at[slot], wfull.at[slot], wp_s.at[8 + r], wp_r.at[8 + r], partner))

    def w_pair_wait():
        for r in range(16):
            zz = (z + r) % NZ
            side = xl if r < 8 else 1 - xl
            ref = wfull.at[(side * NZ + zz) * 2 + o]
            rcopy(ref, ref, wp_s.at[r], wp_r.at[r], partner).wait_recv()

    def cslot(r):
        return ((y + r) % NY) * 2 + c

    def c_first():
        own = cotg.at[cslot(0)]
        begin(rcopy(cot_ref, own, cu_s.at[0], cu_r.at[0], y_up))
        begin(rcopy(cot_ref, own, cd_s.at[0], cd_r.at[0], y_dn))
        begin(rcopy(cot_ref, own, cp_s.at[0], cp_r.at[0], partner))

    def c_pair(r):
        ref = cotg.at[cslot(r)]
        begin(rcopy(ref, ref, cp_s.at[r], cp_r.at[r], partner))

    def c_second():
        below = cotg.at[cslot(3)]
        rcopy(below, below, cu_s.at[0], cu_r.at[0], y_up).wait_recv()
        part = cotg.at[cslot(3), :, left]
        begin(rcopy(part, part, cu_s.at[1], cu_r.at[1], y_up))
        above = cotg.at[cslot(1)]
        rcopy(above, above, cd_s.at[0], cd_r.at[0], y_dn).wait_recv()
        part = cotg.at[cslot(1), :, right]
        begin(rcopy(part, part, cd_s.at[1], cd_r.at[1], y_dn))
        c_pair(3)
        c_pair(1)

    def c_third():
        a = cotg.at[cslot(2), :, left]
        rcopy(a, a, cu_s.at[1], cu_r.at[1], y_up).wait_recv()
        b = cotg.at[cslot(2), :, right]
        rcopy(b, b, cd_s.at[1], cd_r.at[1], y_dn).wait_recv()
        c_pair(2)

    def c_wait():
        for r in range(4):
            ref = cotg.at[((y + r) % NY) * 2 + o]
            rcopy(ref, ref, cp_s.at[r], cp_r.at[r], partner).wait_recv()

    own_heads = pl.ds(8 * c, 8)
    other_heads = pl.ds(8 * o, 8)

    def scan_pair(n):
        xsend[n] = local[other_heads].astype(BF16)
        begin(rcopy(xsend.at[n], xrecv.at[n], sx_s.at[n], sx_r.at[n], partner))

    def scan_spread(n):
        rcopy(xrecv.at[n], xrecv.at[n], sx_s.at[n], sx_r.at[n], partner).wait_recv()
        total = (local[own_heads] + xrecv[n].astype(F32)).astype(BF16)
        pieces[n] = total.reshape(CHIPS, 64, HEAD)
        for t in range(1, CHIPS):
            jj = (j + t) % CHIPS
            begin(rcopy(pieces.at[n, jj], got.at[n, j], s1_s.at[n, jj], s1_r.at[n, j], chip(jj)))
        got[n, j] = pieces[n, j]

    def scan_return(n):
        for t in range(1, CHIPS):
            jj = (j + t) % CHIPS
            ref = got.at[n, jj]
            rcopy(ref, ref, s1_s.at[n, jj], s1_r.at[n, jj], partner).wait_recv()
        total = jnp.zeros((64, HEAD), F32)
        order = range(CHIPS) if n == 0 else range(CHIPS - 1, -1, -1)
        for jj in order:
            back_out[n, jj] = total.astype(BF16)
            total = total + got[n, jj].astype(F32)
        for t in range(1, CHIPS):
            jj = (j + t) % CHIPS
            begin(rcopy(back_out.at[n, jj], back_in.at[n, j], s2_s.at[n, jj], s2_r.at[n, j], chip(jj)))
        back_in[n, j] = back_out[n, j]

    def scan_share(n, out):
        for t in range(1, CHIPS):
            jj = (j + t) % CHIPS
            ref = back_in.at[n, jj]
            rcopy(ref, ref, s2_s.at[n, jj], s2_r.at[n, jj], partner).wait_recv()
        mine = back_in[n].astype(F32).reshape(8, HEAD, HEAD)
        last = (c if n == 0 else o).astype(F32)
        psend[n] = (mine + (1.0 - last) * local[own_heads]).astype(BF16)
        begin(rcopy(psend.at[n], out.at[own_heads], sp_s.at[n], sp_r.at[n], partner))
        out[own_heads] = (mine + last * xrecv[n].astype(F32)).astype(BF16)

    def scan_wait(n, out):
        ref = out.at[other_heads]
        rcopy(ref, ref, sp_s.at[n], sp_r.at[n], partner).wait_recv()

    me8 = y * 2 + c

    def positions(b):
        return pl.ds(pl.multiple_of(b * HEAD, HEAD), HEAD)

    def n_send():
        for t in range(1, 8):
            b = (me8 + t) % 8
            begin(
                rcopy(
                    flipped.at[:, b],
                    normg.at[:, :, positions(me8)],
                    n_s.at[b],
                    n_r.at[me8],
                    at_y(b // 2, b % 2),
                )
            )
        normg[:, :, positions(me8)] = flipped[:, me8]

    def n_wait():
        for t in range(1, 8):
            b = (me8 + t) % 8
            ref = normg.at[:, :, positions(b)]
            rcopy(ref, ref, n_s.at[b], n_r.at[b], partner).wait_recv()

    x_up = at_x((x + 1) % NX)
    x_dn = at_x((x + 3) % NX)
    two = (x + 2) % NX
    one_up = (x + 1) % NX
    one_dn = (x + 3) % NX

    def piece(k, h, lo, size):
        cols = pl.ds(pl.multiple_of(h * CHUNK + (k // 2) * WIDE + lo, HEAD), size)
        return pl.ds(8 * (k % 2), 8), slice(None), cols

    lows, highs = pl.ds(0, WIDE // 2), pl.ds(WIDE // 2, WIDE // 2)

    def low(k, h):
        return piece(k, h, 0, WIDE // 2)

    def high(k, h):
        return piece(k, h, WIDE // 2, WIDE // 2)

    def g_tile(h):
        def loop_g(n, _):
            cols = pl.ds(pl.multiple_of(h * CHUNK + n * 512, 512), 512)
            tile = dot(normg[...].reshape(256, 1024), cotg[:, :, cols].reshape(1024, 512), 1, 0)
            gwf[:, :, cols] = tile.reshape(16, 16, 512)
            gwt[:, :, cols] = tile.astype(BF16).reshape(16, 16, 512)
            return 0

        lax.fori_loop(0, CHUNK // 512, loop_g, 0)

    def g_first(h):
        begin(rcopy(gwt.at[low(two, h)], xh_in.at[h, 0], xa_s.at[h, 0], xa_r.at[h, 0], x_up))
        begin(rcopy(gwt.at[high(two, h)], xh_in.at[h, 1], xa_s.at[h, 1], xa_r.at[h, 1], x_dn))

    def g_second(h):
        for a, to in ((0, x_up), (1, x_dn)):
            rcopy(xh_in.at[h, a], xh_in.at[h, a], xa_s.at[h, a], xa_r.at[h, a], to).wait_recv()
        x_out[h, 0, :, :, lows] = (gwf[low(one_up, h)] + xh_in[h, 0].astype(F32)).astype(BF16)
        x_out[h, 0, :, :, highs] = gwt[high(one_up, h)]
        x_out[h, 1, :, :, lows] = gwt[low(one_dn, h)]
        x_out[h, 1, :, :, highs] = (gwf[high(one_dn, h)] + xh_in[h, 1].astype(F32)).astype(BF16)
        begin(rcopy(x_out.at[h, 0], x_in.at[h, 0], xb_s.at[h, 0], xb_r.at[h, 0], x_up))
        begin(rcopy(x_out.at[h, 1], x_in.at[h, 1], xb_s.at[h, 1], xb_r.at[h, 1], x_dn))

    def g_third(h):
        for a, to in ((0, x_up), (1, x_dn)):
            rcopy(x_in.at[h, a], x_in.at[h, a], xb_s.at[h, a], xb_r.at[h, a], to).wait_recv()
        total = gwf[piece(x, h, 0, WIDE)] + x_in[h, 0].astype(F32) + x_in[h, 1].astype(F32)
        z_out[h] = total.astype(BF16)
        for t in range(1, NZ):
            zz = (z + t) % NZ
            begin(rcopy(z_out.at[h, zz], z_in.at[h, z], z_s.at[h, zz], z_r.at[h, z], at_z(zz)))
        z_in[h, z] = z_out[h, z]

    me_f = (2 * (y % 2) + c) * 2 + xh

    def f_copy(h, t):
        return rcopy(f_out.at[h], f_in.at[h, me_f], f_s.at[h, t], f_r.at[h, me_f], final_to(t))

    def g_fourth(h):
        for t in range(1, NZ):
            zz = (z + t) % NZ
            ref = z_in.at[h, zz]
            rcopy(ref, ref, z_s.at[h, zz], z_r.at[h, zz], partner).wait_recv()
        whole = z_in[h, 0].astype(F32)
        for zz in range(1, NZ):
            whole = whole + z_in[h, zz].astype(F32)
        f_out[h] = whole.astype(BF16)
        for t in range(8):
            to = final_to(t)

            @pl.when(jnp.logical_not(same(to)))
            def _(t=t):
                f_copy(h, t).start()

            @pl.when(same(to))
            def _():
                f_in[h, me_f] = f_out[h]

    def g_end(h):
        for t in range(8):
            source = final_from(t)

            @pl.when(jnp.logical_not(same(source)))
            def _(source=source, t=t):
                ref = f_in.at[h, t]
                rcopy(ref, ref, f_s.at[h, t], f_r.at[h, t], source).wait_recv()

            row, col = 16 * (t // 2), h * CHUNK + WIDE * (t % 2)
            gw_ref[row : row + 16, col : col + WIDE] = f_in[h, t].astype(F32) * loss_scale
        for t in range(8):
            to = final_to(t)

            @pl.when(jnp.logical_not(same(to)))
            def _(t=t):
                f_copy(h, t).wait_send()

    rows_at = lax.broadcasted_iota(jnp.int32, (HEAD, HEAD), 0)
    cols_at = lax.broadcasted_iota(jnp.int32, (HEAD, HEAD), 1)
    causal = rows_at >= cols_at

    def loop_b(h, _):
        cols = head(h)
        scores = dot(fq[:, cols], fk[:, cols], 1, 1)
        p = jnp.where(causal, scores, 0.0).astype(BF16)
        probs[h] = p
        att[:, cols] = dot(p, v_ref[:, cols], 1, 0)
        return 0

    def loop_c(h2, _):
        cols = pl.ds(pl.multiple_of(h2 * 256, 256), 256)
        rows = wfull[pl.ds(h2 * 4, 4)].reshape(256, 2048)
        dnorm[:, cols] = dot(cot_ref[...], rows, 1, 1) * gain_ref[:, cols]
        return 0

    def loop_n(h, _):
        cols = head(h)
        a = att[:, cols] + dot(fq[:, cols], prefix[h], 1, 0)
        inv = lax.rsqrt(jnp.mean(a * a, axis=-1, keepdims=True) + EPSILON)
        att[:, cols] = a
        inverse[h] = inv
        out = a * inv * gain_ref[:, cols]
        normed[:, cols] = out.astype(BF16)
        flipped[h] = jnp.transpose(out).astype(BF16).reshape(8, 16, HEAD)
        return 0

    def loop_d(h, _):
        cols = head(h)
        a = att[:, cols]
        inv = inverse[h]
        s = dnorm[:, cols]
        m = jnp.mean(s * a, axis=-1, keepdims=True)
        g = (inv * (s - a * inv * inv * m)).astype(BF16)
        datt[:, cols] = g
        local[h] = dot(fq[:, cols], g, 0, 0)
        return 0

    def loop_e(h, _):
        cols = head(h)
        g = datt[:, cols]
        fkh = fk[:, cols]
        dp = jnp.where(causal, dot(g, v_ref[:, cols], 1, 1), 0.0).astype(BF16)
        dfq = dot(dp, fkh, 1, 0) + dot(g, prefix[h], 1, 1)
        gq_ref[:, cols] = (dfq * slope(q_ref[:, cols])).astype(BF16)
        dfk[:, cols] = dot(dp, fq[:, cols], 0, 0)
        dgv[:, cols] = dot(probs[h], g, 0, 0)
        return 0

    def loop_m(n, _):
        cols = pl.ds(pl.multiple_of(n * 512, 512), 512)
        rows = wfull[:, :, cols].reshape(2048, 512)
        mixed_ref[:, cols] = dot(normed[...], rows, 1, 0).astype(BF16)
        return 0

    def loop_f(h, _):
        cols = head(h)
        s = suffix[h]
        gk = dfk[:, cols] + dot(v_ref[:, cols], s, 1, 1)
        gk_ref[:, cols] = (gk * slope(k_ref[:, cols])).astype(BF16)
        gv_ref[:, cols] = (dgv[:, cols] + dot(fk[:, cols], s, 1, 0)).astype(BF16)
        return 0

    scan_pair(0)
    w_first()
    c_first()
    scan_spread(0)
    wfull[i] = w_ref[...]
    cotg[cslot(0)] = cot_ref[...]
    w_step(1)
    lax.fori_loop(0, 16, loop_b, 0, unroll=4)
    scan_return(0)
    w_step(2)
    c_second()
    w_rest(1)
    w_rest(7)
    w_rest(2)
    w_rest(6)
    scan_share(0, prefix)
    w_step(3)
    scan_wait(0, prefix)
    lax.fori_loop(0, 16, loop_n, 0, unroll=4)
    n_send()
    c_third()
    w_last()
    for r in (0, 1, 7):
        w_other(r)
    for r in (3, 5):
        w_rest(r)
    for r in (2, 6):
        w_other(r)
    w_rest(4)
    c_wait()
    n_wait()
    for h in range(CHUNKS):
        g_tile(h)
        g_first(h)
    for r in (3, 5, 4):
        w_other(r)
    w_pair_wait()
    lax.fori_loop(0, 8, loop_c, 0)
    lax.fori_loop(0, 16, loop_d, 0, unroll=4)
    scan_pair(1)
    g_second(0)
    scan_spread(1)
    for h in range(1, CHUNKS):
        g_second(h)
    lax.fori_loop(0, 8, loop_e, 0, unroll=4)
    g_third(0)
    lax.fori_loop(8, 16, loop_e, 0, unroll=4)
    for h in range(1, CHUNKS):
        g_third(h)
    scan_return(1)
    g_fourth(0)
    lax.fori_loop(0, 4, loop_m, 0)
    for h in range(1, CHUNKS):
        g_fourth(h)
    scan_share(1, suffix)
    scan_wait(1, suffix)
    lax.fori_loop(0, 16, loop_f, 0, unroll=4)
    for copy in pending:
        copy.wait_send()
    for h in range(CHUNKS):
        g_end(h)


def finish(*refs):
    copies = [pltpu.make_async_copy(refs[n], refs[5 + n], refs[10].at[n]) for n in range(5)]
    for copy in copies:
        copy.start()
    for copy in copies:
        copy.wait()


def on_device(loss_scale, query_rows, key_rows, value_rows, norm_gain, out_weight, cotangent):
    length, width = query_rows.shape[1:]
    rows = out_weight.shape[0]
    vmem = pl.BlockSpec(memory_space=pltpu.VMEM)
    hbm = pl.BlockSpec(memory_space=pltpu.HBM)
    block = jax.ShapeDtypeStruct((length, width), BF16)
    dma = pltpu.SemaphoreType.DMA
    states = (16, HEAD, HEAD)
    scratch = [
        pltpu.VMEM((length, width), BF16),
        pltpu.VMEM((length, width), BF16),
        pltpu.VMEM((length, width), BF16),
        pltpu.VMEM((1, width), F32),
        pltpu.VMEM((rows, width), BF16),
        pltpu.VMEM((length, width), BF16),
        dma((6,)),
        pltpu.VMEM((length, width), BF16),
        pltpu.VMEM((length, width), BF16),
        pltpu.VMEM(states, BF16),
        pltpu.VMEM((length, width), F32),
        pltpu.VMEM((length, width), F32),
        pltpu.VMEM((length, width), BF16),
        pltpu.VMEM((length, width), BF16),
        pltpu.VMEM((length, width), F32),
        pltpu.VMEM((length, width), F32),
        pltpu.VMEM(states, F32),
        pltpu.VMEM((16, length, 1), F32),
        pltpu.VMEM((2, 8, HEAD, HEAD), BF16),
        pltpu.VMEM((2, 8, HEAD, HEAD), BF16),
        pltpu.VMEM((2, CHIPS, 64, HEAD), BF16),
        pltpu.VMEM((2, CHIPS, 64, HEAD), BF16),
        pltpu.VMEM((2, CHIPS, 64, HEAD), BF16),
        pltpu.VMEM((2, CHIPS, 64, HEAD), BF16),
        pltpu.VMEM((2, 8, HEAD, HEAD), BF16),
        pltpu.VMEM(states, BF16),
        pltpu.VMEM(states, BF16),
        pltpu.VMEM((32, 64, width), BF16),
        pltpu.VMEM((8, length, width), BF16),
        pltpu.VMEM((16, 8, 16, length), BF16),
        pltpu.VMEM((16, 16, 8 * length), BF16),
        pltpu.VMEM((16, 16, width), F32),
        pltpu.VMEM((16, 16, width), BF16),
        pltpu.VMEM((CHUNKS, 2, 8, 16, WIDE // 2), BF16),
        pltpu.VMEM((CHUNKS, 2, 8, 16, WIDE), BF16),
        pltpu.VMEM((CHUNKS, 2, 8, 16, WIDE), BF16),
        pltpu.VMEM((CHUNKS, 8, 16, WIDE), BF16),
        pltpu.VMEM((CHUNKS, 8, 16, WIDE), BF16),
        pltpu.VMEM((CHUNKS, 16, WIDE), BF16),
        pltpu.VMEM((CHUNKS, 8, 16, WIDE), BF16),
        dma((2,)), dma((2,)), dma((2, 16)), dma((2, 16)), dma((2, 16)), dma((2, 16)), dma((2,)), dma((2,)),
        dma((4,)), dma((4,)), dma((4,)), dma((4,)), dma((8, 2)), dma((8, 2)), dma((8, 2)), dma((8, 2)), dma((16,)), dma((16,)),
        dma((2,)), dma((2,)), dma((2,)), dma((2,)), dma((4,)), dma((4,)),
        dma((8,)), dma((8,)),
        dma((CHUNKS, 2)), dma((CHUNKS, 2)), dma((CHUNKS, 2)), dma((CHUNKS, 2)),
        dma((CHUNKS, 8)), dma((CHUNKS, 8)), dma((CHUNKS, 8)), dma((CHUNKS, 8)),
    ]

    def body(*refs):
        kernel(loss_scale, *refs)

    shapes = (block, block, block, block, jax.ShapeDtypeStruct((rows, width), F32))
    results = pl.pallas_call(
        body,
        out_shape=shapes,
        in_specs=[hbm] * 6,
        out_specs=(vmem,) * 5,
        scratch_shapes=scratch,
        compiler_params=pltpu.CompilerParams(
            collective_id=0, has_side_effects=True, vmem_limit_bytes=44 * 1024 * 1024
        ),
        name="layer",
    )(
        *(pltpu.with_memory_space_constraint(a, pltpu.HBM) for a in (query_rows[0], key_rows[0], value_rows[0])),
        pltpu.with_memory_space_constraint(norm_gain.reshape(1, width), pltpu.HBM),
        *(pltpu.with_memory_space_constraint(a, pltpu.HBM) for a in (out_weight, cotangent[0])),
    )
    anywhere = pl.BlockSpec(memory_space=pl.ANY)
    mixed, gq, gk, gv, gw = pl.pallas_call(
        finish,
        out_shape=shapes,
        in_specs=[anywhere] * 5,
        out_specs=(hbm,) * 5,
        scratch_shapes=[dma((5,))],
        compiler_params=pltpu.CompilerParams(vmem_limit_bytes=8 * 1024 * 1024),
        name="finish",
    )(*results)
    return mixed[None], gq[None], gk[None], gv[None], gw


def solution(mesh):
    positions = mesh.shape["dp"] * mesh.shape["ctx"] * HEAD
    loss_scale = 1.0 / math.sqrt(positions)

    def run(*args):
        return on_device(loss_scale, *args)

    split = P("dp", "ctx", None)
    return jax.shard_map(
        run,
        mesh=mesh,
        in_specs=(split, split, split, P(), P("ctx", None), split),
        out_specs=(split, split, split, split, P("ctx", None)),
        check_vma=False,
    )
```

```python
import math

import jax
import jax.numpy as jnp
from jax import lax
from jax.experimental import pallas as pl
from jax.experimental.pallas import tpu as pltpu
from jax.sharding import PartitionSpec as P

MESH = pl.DeviceIdType.MESH
F32 = jnp.float32
BF16 = jnp.bfloat16
HEAD = 128
EPSILON = 1e-06
NZ = 8
NX = 4
NY = 4
CHIPS = 16
HALF = 1024
CHUNKS = 2
CHUNK = 2048 // CHUNKS
WIDE = CHUNK // 2


def dot(a, b, ca, cb):
    return lax.dot_general(a, b, (((ca,), (cb,)), ((), ())), preferred_element_type=F32)


def rcopy(src, dst, send, recv, device):
    return pltpu.make_async_remote_copy(
        src_ref=src, dst_ref=dst, send_sem=send, recv_sem=recv, device_id=device, device_id_type=MESH
    )


def exp_low(wide):
    return jnp.exp(jnp.minimum(wide, 0.0))


def feature(values):
    wide = values.astype(F32)
    return jnp.where(wide > 0, wide + 1.0, exp_low(wide)).astype(BF16)


def slope(values):
    wide = values.astype(F32)
    return jnp.where(wide > 0, 1.0, exp_low(wide))


def kernel(
    loss_scale,
    q_hbm, k_hbm, v_hbm, gain_hbm, w_hbm, cot_hbm,
    mixed_ref, gq_ref, gk_ref, gv_ref, gw_ref,
    q_ref, k_ref, v_ref, gain_ref, w_ref, cot_ref, in_s,
    fq, fk, probs, att, dnorm, normed, datt, dfk, dgv, local, inverse,
    xsend, xrecv, pieces, got, back_out, back_in, psend, prefix, suffix,
    wfull, cotg, flipped, normg, gwf, gwt, xh_in, x_out, x_in, z_out, z_in, f_out, f_in,
    sx_s, sx_r, s1_s, s1_r, s2_s, s2_r, sp_s, sp_r,
    up_s, up_r, dn_s, dn_r, wx_s, wx_r, wy_s, wy_r, wp_s, wp_r,
    cu_s, cu_r, cd_s, cd_r, cp_s, cp_r,
    n_s, n_r, xa_s, xa_r, xb_s, xb_r, z_s, z_r, f_s, f_r,
):
    d = lax.axis_index("dp")
    i = lax.axis_index("ctx")
    c = i % 2
    j = i // 2
    z = j % NZ
    xl = j // NZ
    y = d // 2
    xh = d % 2
    x = xh * 2 + xl
    o = 1 - c
    partner = (d, j * 2 + o)

    def chip(jj):
        return (d, jj * 2 + c)

    def at_x(xx):
        return (y * 2 + xx // 2, ((xx % 2) * NZ + z) * 2 + c)

    def at_z(zz):
        return (d, (xl * NZ + zz) * 2 + c)

    def at_y(yy, cc):
        return (yy * 2 + xh, j * 2 + cc)

    def final_to(t):
        return (t, (xl * NZ + z) * 2 + y // 2)

    def final_from(t):
        return ((2 * c + t // 4) * 2 + t % 2, (xl * NZ + z) * 2 + (t // 2) % 2)

    def same(device):
        return jnp.logical_and(device[0] == d, device[1] == i)

    inputs = ((k_hbm, k_ref), (v_hbm, v_ref), (q_hbm, q_ref), (w_hbm, w_ref), (cot_hbm, cot_ref), (gain_hbm, gain_ref))
    loads = [pltpu.make_async_copy(a, b, in_s.at[n]) for n, (a, b) in enumerate(inputs)]
    for load in loads:
        load.start()

    barrier = pltpu.get_barrier_semaphore()

    def greet(device):
        pl.semaphore_signal(barrier, inc=1, device_id=device, device_id_type=MESH)

    def greet_maybe_self(device):
        @pl.when(jnp.logical_not(same(device)))
        def _():
            greet(device)

    for t in range(1, CHIPS):
        greet(chip((j + t) % CHIPS))
    greet(partner)
    for t in range(1, NX):
        greet(at_x((x + t) % NX))
    for t in range(1, NY):
        greet(at_y((y + t) % NY, 0))
        greet(at_y((y + t) % NY, 1))
    for t in range(8):
        greet_maybe_self(final_to(t))
        greet_maybe_self(final_from(t))

    def head(h):
        return pl.ds(pl.multiple_of(h * HEAD, HEAD), HEAD)

    def loop_a(h, _):
        cols = head(h)
        fq[:, cols] = feature(q_ref[:, cols])
        kf = feature(k_ref[:, cols])
        fk[:, cols] = kf
        local[h] = dot(kf, v_ref[:, cols], 0, 0)
        return 0

    for load in loads[:3]:
        load.wait()
    lax.fori_loop(0, 16, loop_a, 0, unroll=8)
    for load in loads[3:]:
        load.wait()

    selves = jnp.where(y // 2 == c, 2, 0)
    pl.semaphore_wait(barrier, 15 + 1 + 3 + 6 + 16 - selves)

    left = pl.ds(0, HALF)
    right = pl.ds(HALF, HALF)

    pending = []

    def begin(copy):
        copy.start()
        pending.append(copy)
        return copy

    def wslot(zz):
        return (xl * NZ + zz) * 2 + c

    def oslot(zz):
        return ((1 - xl) * NZ + zz) * 2 + c

    near_x = (y * 2 + xh, ((1 - xl) * NZ + z) * 2 + c)
    far_x = (y * 2 + (1 - xh), ((1 - xl) * NZ + z) * 2 + c)
    z_up = at_z((z + 1) % NZ)
    z_dn = at_z((z + NZ - 1) % NZ)

    p = y % 2
    mine_w = pl.ds(pl.multiple_of(p * HALF, HALF), HALF)
    rest_w = pl.ds(pl.multiple_of((1 - p) * HALF, HALF), HALF)

    def quarter(side, a):
        return pl.ds(pl.multiple_of(side * HALF + a * 512, 512), 512)

    y_up = at_y((y + 1) % NY, c)
    y_dn = at_y((y + NY - 1) % NY, c)

    def wcols(r, cols, own=False):
        if r == 0 and not own:
            return w_ref.at[:, cols]
        return wfull.at[wslot((z + r) % NZ), :, cols]

    def z_cols(k, a):
        return quarter(p, a) if k == 3 else mine_w

    def w_up(k):
        r = (-k) % NZ
        cols = z_cols(k, 0)
        begin(rcopy(wcols(r, cols), wcols(r, cols, True), up_s.at[k], up_r.at[k], z_up))

    def w_dn(k):
        cols = z_cols(k, 1)
        begin(rcopy(wcols(k, cols), wcols(k, cols, True), dn_s.at[k], dn_r.at[k], z_dn))

    def w_up_wait(k):
        ref = wcols((-k - 1) % NZ, z_cols(k, 0), True)
        rcopy(ref, ref, up_s.at[k], up_r.at[k], z_up).wait_recv()

    def w_dn_wait(k):
        ref = wcols(k + 1, z_cols(k, 1), True)
        rcopy(ref, ref, dn_s.at[k], dn_r.at[k], z_dn).wait_recv()

    def w_near(r):
        begin(rcopy(wcols(r, mine_w), wcols(r, mine_w, True), wx_s.at[r, 0], wx_r.at[r, 0], near_x))

    def w_far(r):
        begin(rcopy(wcols(r, rest_w), wcols(r, rest_w, True), wx_s.at[r, 1], wx_r.at[r, 1], far_x))

    def w_pair(r):
        dst = wfull.at[wslot((z + r) % NZ)]
        begin(rcopy(w_ref if r == 0 else dst, dst, wp_s.at[r], wp_r.at[r], partner))

    def w_side(r, a):
        ref = wcols(r, quarter(p, a))
        begin(rcopy(ref, ref, wy_s.at[r, a], wy_r.at[r, a], y_dn if a else y_up))

    def w_first():
        w_up(0)
        w_dn(0)
        w_near(0)
        w_far(0)
        w_pair(0)

    def w_step(k):
        w_up_wait(k - 1)
        w_up(k)
        w_dn_wait(k - 1)
        w_dn(k)
        for r in ((-k) % NZ, k):
            w_near(r)
            w_side(r, 0)
            w_side(r, 1)

    def w_last():
        w_up_wait(3)
        w_side(4, 0)
        w_dn_wait(3)
        w_side(4, 1)
        w_near(4)

    def w_rest(r):
        for a in (0, 1):
            ref = wcols(r, quarter(1 - p, a))
            rcopy(ref, ref, wy_s.at[r, a], wy_r.at[r, a], y_up).wait_recv()
        w_far(r)
        w_pair(r)

    def w_other(r):
        slot = oslot((z + r) % NZ)
        for a, cols in ((0, mine_w), (1, rest_w)):
            ref = wfull.at[slot, :, cols]
            rcopy(ref, ref, wx_s.at[r, a], wx_r.at[r, a], near_x).wait_recv()
        begin(rcopy(wfull.at[slot], wfull.at[slot], wp_s.at[8 + r], wp_r.at[8 + r], partner))

    def w_pair_wait(own):
        for r in range(8) if own else range(8, 16):
            zz = (z + r) % NZ
            side = xl if r < 8 else 1 - xl
            ref = wfull.at[(side * NZ + zz) * 2 + o]
            rcopy(ref, ref, wp_s.at[r], wp_r.at[r], partner).wait_recv()

    def cslot(r):
        return ((y + r) % NY) * 2 + c

    def c_first():
        own = cotg.at[cslot(0)]
        begin(rcopy(cot_ref, own, cu_s.at[0], cu_r.at[0], y_up))
        begin(rcopy(cot_ref, own, cd_s.at[0], cd_r.at[0], y_dn))
        begin(rcopy(cot_ref, own, cp_s.at[0], cp_r.at[0], partner))

    def c_pair(r):
        ref = cotg.at[cslot(r)]
        begin(rcopy(ref, ref, cp_s.at[r], cp_r.at[r], partner))

    def c_second():
        below = cotg.at[cslot(3)]
        rcopy(below, below, cu_s.at[0], cu_r.at[0], y_up).wait_recv()
        part = cotg.at[cslot(3), :, left]
        begin(rcopy(part, part, cu_s.at[1], cu_r.at[1], y_up))
        above = cotg.at[cslot(1)]
        rcopy(above, above, cd_s.at[0], cd_r.at[0], y_dn).wait_recv()
        part = cotg.at[cslot(1), :, right]
        begin(rcopy(part, part, cd_s.at[1], cd_r.at[1], y_dn))
        c_pair(3)
        c_pair(1)

    def c_third():
        a = cotg.at[cslot(2), :, left]
        rcopy(a, a, cu_s.at[1], cu_r.at[1], y_up).wait_recv()
        b = cotg.at[cslot(2), :, right]
        rcopy(b, b, cd_s.at[1], cd_r.at[1], y_dn).wait_recv()
        c_pair(2)

    def c_wait():
        for r in range(4):
            ref = cotg.at[((y + r) % NY) * 2 + o]
            rcopy(ref, ref, cp_s.at[r], cp_r.at[r], partner).wait_recv()

    own_heads = pl.ds(8 * c, 8)
    other_heads = pl.ds(8 * o, 8)

    def scan_pair(n):
        xsend[n] = local[other_heads].astype(BF16)
        begin(rcopy(xsend.at[n], xrecv.at[n], sx_s.at[n], sx_r.at[n], partner))

    def scan_spread(n):
        rcopy(xrecv.at[n], xrecv.at[n], sx_s.at[n], sx_r.at[n], partner).wait_recv()
        total = (local[own_heads] + xrecv[n].astype(F32)).astype(BF16)
        pieces[n] = total.reshape(CHIPS, 64, HEAD)
        for t in range(1, CHIPS):
            jj = (j + t) % CHIPS
            begin(rcopy(pieces.at[n, jj], got.at[n, j], s1_s.at[n, jj], s1_r.at[n, j], chip(jj)))
        got[n, j] = pieces[n, j]

    def scan_return(n):
        for t in range(1, CHIPS):
            jj = (j + t) % CHIPS
            ref = got.at[n, jj]
            rcopy(ref, ref, s1_s.at[n, jj], s1_r.at[n, jj], partner).wait_recv()
        total = jnp.zeros((64, HEAD), F32)
        order = range(CHIPS) if n == 0 else range(CHIPS - 1, -1, -1)
        for jj in order:
            back_out[n, jj] = total.astype(BF16)
            total = total + got[n, jj].astype(F32)
        for t in range(1, CHIPS):
            jj = (j + t) % CHIPS
            begin(rcopy(back_out.at[n, jj], back_in.at[n, j], s2_s.at[n, jj], s2_r.at[n, j], chip(jj)))
        back_in[n, j] = back_out[n, j]

    def scan_share(n, out):
        for t in range(1, CHIPS):
            jj = (j + t) % CHIPS
            ref = back_in.at[n, jj]
            rcopy(ref, ref, s2_s.at[n, jj], s2_r.at[n, jj], partner).wait_recv()
        mine = back_in[n].astype(F32).reshape(8, HEAD, HEAD)
        last = (c if n == 0 else o).astype(F32)
        psend[n] = (mine + (1.0 - last) * local[own_heads]).astype(BF16)
        begin(rcopy(psend.at[n], out.at[own_heads], sp_s.at[n], sp_r.at[n], partner))
        out[own_heads] = (mine + last * xrecv[n].astype(F32)).astype(BF16)

    def scan_wait(n, out):
        ref = out.at[other_heads]
        rcopy(ref, ref, sp_s.at[n], sp_r.at[n], partner).wait_recv()

    me8 = y * 2 + c

    def positions(b):
        return pl.ds(pl.multiple_of(b * HEAD, HEAD), HEAD)

    def n_send():
        for t in range(1, 8):
            b = (me8 + t) % 8
            begin(
                rcopy(
                    flipped.at[:, b],
                    normg.at[:, :, positions(me8)],
                    n_s.at[b],
                    n_r.at[me8],
                    at_y(b // 2, b % 2),
                )
            )
        normg[:, :, positions(me8)] = flipped[:, me8]

    def n_wait():
        for t in range(1, 8):
            b = (me8 + t) % 8
            ref = normg.at[:, :, positions(b)]
            rcopy(ref, ref, n_s.at[b], n_r.at[b], partner).wait_recv()

    x_up = at_x((x + 1) % NX)
    x_dn = at_x((x + 3) % NX)
    two = (x + 2) % NX
    one_up = (x + 1) % NX
    one_dn = (x + 3) % NX

    def piece(k, h, lo, size):
        cols = pl.ds(pl.multiple_of(h * CHUNK + (k // 2) * WIDE + lo, HEAD), size)
        return pl.ds(8 * (k % 2), 8), slice(None), cols

    lows, highs = pl.ds(0, WIDE // 2), pl.ds(WIDE // 2, WIDE // 2)

    def low(k, h):
        return piece(k, h, 0, WIDE // 2)

    def high(k, h):
        return piece(k, h, WIDE // 2, WIDE // 2)

    def g_tile(h):
        def loop_g(n, _):
            cols = pl.ds(pl.multiple_of(h * CHUNK + n * 512, 512), 512)
            tile = dot(normg[...].reshape(256, 1024), cotg[:, :, cols].reshape(1024, 512), 1, 0)
            gwf[:, :, cols] = tile.reshape(16, 16, 512)
            gwt[:, :, cols] = tile.astype(BF16).reshape(16, 16, 512)
            return 0

        lax.fori_loop(0, CHUNK // 512, loop_g, 0)

    def g_first(h):
        begin(rcopy(gwt.at[low(two, h)], xh_in.at[h, 0], xa_s.at[h, 0], xa_r.at[h, 0], x_up))
        begin(rcopy(gwt.at[high(two, h)], xh_in.at[h, 1], xa_s.at[h, 1], xa_r.at[h, 1], x_dn))

    def g_second(h):
        for a, to in ((0, x_up), (1, x_dn)):
            rcopy(xh_in.at[h, a], xh_in.at[h, a], xa_s.at[h, a], xa_r.at[h, a], to).wait_recv()
        x_out[h, 0, :, :, lows] = (gwf[low(one_up, h)] + xh_in[h, 0].astype(F32)).astype(BF16)
        x_out[h, 0, :, :, highs] = gwt[high(one_up, h)]
        x_out[h, 1, :, :, lows] = gwt[low(one_dn, h)]
        x_out[h, 1, :, :, highs] = (gwf[high(one_dn, h)] + xh_in[h, 1].astype(F32)).astype(BF16)
        begin(rcopy(x_out.at[h, 0], x_in.at[h, 0], xb_s.at[h, 0], xb_r.at[h, 0], x_up))
        begin(rcopy(x_out.at[h, 1], x_in.at[h, 1], xb_s.at[h, 1], xb_r.at[h, 1], x_dn))

    def g_third(h):
        for a, to in ((0, x_up), (1, x_dn)):
            rcopy(x_in.at[h, a], x_in.at[h, a], xb_s.at[h, a], xb_r.at[h, a], to).wait_recv()
        total = gwf[piece(x, h, 0, WIDE)] + x_in[h, 0].astype(F32) + x_in[h, 1].astype(F32)
        z_out[h] = total.astype(BF16)
        for t in range(1, NZ):
            zz = (z + t) % NZ
            begin(rcopy(z_out.at[h, zz], z_in.at[h, z], z_s.at[h, zz], z_r.at[h, z], at_z(zz)))
        z_in[h, z] = z_out[h, z]

    me_f = (2 * (y % 2) + c) * 2 + xh

    def f_copy(h, t):
        return rcopy(f_out.at[h], f_in.at[h, me_f], f_s.at[h, t], f_r.at[h, me_f], final_to(t))

    def g_fourth(h):
        for t in range(1, NZ):
            zz = (z + t) % NZ
            ref = z_in.at[h, zz]
            rcopy(ref, ref, z_s.at[h, zz], z_r.at[h, zz], partner).wait_recv()
        whole = z_in[h, 0].astype(F32)
        for zz in range(1, NZ):
            whole = whole + z_in[h, zz].astype(F32)
        f_out[h] = whole.astype(BF16)
        for t in range(8):
            to = final_to(t)

            @pl.when(jnp.logical_not(same(to)))
            def _(t=t):
                f_copy(h, t).start()

            @pl.when(same(to))
            def _():
                f_in[h, me_f] = f_out[h]

    def g_end(h):
        for t in range(8):
            source = final_from(t)

            @pl.when(jnp.logical_not(same(source)))
            def _(source=source, t=t):
                ref = f_in.at[h, t]
                rcopy(ref, ref, f_s.at[h, t], f_r.at[h, t], source).wait_recv()

            row, col = 16 * (t // 2), h * CHUNK + WIDE * (t % 2)
            gw_ref[row : row + 16, col : col + WIDE] = f_in[h, t].astype(F32) * loss_scale
        for t in range(8):
            to = final_to(t)

            @pl.when(jnp.logical_not(same(to)))
            def _(t=t):
                f_copy(h, t).wait_send()

    rows_at = lax.broadcasted_iota(jnp.int32, (HEAD, HEAD), 0)
    cols_at = lax.broadcasted_iota(jnp.int32, (HEAD, HEAD), 1)
    causal = rows_at >= cols_at

    def loop_b(h, _):
        cols = head(h)
        scores = dot(fq[:, cols], fk[:, cols], 1, 1)
        p = jnp.where(causal, scores, 0.0).astype(BF16)
        probs[h] = p
        att[:, cols] = dot(p, v_ref[:, cols], 1, 0)
        return 0

    def loop_c(h2, _):
        cols = pl.ds(pl.multiple_of(h2 * 256, 256), 256)
        rows = wfull[pl.ds(h2 * 4, 4)].reshape(256, 2048)
        dnorm[:, cols] = dot(cot_ref[...], rows, 1, 1) * gain_ref[:, cols]
        return 0

    def loop_n(h, _):
        cols = head(h)
        a = att[:, cols] + dot(fq[:, cols], prefix[h], 1, 0)
        inv = lax.rsqrt(jnp.mean(a * a, axis=-1, keepdims=True) + EPSILON)
        att[:, cols] = a
        inverse[h] = inv
        out = a * inv * gain_ref[:, cols]
        normed[:, cols] = out.astype(BF16)
        flipped[h] = jnp.transpose(out).astype(BF16).reshape(8, 16, HEAD)
        return 0

    def loop_d(h, _):
        cols = head(h)
        a = att[:, cols]
        inv = inverse[h]
        s = dnorm[:, cols]
        m = jnp.mean(s * a, axis=-1, keepdims=True)
        g = (inv * (s - a * inv * inv * m)).astype(BF16)
        datt[:, cols] = g
        local[h] = dot(fq[:, cols], g, 0, 0)
        return 0

    def loop_e(h, _):
        cols = head(h)
        g = datt[:, cols]
        fkh = fk[:, cols]
        dp = jnp.where(causal, dot(g, v_ref[:, cols], 1, 1), 0.0).astype(BF16)
        dfq = dot(dp, fkh, 1, 0) + dot(g, prefix[h], 1, 1)
        gq_ref[:, cols] = (dfq * slope(q_ref[:, cols])).astype(BF16)
        dfk[:, cols] = dot(dp, fq[:, cols], 0, 0)
        dgv[:, cols] = dot(probs[h], g, 0, 0)
        return 0

    def loop_m(n, _):
        cols = pl.ds(pl.multiple_of(n * 512, 512), 512)
        rows = wfull[:, :, cols].reshape(2048, 512)
        mixed_ref[:, cols] = dot(normed[...], rows, 1, 0).astype(BF16)
        return 0

    def loop_f(h, _):
        cols = head(h)
        s = suffix[h]
        gk = dfk[:, cols] + dot(v_ref[:, cols], s, 1, 1)
        gk_ref[:, cols] = (gk * slope(k_ref[:, cols])).astype(BF16)
        gv_ref[:, cols] = (dgv[:, cols] + dot(fk[:, cols], s, 1, 0)).astype(BF16)
        return 0

    def half(body, core):
        lax.fori_loop(0, 8, lambda h, _: body(h + 8 * core, 0), 0, unroll=8)

    def weights(side):
        lax.fori_loop(0, 4, lambda h, _: loop_c(h + 4 * side, 0), 0, unroll=4)

    scan_pair(0)
    w_first()
    c_first()
    scan_spread(0)
    wfull[i] = w_ref[...]
    cotg[cslot(0)] = cot_ref[...]
    w_step(1)
    lax.fori_loop(0, 16, loop_b, 0, unroll=8)
    scan_return(0)
    w_step(2)
    c_second()
    w_rest(1)
    w_rest(7)
    w_rest(2)
    w_rest(6)
    scan_share(0, prefix)
    w_step(3)
    half(loop_n, c)
    scan_wait(0, prefix)
    half(loop_n, o)
    n_send()
    c_third()
    w_last()
    for r in (0, 1, 7):
        w_other(r)
    for r in (3, 5):
        w_rest(r)
    for r in (2, 6):
        w_other(r)
    w_rest(4)
    c_wait()
    n_wait()
    for h in range(CHUNKS):
        g_tile(h)
        g_first(h)
    for r in (3, 5, 4):
        w_other(r)
    w_pair_wait(True)
    weights(xl)
    half(loop_d, xl)
    w_pair_wait(False)
    weights(1 - xl)
    half(loop_d, 1 - xl)
    scan_pair(1)
    g_second(0)
    scan_spread(1)
    for h in range(1, CHUNKS):
        g_second(h)
    lax.fori_loop(0, 8, loop_e, 0, unroll=8)
    g_third(0)
    lax.fori_loop(8, 16, loop_e, 0, unroll=8)
    for h in range(1, CHUNKS):
        g_third(h)
    scan_return(1)
    g_fourth(0)
    lax.fori_loop(0, 4, loop_m, 0)
    for h in range(1, CHUNKS):
        g_fourth(h)
    scan_share(1, suffix)
    half(loop_f, c)
    scan_wait(1, suffix)
    half(loop_f, o)
    for copy in pending:
        copy.wait_send()
    for h in range(CHUNKS):
        g_end(h)


def finish(*refs):
    copies = [pltpu.make_async_copy(refs[n], refs[5 + n], refs[10].at[n]) for n in range(5)]
    for copy in copies:
        copy.start()
    for copy in copies:
        copy.wait()


def on_device(loss_scale, query_rows, key_rows, value_rows, norm_gain, out_weight, cotangent):
    length, width = query_rows.shape[1:]
    rows = out_weight.shape[0]
    vmem = pl.BlockSpec(memory_space=pltpu.VMEM)
    hbm = pl.BlockSpec(memory_space=pltpu.HBM)
    block = jax.ShapeDtypeStruct((length, width), BF16)
    dma = pltpu.SemaphoreType.DMA
    states = (16, HEAD, HEAD)
    scratch = [
        pltpu.VMEM((length, width), BF16),
        pltpu.VMEM((length, width), BF16),
        pltpu.VMEM((length, width), BF16),
        pltpu.VMEM((1, width), F32),
        pltpu.VMEM((rows, width), BF16),
        pltpu.VMEM((length, width), BF16),
        dma((6,)),
        pltpu.VMEM((length, width), BF16),
        pltpu.VMEM((length, width), BF16),
        pltpu.VMEM(states, BF16),
        pltpu.VMEM((length, width), F32),
        pltpu.VMEM((length, width), F32),
        pltpu.VMEM((length, width), BF16),
        pltpu.VMEM((length, width), BF16),
        pltpu.VMEM((length, width), F32),
        pltpu.VMEM((length, width), F32),
        pltpu.VMEM(states, F32),
        pltpu.VMEM((16, length, 1), F32),
        pltpu.VMEM((2, 8, HEAD, HEAD), BF16),
        pltpu.VMEM((2, 8, HEAD, HEAD), BF16),
        pltpu.VMEM((2, CHIPS, 64, HEAD), BF16),
        pltpu.VMEM((2, CHIPS, 64, HEAD), BF16),
        pltpu.VMEM((2, CHIPS, 64, HEAD), BF16),
        pltpu.VMEM((2, CHIPS, 64, HEAD), BF16),
        pltpu.VMEM((2, 8, HEAD, HEAD), BF16),
        pltpu.VMEM(states, BF16),
        pltpu.VMEM(states, BF16),
        pltpu.VMEM((32, 64, width), BF16),
        pltpu.VMEM((8, length, width), BF16),
        pltpu.VMEM((16, 8, 16, length), BF16),
        pltpu.VMEM((16, 16, 8 * length), BF16),
        pltpu.VMEM((16, 16, width), F32),
        pltpu.VMEM((16, 16, width), BF16),
        pltpu.VMEM((CHUNKS, 2, 8, 16, WIDE // 2), BF16),
        pltpu.VMEM((CHUNKS, 2, 8, 16, WIDE), BF16),
        pltpu.VMEM((CHUNKS, 2, 8, 16, WIDE), BF16),
        pltpu.VMEM((CHUNKS, 8, 16, WIDE), BF16),
        pltpu.VMEM((CHUNKS, 8, 16, WIDE), BF16),
        pltpu.VMEM((CHUNKS, 16, WIDE), BF16),
        pltpu.VMEM((CHUNKS, 8, 16, WIDE), BF16),
        dma((2,)), dma((2,)), dma((2, 16)), dma((2, 16)), dma((2, 16)), dma((2, 16)), dma((2,)), dma((2,)),
        dma((4,)), dma((4,)), dma((4,)), dma((4,)), dma((8, 2)), dma((8, 2)), dma((8, 2)), dma((8, 2)), dma((16,)), dma((16,)),
        dma((2,)), dma((2,)), dma((2,)), dma((2,)), dma((4,)), dma((4,)),
        dma((8,)), dma((8,)),
        dma((CHUNKS, 2)), dma((CHUNKS, 2)), dma((CHUNKS, 2)), dma((CHUNKS, 2)),
        dma((CHUNKS, 8)), dma((CHUNKS, 8)), dma((CHUNKS, 8)), dma((CHUNKS, 8)),
    ]

    def body(*refs):
        kernel(loss_scale, *refs)

    shapes = (block, block, block, block, jax.ShapeDtypeStruct((rows, width), F32))
    results = pl.pallas_call(
        body,
        out_shape=shapes,
        in_specs=[hbm] * 6,
        out_specs=(vmem,) * 5,
        scratch_shapes=scratch,
        compiler_params=pltpu.CompilerParams(
            collective_id=0, has_side_effects=True, vmem_limit_bytes=44 * 1024 * 1024
        ),
        name="layer",
    )(
        *(pltpu.with_memory_space_constraint(a, pltpu.HBM) for a in (query_rows[0], key_rows[0], value_rows[0])),
        pltpu.with_memory_space_constraint(norm_gain.reshape(1, width), pltpu.HBM),
        *(pltpu.with_memory_space_constraint(a, pltpu.HBM) for a in (out_weight, cotangent[0])),
    )
    anywhere = pl.BlockSpec(memory_space=pl.ANY)
    mixed, gq, gk, gv, gw = pl.pallas_call(
        finish,
        out_shape=shapes,
        in_specs=[anywhere] * 5,
        out_specs=(hbm,) * 5,
        scratch_shapes=[dma((5,))],
        compiler_params=pltpu.CompilerParams(vmem_limit_bytes=8 * 1024 * 1024),
        name="finish",
    )(*results)
    return mixed[None], gq[None], gk[None], gv[None], gw


def solution(mesh):
    positions = mesh.shape["dp"] * mesh.shape["ctx"] * HEAD
    loss_scale = 1.0 / math.sqrt(positions)

    def run(*args):
        return on_device(loss_scale, *args)

    split = P("dp", "ctx", None)
    return jax.shard_map(
        run,
        mesh=mesh,
        in_specs=(split, split, split, P(), P("ctx", None), split),
        out_specs=(split, split, split, split, P("ctx", None)),
        check_vma=False,
    )
```

```python
import math

import jax
import jax.numpy as jnp
from jax import lax
from jax.experimental import pallas as pl
from jax.experimental.pallas import tpu as pltpu
from jax.sharding import PartitionSpec as P

MESH = pl.DeviceIdType.MESH
F32 = jnp.float32
BF16 = jnp.bfloat16
HEAD = 128
EPSILON = 1e-06
NZ = 8
NX = 4
NY = 4
CHIPS = 16
HALF = 1024
CHUNKS = 2
CHUNK = 2048 // CHUNKS
WIDE = CHUNK // 2


def dot(a, b, ca, cb):
    return lax.dot_general(a, b, (((ca,), (cb,)), ((), ())), preferred_element_type=F32)


def rcopy(src, dst, send, recv, device):
    return pltpu.make_async_remote_copy(
        src_ref=src, dst_ref=dst, send_sem=send, recv_sem=recv, device_id=device, device_id_type=MESH
    )


def exp_low(wide):
    return jnp.exp(jnp.minimum(wide, 0.0))


def feature(values):
    wide = values.astype(F32)
    return jnp.where(wide > 0, wide + 1.0, exp_low(wide)).astype(BF16)


def slope(values):
    wide = values.astype(F32)
    return jnp.where(wide > 0, 1.0, exp_low(wide))


def kernel(
    loss_scale,
    q_hbm, k_hbm, v_hbm, gain_hbm, w_hbm, cot_hbm,
    mixed_ref, gq_ref, gk_ref, gv_ref, gw_ref,
    q_ref, k_ref, v_ref, gain_ref, w_ref, cot_ref, in_s,
    fq, fk, probs, att, dnorm, normed, datt, dfk, dgv, local, inverse,
    xsend, xrecv, pieces, got, back_out, back_in, psend, prefix, suffix,
    wfull, cotg, flipped, normg, gwf, gwt, xh_in, x_out, x_in, z_out, z_in, f_out, f_in,
    sx_s, sx_r, s1_s, s1_r, s2_s, s2_r, sp_s, sp_r,
    up_s, up_r, dn_s, dn_r, wx_s, wx_r, wy_s, wy_r, wp_s, wp_r,
    cu_s, cu_r, cd_s, cd_r, cp_s, cp_r,
    n_s, n_r, xa_s, xa_r, xb_s, xb_r, z_s, z_r, f_s, f_r,
):
    d = lax.axis_index("dp")
    i = lax.axis_index("ctx")
    c = i % 2
    j = i // 2
    z = j % NZ
    xl = j // NZ
    y = d // 2
    xh = d % 2
    x = xh * 2 + xl
    o = 1 - c
    partner = (d, j * 2 + o)

    def chip(jj):
        return (d, jj * 2 + c)

    def at_x(xx):
        return (y * 2 + xx // 2, ((xx % 2) * NZ + z) * 2 + c)

    def at_z(zz):
        return (d, (xl * NZ + zz) * 2 + c)

    def at_y(yy, cc):
        return (yy * 2 + xh, j * 2 + cc)

    def final_to(t):
        return (t, (xl * NZ + z) * 2 + y // 2)

    def final_from(t):
        return ((2 * c + t // 4) * 2 + t % 2, (xl * NZ + z) * 2 + (t // 2) % 2)

    def same(device):
        return jnp.logical_and(device[0] == d, device[1] == i)

    inputs = ((k_hbm, k_ref), (v_hbm, v_ref), (q_hbm, q_ref), (w_hbm, w_ref), (cot_hbm, cot_ref), (gain_hbm, gain_ref))
    loads = [pltpu.make_async_copy(a, b, in_s.at[n]) for n, (a, b) in enumerate(inputs)]
    for load in loads:
        load.start()

    barrier = pltpu.get_barrier_semaphore()

    def greet(device):
        pl.semaphore_signal(barrier, inc=1, device_id=device, device_id_type=MESH)

    def greet_maybe_self(device):
        @pl.when(jnp.logical_not(same(device)))
        def _():
            greet(device)

    for t in range(1, CHIPS):
        greet(chip((j + t) % CHIPS))
    greet(partner)
    for t in range(1, NX):
        greet(at_x((x + t) % NX))
    for t in range(1, NY):
        greet(at_y((y + t) % NY, 0))
        greet(at_y((y + t) % NY, 1))
    for t in range(8):
        greet_maybe_self(final_to(t))
        greet_maybe_self(final_from(t))

    def head(h):
        return pl.ds(pl.multiple_of(h * HEAD, HEAD), HEAD)

    def loop_a(h, _):
        cols = head(h)
        fq[:, cols] = feature(q_ref[:, cols])
        kf = feature(k_ref[:, cols])
        fk[:, cols] = kf
        local[h] = dot(kf, v_ref[:, cols], 0, 0)
        return 0

    for load in loads[:3]:
        load.wait()
    lax.fori_loop(0, 16, loop_a, 0, unroll=8)
    for load in loads[3:]:
        load.wait()

    selves = jnp.where(y // 2 == c, 2, 0)
    pl.semaphore_wait(barrier, 15 + 1 + 3 + 6 + 16 - selves)

    left = pl.ds(0, HALF)
    right = pl.ds(HALF, HALF)

    pending = []

    def begin(copy):
        copy.start()
        pending.append(copy)
        return copy

    def wslot(zz):
        return (xl * NZ + zz) * 2 + c

    def oslot(zz):
        return ((1 - xl) * NZ + zz) * 2 + c

    near_x = (y * 2 + xh, ((1 - xl) * NZ + z) * 2 + c)
    far_x = (y * 2 + (1 - xh), ((1 - xl) * NZ + z) * 2 + c)
    z_up = at_z((z + 1) % NZ)
    z_dn = at_z((z + NZ - 1) % NZ)

    p = y % 2
    mine_w = pl.ds(pl.multiple_of(p * HALF, HALF), HALF)
    rest_w = pl.ds(pl.multiple_of((1 - p) * HALF, HALF), HALF)

    def quarter(side, a):
        return pl.ds(pl.multiple_of(side * HALF + a * 512, 512), 512)

    y_up = at_y((y + 1) % NY, c)
    y_dn = at_y((y + NY - 1) % NY, c)

    def wcols(r, cols, own=False):
        if r == 0 and not own:
            return w_ref.at[:, cols]
        return wfull.at[wslot((z + r) % NZ), :, cols]

    def z_cols(k, a):
        return quarter(p, a) if k == 3 else mine_w

    def w_up(k):
        r = (-k) % NZ
        cols = z_cols(k, 0)
        begin(rcopy(wcols(r, cols), wcols(r, cols, True), up_s.at[k], up_r.at[k], z_up))

    def w_dn(k):
        cols = z_cols(k, 1)
        begin(rcopy(wcols(k, cols), wcols(k, cols, True), dn_s.at[k], dn_r.at[k], z_dn))

    def w_up_wait(k):
        ref = wcols((-k - 1) % NZ, z_cols(k, 0), True)
        rcopy(ref, ref, up_s.at[k], up_r.at[k], z_up).wait_recv()

    def w_dn_wait(k):
        ref = wcols(k + 1, z_cols(k, 1), True)
        rcopy(ref, ref, dn_s.at[k], dn_r.at[k], z_dn).wait_recv()

    def w_near(r):
        begin(rcopy(wcols(r, mine_w), wcols(r, mine_w, True), wx_s.at[r, 0], wx_r.at[r, 0], near_x))

    def w_far(r):
        begin(rcopy(wcols(r, rest_w), wcols(r, rest_w, True), wx_s.at[r, 1], wx_r.at[r, 1], far_x))

    def w_pair(r):
        dst = wfull.at[wslot((z + r) % NZ)]
        begin(rcopy(w_ref if r == 0 else dst, dst, wp_s.at[r], wp_r.at[r], partner))

    def w_side(r, a):
        ref = wcols(r, quarter(p, a))
        begin(rcopy(ref, ref, wy_s.at[r, a], wy_r.at[r, a], y_dn if a else y_up))

    def w_first():
        w_up(0)
        w_dn(0)
        w_near(0)
        w_far(0)
        w_pair(0)

    def w_step(k):
        w_up_wait(k - 1)
        w_up(k)
        w_dn_wait(k - 1)
        w_dn(k)
        for r in ((-k) % NZ, k):
            w_near(r)
            w_side(r, 0)
            w_side(r, 1)

    def w_last():
        w_up_wait(3)
        w_side(4, 0)
        w_dn_wait(3)
        w_side(4, 1)
        w_near(4)

    def w_rest(r):
        for a in (0, 1):
            ref = wcols(r, quarter(1 - p, a))
            rcopy(ref, ref, wy_s.at[r, a], wy_r.at[r, a], y_up).wait_recv()
        w_far(r)
        w_pair(r)

    def w_other(r):
        slot = oslot((z + r) % NZ)
        for a, cols in ((0, mine_w), (1, rest_w)):
            ref = wfull.at[slot, :, cols]
            rcopy(ref, ref, wx_s.at[r, a], wx_r.at[r, a], near_x).wait_recv()
        begin(rcopy(wfull.at[slot], wfull.at[slot], wp_s.at[8 + r], wp_r.at[8 + r], partner))

    def w_pair_wait(own):
        for r in range(8) if own else range(8, 16):
            zz = (z + r) % NZ
            side = xl if r < 8 else 1 - xl
            ref = wfull.at[(side * NZ + zz) * 2 + o]
            rcopy(ref, ref, wp_s.at[r], wp_r.at[r], partner).wait_recv()

    def cslot(r):
        return ((y + r) % NY) * 2 + c

    def c_first():
        own = cotg.at[cslot(0)]
        begin(rcopy(cot_ref, own, cu_s.at[0], cu_r.at[0], y_up))
        begin(rcopy(cot_ref, own, cd_s.at[0], cd_r.at[0], y_dn))
        begin(rcopy(cot_ref, own, cp_s.at[0], cp_r.at[0], partner))

    def c_pair(r):
        ref = cotg.at[cslot(r)]
        begin(rcopy(ref, ref, cp_s.at[r], cp_r.at[r], partner))

    def c_second():
        below = cotg.at[cslot(3)]
        rcopy(below, below, cu_s.at[0], cu_r.at[0], y_up).wait_recv()
        part = cotg.at[cslot(3), :, left]
        begin(rcopy(part, part, cu_s.at[1], cu_r.at[1], y_up))
        above = cotg.at[cslot(1)]
        rcopy(above, above, cd_s.at[0], cd_r.at[0], y_dn).wait_recv()
        part = cotg.at[cslot(1), :, right]
        begin(rcopy(part, part, cd_s.at[1], cd_r.at[1], y_dn))
        c_pair(3)
        c_pair(1)

    def c_third():
        a = cotg.at[cslot(2), :, left]
        rcopy(a, a, cu_s.at[1], cu_r.at[1], y_up).wait_recv()
        b = cotg.at[cslot(2), :, right]
        rcopy(b, b, cd_s.at[1], cd_r.at[1], y_dn).wait_recv()
        c_pair(2)

    def c_wait():
        for r in range(4):
            ref = cotg.at[((y + r) % NY) * 2 + o]
            rcopy(ref, ref, cp_s.at[r], cp_r.at[r], partner).wait_recv()

    own_heads = pl.ds(8 * c, 8)
    other_heads = pl.ds(8 * o, 8)

    def scan_pair(n):
        xsend[n] = local[other_heads].astype(BF16)
        begin(rcopy(xsend.at[n], xrecv.at[n], sx_s.at[n], sx_r.at[n], partner))

    def scan_spread(n):
        rcopy(xrecv.at[n], xrecv.at[n], sx_s.at[n], sx_r.at[n], partner).wait_recv()
        total = (local[own_heads] + xrecv[n].astype(F32)).astype(BF16)
        pieces[n] = total.reshape(CHIPS, 64, HEAD)
        for t in range(1, CHIPS):
            jj = (j + t) % CHIPS
            begin(rcopy(pieces.at[n, jj], got.at[n, j], s1_s.at[n, jj], s1_r.at[n, j], chip(jj)))
        got[n, j] = pieces[n, j]

    def scan_return(n):
        for t in range(1, CHIPS):
            jj = (j + t) % CHIPS
            ref = got.at[n, jj]
            rcopy(ref, ref, s1_s.at[n, jj], s1_r.at[n, jj], partner).wait_recv()
        total = jnp.zeros((64, HEAD), F32)
        order = range(CHIPS) if n == 0 else range(CHIPS - 1, -1, -1)
        for jj in order:
            back_out[n, jj] = total.astype(BF16)
            total = total + got[n, jj].astype(F32)
        for t in range(1, CHIPS):
            jj = (j + t) % CHIPS
            begin(rcopy(back_out.at[n, jj], back_in.at[n, j], s2_s.at[n, jj], s2_r.at[n, j], chip(jj)))
        back_in[n, j] = back_out[n, j]

    def scan_share(n, out):
        for t in range(1, CHIPS):
            jj = (j + t) % CHIPS
            ref = back_in.at[n, jj]
            rcopy(ref, ref, s2_s.at[n, jj], s2_r.at[n, jj], partner).wait_recv()
        mine = back_in[n].astype(F32).reshape(8, HEAD, HEAD)
        last = (c if n == 0 else o).astype(F32)
        psend[n] = (mine + (1.0 - last) * local[own_heads]).astype(BF16)
        begin(rcopy(psend.at[n], out.at[own_heads], sp_s.at[n], sp_r.at[n], partner))
        out[own_heads] = (mine + last * xrecv[n].astype(F32)).astype(BF16)

    def scan_wait(n, out):
        ref = out.at[other_heads]
        rcopy(ref, ref, sp_s.at[n], sp_r.at[n], partner).wait_recv()

    me8 = y * 2 + c

    def positions(b):
        return pl.ds(pl.multiple_of(b * HEAD, HEAD), HEAD)

    def n_send(core):
        some = pl.ds(8 * core, 8)
        for t in range(1, 8):
            b = (me8 + t) % 8
            begin(
                rcopy(
                    flipped.at[some, b],
                    normg.at[some, :, positions(me8)],
                    n_s.at[core, b],
                    n_r.at[core, me8],
                    at_y(b // 2, b % 2),
                )
            )
        normg[some, :, positions(me8)] = flipped[some, me8]

    def n_wait():
        for core in (0, 1):
            for t in range(1, 8):
                b = (me8 + t) % 8
                ref = normg.at[pl.ds(8 * core, 8), :, positions(b)]
                rcopy(ref, ref, n_s.at[core, b], n_r.at[core, b], partner).wait_recv()

    x_up = at_x((x + 1) % NX)
    x_dn = at_x((x + 3) % NX)
    two = (x + 2) % NX
    one_up = (x + 1) % NX
    one_dn = (x + 3) % NX

    def piece(k, h, lo, size):
        cols = pl.ds(pl.multiple_of(h * CHUNK + (k // 2) * WIDE + lo, HEAD), size)
        return pl.ds(8 * (k % 2), 8), slice(None), cols

    lows, highs = pl.ds(0, WIDE // 2), pl.ds(WIDE // 2, WIDE // 2)

    def low(k, h):
        return piece(k, h, 0, WIDE // 2)

    def high(k, h):
        return piece(k, h, WIDE // 2, WIDE // 2)

    def g_tile(h):
        def loop_g(n, _):
            cols = pl.ds(pl.multiple_of(h * CHUNK + n * 512, 512), 512)
            tile = dot(normg[...].reshape(256, 1024), cotg[:, :, cols].reshape(1024, 512), 1, 0)
            gwf[:, :, cols] = tile.reshape(16, 16, 512)
            gwt[:, :, cols] = tile.astype(BF16).reshape(16, 16, 512)
            return 0

        lax.fori_loop(0, CHUNK // 512, loop_g, 0)

    def g_first(h):
        begin(rcopy(gwt.at[low(two, h)], xh_in.at[h, 0], xa_s.at[h, 0], xa_r.at[h, 0], x_up))
        begin(rcopy(gwt.at[high(two, h)], xh_in.at[h, 1], xa_s.at[h, 1], xa_r.at[h, 1], x_dn))

    def g_second(h):
        for a, to in ((0, x_up), (1, x_dn)):
            rcopy(xh_in.at[h, a], xh_in.at[h, a], xa_s.at[h, a], xa_r.at[h, a], to).wait_recv()
        x_out[h, 0, :, :, lows] = (gwf[low(one_up, h)] + xh_in[h, 0].astype(F32)).astype(BF16)
        x_out[h, 0, :, :, highs] = gwt[high(one_up, h)]
        x_out[h, 1, :, :, lows] = gwt[low(one_dn, h)]
        x_out[h, 1, :, :, highs] = (gwf[high(one_dn, h)] + xh_in[h, 1].astype(F32)).astype(BF16)
        begin(rcopy(x_out.at[h, 0], x_in.at[h, 0], xb_s.at[h, 0], xb_r.at[h, 0], x_up))
        begin(rcopy(x_out.at[h, 1], x_in.at[h, 1], xb_s.at[h, 1], xb_r.at[h, 1], x_dn))

    def g_third(h):
        for a, to in ((0, x_up), (1, x_dn)):
            rcopy(x_in.at[h, a], x_in.at[h, a], xb_s.at[h, a], xb_r.at[h, a], to).wait_recv()
        total = gwf[piece(x, h, 0, WIDE)] + x_in[h, 0].astype(F32) + x_in[h, 1].astype(F32)
        z_out[h] = total.astype(BF16)
        for t in range(1, NZ):
            zz = (z + t) % NZ
            begin(rcopy(z_out.at[h, zz], z_in.at[h, z], z_s.at[h, zz], z_r.at[h, z], at_z(zz)))
        z_in[h, z] = z_out[h, z]

    me_f = (2 * (y % 2) + c) * 2 + xh

    def f_copy(h, t):
        return rcopy(f_out.at[h], f_in.at[h, me_f], f_s.at[h, t], f_r.at[h, me_f], final_to(t))

    def g_fourth(h):
        for t in range(1, NZ):
            zz = (z + t) % NZ
            ref = z_in.at[h, zz]
            rcopy(ref, ref, z_s.at[h, zz], z_r.at[h, zz], partner).wait_recv()
        whole = z_in[h, 0].astype(F32)
        for zz in range(1, NZ):
            whole = whole + z_in[h, zz].astype(F32)
        f_out[h] = whole.astype(BF16)
        for t in range(8):
            to = final_to(t)

            @pl.when(jnp.logical_not(same(to)))
            def _(t=t):
                f_copy(h, t).start()

            @pl.when(same(to))
            def _():
                f_in[h, me_f] = f_out[h]

    def g_end(h):
        for t in range(8):
            source = final_from(t)

            @pl.when(jnp.logical_not(same(source)))
            def _(source=source, t=t):
                ref = f_in.at[h, t]
                rcopy(ref, ref, f_s.at[h, t], f_r.at[h, t], source).wait_recv()

            row, col = 16 * (t // 2), h * CHUNK + WIDE * (t % 2)
            gw_ref[row : row + 16, col : col + WIDE] = f_in[h, t].astype(F32) * loss_scale
        for t in range(8):
            to = final_to(t)

            @pl.when(jnp.logical_not(same(to)))
            def _(t=t):
                f_copy(h, t).wait_send()

    rows_at = lax.broadcasted_iota(jnp.int32, (HEAD, HEAD), 0)
    cols_at = lax.broadcasted_iota(jnp.int32, (HEAD, HEAD), 1)
    causal = rows_at >= cols_at

    def loop_b(h, _):
        cols = head(h)
        scores = dot(fq[:, cols], fk[:, cols], 1, 1)
        p = jnp.where(causal, scores, 0.0).astype(BF16)
        probs[h] = p
        att[:, cols] = dot(p, v_ref[:, cols], 1, 0)
        return 0

    def loop_c(h2, _):
        cols = pl.ds(pl.multiple_of(h2 * 256, 256), 256)
        rows = wfull[pl.ds(h2 * 4, 4)].reshape(256, 2048)
        dnorm[:, cols] = dot(cot_ref[...], rows, 1, 1) * gain_ref[:, cols]
        return 0

    def loop_n(h, _):
        cols = head(h)
        a = att[:, cols] + dot(fq[:, cols], prefix[h], 1, 0)
        inv = lax.rsqrt(jnp.mean(a * a, axis=-1, keepdims=True) + EPSILON)
        att[:, cols] = a
        inverse[h] = inv
        out = a * inv * gain_ref[:, cols]
        normed[:, cols] = out.astype(BF16)
        flipped[h] = jnp.transpose(out).astype(BF16).reshape(8, 16, HEAD)
        return 0

    def loop_d(h, _):
        cols = head(h)
        a = att[:, cols]
        inv = inverse[h]
        s = dnorm[:, cols]
        m = jnp.mean(s * a, axis=-1, keepdims=True)
        g = (inv * (s - a * inv * inv * m)).astype(BF16)
        datt[:, cols] = g
        local[h] = dot(fq[:, cols], g, 0, 0)
        return 0

    def loop_e(h, _):
        cols = head(h)
        g = datt[:, cols]
        fkh = fk[:, cols]
        dp = jnp.where(causal, dot(g, v_ref[:, cols], 1, 1), 0.0).astype(BF16)
        dfq = dot(dp, fkh, 1, 0) + dot(g, prefix[h], 1, 1)
        gq_ref[:, cols] = (dfq * slope(q_ref[:, cols])).astype(BF16)
        dfk[:, cols] = dot(dp, fq[:, cols], 0, 0)
        dgv[:, cols] = dot(probs[h], g, 0, 0)
        return 0

    def loop_m(n, _):
        cols = pl.ds(pl.multiple_of(n * 512, 512), 512)
        rows = wfull[:, :, cols].reshape(2048, 512)
        mixed_ref[:, cols] = dot(normed[...], rows, 1, 0).astype(BF16)
        return 0

    def loop_f(h, _):
        cols = head(h)
        s = suffix[h]
        gk = dfk[:, cols] + dot(v_ref[:, cols], s, 1, 1)
        gk_ref[:, cols] = (gk * slope(k_ref[:, cols])).astype(BF16)
        gv_ref[:, cols] = (dgv[:, cols] + dot(fk[:, cols], s, 1, 0)).astype(BF16)
        return 0

    def half(body, core):
        lax.fori_loop(0, 8, lambda h, _: body(h + 8 * core, 0), 0, unroll=8)

    def weights(side):
        lax.fori_loop(0, 4, lambda h, _: loop_c(h + 4 * side, 0), 0, unroll=4)

    scan_pair(0)
    w_first()
    c_first()
    scan_spread(0)
    wfull[i] = w_ref[...]
    cotg[cslot(0)] = cot_ref[...]
    w_step(1)
    lax.fori_loop(0, 16, loop_b, 0, unroll=8)
    scan_return(0)
    w_step(2)
    c_second()
    w_rest(1)
    w_rest(7)
    w_rest(2)
    w_rest(6)
    scan_share(0, prefix)
    w_step(3)
    half(loop_n, c)
    n_send(c)
    scan_wait(0, prefix)
    half(loop_n, o)
    n_send(o)
    c_third()
    w_last()
    for r in (0, 1, 7):
        w_other(r)
    for r in (3, 5):
        w_rest(r)
    for r in (2, 6):
        w_other(r)
    w_rest(4)
    c_wait()
    n_wait()
    for h in range(CHUNKS):
        g_tile(h)
        g_first(h)
    for r in (3, 5, 4):
        w_other(r)
    w_pair_wait(True)
    weights(xl)
    half(loop_d, xl)
    w_pair_wait(False)
    weights(1 - xl)
    half(loop_d, 1 - xl)
    scan_pair(1)
    g_second(0)
    scan_spread(1)
    for h in range(1, CHUNKS):
        g_second(h)
    lax.fori_loop(0, 8, loop_e, 0, unroll=8)
    g_third(0)
    lax.fori_loop(8, 16, loop_e, 0, unroll=8)
    for h in range(1, CHUNKS):
        g_third(h)
    scan_return(1)
    g_fourth(0)
    lax.fori_loop(0, 4, loop_m, 0)
    for h in range(1, CHUNKS):
        g_fourth(h)
    scan_share(1, suffix)
    half(loop_f, c)
    scan_wait(1, suffix)
    half(loop_f, o)
    for copy in pending:
        copy.wait_send()
    for h in range(CHUNKS):
        g_end(h)


def finish(*refs):
    copies = [pltpu.make_async_copy(refs[n], refs[5 + n], refs[10].at[n]) for n in range(5)]
    for copy in copies:
        copy.start()
    for copy in copies:
        copy.wait()


def on_device(loss_scale, query_rows, key_rows, value_rows, norm_gain, out_weight, cotangent):
    length, width = query_rows.shape[1:]
    rows = out_weight.shape[0]
    vmem = pl.BlockSpec(memory_space=pltpu.VMEM)
    hbm = pl.BlockSpec(memory_space=pltpu.HBM)
    block = jax.ShapeDtypeStruct((length, width), BF16)
    dma = pltpu.SemaphoreType.DMA
    states = (16, HEAD, HEAD)
    scratch = [
        pltpu.VMEM((length, width), BF16),
        pltpu.VMEM((length, width), BF16),
        pltpu.VMEM((length, width), BF16),
        pltpu.VMEM((1, width), F32),
        pltpu.VMEM((rows, width), BF16),
        pltpu.VMEM((length, width), BF16),
        dma((6,)),
        pltpu.VMEM((length, width), BF16),
        pltpu.VMEM((length, width), BF16),
        pltpu.VMEM(states, BF16),
        pltpu.VMEM((length, width), F32),
        pltpu.VMEM((length, width), F32),
        pltpu.VMEM((length, width), BF16),
        pltpu.VMEM((length, width), BF16),
        pltpu.VMEM((length, width), F32),
        pltpu.VMEM((length, width), F32),
        pltpu.VMEM(states, F32),
        pltpu.VMEM((16, length, 1), F32),
        pltpu.VMEM((2, 8, HEAD, HEAD), BF16),
        pltpu.VMEM((2, 8, HEAD, HEAD), BF16),
        pltpu.VMEM((2, CHIPS, 64, HEAD), BF16),
        pltpu.VMEM((2, CHIPS, 64, HEAD), BF16),
        pltpu.VMEM((2, CHIPS, 64, HEAD), BF16),
        pltpu.VMEM((2, CHIPS, 64, HEAD), BF16),
        pltpu.VMEM((2, 8, HEAD, HEAD), BF16),
        pltpu.VMEM(states, BF16),
        pltpu.VMEM(states, BF16),
        pltpu.VMEM((32, 64, width), BF16),
        pltpu.VMEM((8, length, width), BF16),
        pltpu.VMEM((16, 8, 16, length), BF16),
        pltpu.VMEM((16, 16, 8 * length), BF16),
        pltpu.VMEM((16, 16, width), F32),
        pltpu.VMEM((16, 16, width), BF16),
        pltpu.VMEM((CHUNKS, 2, 8, 16, WIDE // 2), BF16),
        pltpu.VMEM((CHUNKS, 2, 8, 16, WIDE), BF16),
        pltpu.VMEM((CHUNKS, 2, 8, 16, WIDE), BF16),
        pltpu.VMEM((CHUNKS, 8, 16, WIDE), BF16),
        pltpu.VMEM((CHUNKS, 8, 16, WIDE), BF16),
        pltpu.VMEM((CHUNKS, 16, WIDE), BF16),
        pltpu.VMEM((CHUNKS, 8, 16, WIDE), BF16),
        dma((2,)), dma((2,)), dma((2, 16)), dma((2, 16)), dma((2, 16)), dma((2, 16)), dma((2,)), dma((2,)),
        dma((4,)), dma((4,)), dma((4,)), dma((4,)), dma((8, 2)), dma((8, 2)), dma((8, 2)), dma((8, 2)), dma((16,)), dma((16,)),
        dma((2,)), dma((2,)), dma((2,)), dma((2,)), dma((4,)), dma((4,)),
        dma((2, 8)), dma((2, 8)),
        dma((CHUNKS, 2)), dma((CHUNKS, 2)), dma((CHUNKS, 2)), dma((CHUNKS, 2)),
        dma((CHUNKS, 8)), dma((CHUNKS, 8)), dma((CHUNKS, 8)), dma((CHUNKS, 8)),
    ]

    def body(*refs):
        kernel(loss_scale, *refs)

    shapes = (block, block, block, block, jax.ShapeDtypeStruct((rows, width), F32))
    results = pl.pallas_call(
        body,
        out_shape=shapes,
        in_specs=[hbm] * 6,
        out_specs=(vmem,) * 5,
        scratch_shapes=scratch,
        compiler_params=pltpu.CompilerParams(
            collective_id=0, has_side_effects=True, vmem_limit_bytes=44 * 1024 * 1024
        ),
        name="layer",
    )(
        *(pltpu.with_memory_space_constraint(a, pltpu.HBM) for a in (query_rows[0], key_rows[0], value_rows[0])),
        pltpu.with_memory_space_constraint(norm_gain.reshape(1, width), pltpu.HBM),
        *(pltpu.with_memory_space_constraint(a, pltpu.HBM) for a in (out_weight, cotangent[0])),
    )
    anywhere = pl.BlockSpec(memory_space=pl.ANY)
    mixed, gq, gk, gv, gw = pl.pallas_call(
        finish,
        out_shape=shapes,
        in_specs=[anywhere] * 5,
        out_specs=(hbm,) * 5,
        scratch_shapes=[dma((5,))],
        compiler_params=pltpu.CompilerParams(vmem_limit_bytes=8 * 1024 * 1024),
        name="finish",
    )(*results)
    return mixed[None], gq[None], gk[None], gv[None], gw


def solution(mesh):
    positions = mesh.shape["dp"] * mesh.shape["ctx"] * HEAD
    loss_scale = 1.0 / math.sqrt(positions)

    def run(*args):
        return on_device(loss_scale, *args)

    split = P("dp", "ctx", None)
    return jax.shard_map(
        run,
        mesh=mesh,
        in_specs=(split, split, split, P(), P("ctx", None), split),
        out_specs=(split, split, split, split, P("ctx", None)),
        check_vma=False,
    )
```

```python
import math

import jax
import jax.numpy as jnp
from jax import lax
from jax.experimental import pallas as pl
from jax.experimental.pallas import tpu as pltpu
from jax.sharding import PartitionSpec as P

MESH = pl.DeviceIdType.MESH
F32 = jnp.float32
BF16 = jnp.bfloat16
HEAD = 128
EPSILON = 1e-06
NZ = 8
NX = 4
NY = 4
CHIPS = 16
HALF = 1024
CHIPS_FAR_FIRST = sorted(range(1, CHIPS), key=lambda t: abs(t % NZ - NZ // 2))
Z_FAR_FIRST = sorted(range(1, NZ), key=lambda t: abs(t - NZ // 2))
CHUNKS = 2
CHUNK = 2048 // CHUNKS
WIDE = CHUNK // 2


def dot(a, b, ca, cb):
    return lax.dot_general(a, b, (((ca,), (cb,)), ((), ())), preferred_element_type=F32)


def rcopy(src, dst, send, recv, device):
    return pltpu.make_async_remote_copy(
        src_ref=src, dst_ref=dst, send_sem=send, recv_sem=recv, device_id=device, device_id_type=MESH
    )


def exp_low(wide):
    return jnp.exp(jnp.minimum(wide, 0.0))


def feature(values):
    wide = values.astype(F32)
    return jnp.where(wide > 0, wide + 1.0, exp_low(wide)).astype(BF16)


def slope(values):
    wide = values.astype(F32)
    return jnp.where(wide > 0, 1.0, exp_low(wide))


def kernel(
    loss_scale,
    q_hbm, k_hbm, v_hbm, gain_hbm, w_hbm, cot_hbm,
    mixed_ref, gq_ref, gk_ref, gv_ref, gw_ref,
    q_ref, k_ref, v_ref, gain_ref, w_ref, cot_ref, in_s,
    fq, fk, probs, att, dnorm, normed, datt, dfk, dgv, local, inverse,
    xsend, xrecv, pieces, got, back_out, back_in, psend, prefix, suffix,
    wfull, cotg, flipped, normg, gwf, gwt, xh_in, x_out, x_in, z_out, z_in, f_out, f_in,
    sx_s, sx_r, s1_s, s1_r, s2_s, s2_r, sp_s, sp_r,
    up_s, up_r, dn_s, dn_r, wx_s, wx_r, wy_s, wy_r, wp_s, wp_r,
    cu_s, cu_r, cd_s, cd_r, cp_s, cp_r,
    n_s, n_r, xa_s, xa_r, xb_s, xb_r, z_s, z_r, f_s, f_r,
):
    d = lax.axis_index("dp")
    i = lax.axis_index("ctx")
    c = i % 2
    j = i // 2
    z = j % NZ
    xl = j // NZ
    y = d // 2
    xh = d % 2
    x = xh * 2 + xl
    o = 1 - c
    partner = (d, j * 2 + o)

    def chip(jj):
        return (d, jj * 2 + c)

    def at_x(xx):
        return (y * 2 + xx // 2, ((xx % 2) * NZ + z) * 2 + c)

    def at_z(zz):
        return (d, (xl * NZ + zz) * 2 + c)

    def at_y(yy, cc):
        return (yy * 2 + xh, j * 2 + cc)

    def final_to(t):
        return (t, (xl * NZ + z) * 2 + y // 2)

    def final_from(t):
        return ((2 * c + t // 4) * 2 + t % 2, (xl * NZ + z) * 2 + (t // 2) % 2)

    def same(device):
        return jnp.logical_and(device[0] == d, device[1] == i)

    inputs = ((k_hbm, k_ref), (v_hbm, v_ref), (q_hbm, q_ref), (w_hbm, w_ref), (cot_hbm, cot_ref), (gain_hbm, gain_ref))
    loads = [pltpu.make_async_copy(a, b, in_s.at[n]) for n, (a, b) in enumerate(inputs)]
    for load in loads:
        load.start()

    barrier = pltpu.get_barrier_semaphore()

    def greet(device):
        pl.semaphore_signal(barrier, inc=1, device_id=device, device_id_type=MESH)

    def greet_maybe_self(device):
        @pl.when(jnp.logical_not(same(device)))
        def _():
            greet(device)

    for t in range(1, CHIPS):
        greet(chip((j + t) % CHIPS))
    greet(partner)
    for t in range(1, NX):
        greet(at_x((x + t) % NX))
    for t in range(1, NY):
        greet(at_y((y + t) % NY, 0))
        greet(at_y((y + t) % NY, 1))
    for t in range(8):
        greet_maybe_self(final_to(t))
        greet_maybe_self(final_from(t))

    def head(h):
        return pl.ds(pl.multiple_of(h * HEAD, HEAD), HEAD)

    def loop_a(h, _):
        cols = head(h)
        fq[:, cols] = feature(q_ref[:, cols])
        kf = feature(k_ref[:, cols])
        fk[:, cols] = kf
        local[h] = dot(kf, v_ref[:, cols], 0, 0)
        return 0

    for load in loads[:3]:
        load.wait()
    lax.fori_loop(0, 16, loop_a, 0, unroll=8)
    for load in loads[3:]:
        load.wait()

    selves = jnp.where(y // 2 == c, 2, 0)
    pl.semaphore_wait(barrier, 15 + 1 + 3 + 6 + 16 - selves)

    left = pl.ds(0, HALF)
    right = pl.ds(HALF, HALF)

    pending = []

    def begin(copy):
        copy.start()
        pending.append(copy)
        return copy

    def wslot(zz):
        return (xl * NZ + zz) * 2 + c

    def oslot(zz):
        return ((1 - xl) * NZ + zz) * 2 + c

    near_x = (y * 2 + xh, ((1 - xl) * NZ + z) * 2 + c)
    far_x = (y * 2 + (1 - xh), ((1 - xl) * NZ + z) * 2 + c)
    z_up = at_z((z + 1) % NZ)
    z_dn = at_z((z + NZ - 1) % NZ)

    p = y % 2
    mine_w = pl.ds(pl.multiple_of(p * HALF, HALF), HALF)
    rest_w = pl.ds(pl.multiple_of((1 - p) * HALF, HALF), HALF)

    def quarter(side, a):
        return pl.ds(pl.multiple_of(side * HALF + a * 512, 512), 512)

    y_up = at_y((y + 1) % NY, c)
    y_dn = at_y((y + NY - 1) % NY, c)

    def wcols(r, cols, own=False):
        if r == 0 and not own:
            return w_ref.at[:, cols]
        return wfull.at[wslot((z + r) % NZ), :, cols]

    def z_cols(k, a):
        return quarter(p, a) if k == 3 else mine_w

    def w_up(k):
        r = (-k) % NZ
        cols = z_cols(k, 0)
        begin(rcopy(wcols(r, cols), wcols(r, cols, True), up_s.at[k], up_r.at[k], z_up))

    def w_dn(k):
        cols = z_cols(k, 1)
        begin(rcopy(wcols(k, cols), wcols(k, cols, True), dn_s.at[k], dn_r.at[k], z_dn))

    def w_up_wait(k):
        ref = wcols((-k - 1) % NZ, z_cols(k, 0), True)
        rcopy(ref, ref, up_s.at[k], up_r.at[k], z_up).wait_recv()

    def w_dn_wait(k):
        ref = wcols(k + 1, z_cols(k, 1), True)
        rcopy(ref, ref, dn_s.at[k], dn_r.at[k], z_dn).wait_recv()

    def w_near(r):
        begin(rcopy(wcols(r, mine_w), wcols(r, mine_w, True), wx_s.at[r, 0], wx_r.at[r, 0], near_x))

    def w_far(r):
        begin(rcopy(wcols(r, rest_w), wcols(r, rest_w, True), wx_s.at[r, 1], wx_r.at[r, 1], far_x))

    def w_pair(r):
        dst = wfull.at[wslot((z + r) % NZ)]
        begin(rcopy(w_ref if r == 0 else dst, dst, wp_s.at[r], wp_r.at[r], partner))

    def w_side(r, a):
        ref = wcols(r, quarter(p, a))
        begin(rcopy(ref, ref, wy_s.at[r, a], wy_r.at[r, a], y_dn if a else y_up))

    def w_first():
        w_up(0)
        w_dn(0)
        w_near(0)
        w_far(0)
        w_pair(0)

    def w_step(k):
        w_up_wait(k - 1)
        w_up(k)
        w_dn_wait(k - 1)
        w_dn(k)
        for r in ((-k) % NZ, k):
            w_near(r)
            w_side(r, 0)
            w_side(r, 1)

    def w_last():
        w_up_wait(3)
        w_side(4, 0)
        w_dn_wait(3)
        w_side(4, 1)
        w_near(4)

    def w_rest(r):
        for a in (0, 1):
            ref = wcols(r, quarter(1 - p, a))
            rcopy(ref, ref, wy_s.at[r, a], wy_r.at[r, a], y_up).wait_recv()
        w_far(r)
        w_pair(r)

    def w_other(r):
        slot = oslot((z + r) % NZ)
        for a, cols in ((0, mine_w), (1, rest_w)):
            ref = wfull.at[slot, :, cols]
            rcopy(ref, ref, wx_s.at[r, a], wx_r.at[r, a], near_x).wait_recv()
        begin(rcopy(wfull.at[slot], wfull.at[slot], wp_s.at[8 + r], wp_r.at[8 + r], partner))

    def w_pair_wait(own):
        for r in range(8) if own else range(8, 16):
            zz = (z + r) % NZ
            side = xl if r < 8 else 1 - xl
            ref = wfull.at[(side * NZ + zz) * 2 + o]
            rcopy(ref, ref, wp_s.at[r], wp_r.at[r], partner).wait_recv()

    def cslot(r):
        return ((y + r) % NY) * 2 + c

    def c_first():
        own = cotg.at[cslot(0)]
        begin(rcopy(cot_ref, own, cu_s.at[0], cu_r.at[0], y_up))
        begin(rcopy(cot_ref, own, cd_s.at[0], cd_r.at[0], y_dn))
        begin(rcopy(cot_ref, own, cp_s.at[0], cp_r.at[0], partner))

    def c_pair(r):
        ref = cotg.at[cslot(r)]
        begin(rcopy(ref, ref, cp_s.at[r], cp_r.at[r], partner))

    def c_second():
        below = cotg.at[cslot(3)]
        rcopy(below, below, cu_s.at[0], cu_r.at[0], y_up).wait_recv()
        part = cotg.at[cslot(3), :, left]
        begin(rcopy(part, part, cu_s.at[1], cu_r.at[1], y_up))
        above = cotg.at[cslot(1)]
        rcopy(above, above, cd_s.at[0], cd_r.at[0], y_dn).wait_recv()
        part = cotg.at[cslot(1), :, right]
        begin(rcopy(part, part, cd_s.at[1], cd_r.at[1], y_dn))
        c_pair(3)
        c_pair(1)

    def c_third():
        a = cotg.at[cslot(2), :, left]
        rcopy(a, a, cu_s.at[1], cu_r.at[1], y_up).wait_recv()
        b = cotg.at[cslot(2), :, right]
        rcopy(b, b, cd_s.at[1], cd_r.at[1], y_dn).wait_recv()
        c_pair(2)

    def c_wait():
        for r in range(4):
            ref = cotg.at[((y + r) % NY) * 2 + o]
            rcopy(ref, ref, cp_s.at[r], cp_r.at[r], partner).wait_recv()

    own_heads = pl.ds(8 * c, 8)
    other_heads = pl.ds(8 * o, 8)

    def scan_pair(n):
        xsend[n] = local[other_heads].astype(BF16)
        begin(rcopy(xsend.at[n], xrecv.at[n], sx_s.at[n], sx_r.at[n], partner))

    def scan_spread(n):
        rcopy(xrecv.at[n], xrecv.at[n], sx_s.at[n], sx_r.at[n], partner).wait_recv()
        total = (local[own_heads] + xrecv[n].astype(F32)).astype(BF16)
        pieces[n] = total.reshape(CHIPS, 64, HEAD)
        for t in CHIPS_FAR_FIRST:
            jj = (j + t) % CHIPS
            begin(rcopy(pieces.at[n, jj], got.at[n, j], s1_s.at[n, jj], s1_r.at[n, j], chip(jj)))
        got[n, j] = pieces[n, j]

    def scan_return(n):
        for t in range(1, CHIPS):
            jj = (j + t) % CHIPS
            ref = got.at[n, jj]
            rcopy(ref, ref, s1_s.at[n, jj], s1_r.at[n, jj], partner).wait_recv()
        total = jnp.zeros((64, HEAD), F32)
        order = range(CHIPS) if n == 0 else range(CHIPS - 1, -1, -1)
        for jj in order:
            back_out[n, jj] = total.astype(BF16)
            total = total + got[n, jj].astype(F32)
        for t in CHIPS_FAR_FIRST:
            jj = (j + t) % CHIPS
            begin(rcopy(back_out.at[n, jj], back_in.at[n, j], s2_s.at[n, jj], s2_r.at[n, j], chip(jj)))
        back_in[n, j] = back_out[n, j]

    def scan_share(n, out):
        for t in range(1, CHIPS):
            jj = (j + t) % CHIPS
            ref = back_in.at[n, jj]
            rcopy(ref, ref, s2_s.at[n, jj], s2_r.at[n, jj], partner).wait_recv()
        mine = back_in[n].astype(F32).reshape(8, HEAD, HEAD)
        last = (c if n == 0 else o).astype(F32)
        psend[n] = (mine + (1.0 - last) * local[own_heads]).astype(BF16)
        begin(rcopy(psend.at[n], out.at[own_heads], sp_s.at[n], sp_r.at[n], partner))
        out[own_heads] = (mine + last * xrecv[n].astype(F32)).astype(BF16)

    def scan_wait(n, out):
        ref = out.at[other_heads]
        rcopy(ref, ref, sp_s.at[n], sp_r.at[n], partner).wait_recv()

    me8 = y * 2 + c

    def positions(b):
        return pl.ds(pl.multiple_of(b * HEAD, HEAD), HEAD)

    def n_send():
        for t in range(1, 8):
            b = (me8 + t) % 8
            begin(
                rcopy(
                    flipped.at[:, b],
                    normg.at[:, :, positions(me8)],
                    n_s.at[b],
                    n_r.at[me8],
                    at_y(b // 2, b % 2),
                )
            )
        normg[:, :, positions(me8)] = flipped[:, me8]

    def n_wait():
        for t in range(1, 8):
            b = (me8 + t) % 8
            ref = normg.at[:, :, positions(b)]
            rcopy(ref, ref, n_s.at[b], n_r.at[b], partner).wait_recv()

    x_up = at_x((x + 1) % NX)
    x_dn = at_x((x + 3) % NX)
    two = (x + 2) % NX
    one_up = (x + 1) % NX
    one_dn = (x + 3) % NX

    def piece(k, h, lo, size):
        cols = pl.ds(pl.multiple_of(h * CHUNK + (k // 2) * WIDE + lo, HEAD), size)
        return pl.ds(8 * (k % 2), 8), slice(None), cols

    lows, highs = pl.ds(0, WIDE // 2), pl.ds(WIDE // 2, WIDE // 2)

    def low(k, h):
        return piece(k, h, 0, WIDE // 2)

    def high(k, h):
        return piece(k, h, WIDE // 2, WIDE // 2)

    def g_tile(h):
        def loop_g(n, _):
            cols = pl.ds(pl.multiple_of(h * CHUNK + n * 512, 512), 512)
            tile = dot(normg[...].reshape(256, 1024), cotg[:, :, cols].reshape(1024, 512), 1, 0)
            gwf[:, :, cols] = tile.reshape(16, 16, 512)
            gwt[:, :, cols] = tile.astype(BF16).reshape(16, 16, 512)
            return 0

        lax.fori_loop(0, CHUNK // 512, loop_g, 0)

    def g_first(h):
        begin(rcopy(gwt.at[low(two, h)], xh_in.at[h, 0], xa_s.at[h, 0], xa_r.at[h, 0], x_up))
        begin(rcopy(gwt.at[high(two, h)], xh_in.at[h, 1], xa_s.at[h, 1], xa_r.at[h, 1], x_dn))

    def g_second(h):
        for a, to in ((0, x_up), (1, x_dn)):
            rcopy(xh_in.at[h, a], xh_in.at[h, a], xa_s.at[h, a], xa_r.at[h, a], to).wait_recv()
        x_out[h, 0, :, :, lows] = (gwf[low(one_up, h)] + xh_in[h, 0].astype(F32)).astype(BF16)
        x_out[h, 0, :, :, highs] = gwt[high(one_up, h)]
        x_out[h, 1, :, :, lows] = gwt[low(one_dn, h)]
        x_out[h, 1, :, :, highs] = (gwf[high(one_dn, h)] + xh_in[h, 1].astype(F32)).astype(BF16)
        begin(rcopy(x_out.at[h, 0], x_in.at[h, 0], xb_s.at[h, 0], xb_r.at[h, 0], x_up))
        begin(rcopy(x_out.at[h, 1], x_in.at[h, 1], xb_s.at[h, 1], xb_r.at[h, 1], x_dn))

    def g_third(h):
        for a, to in ((0, x_up), (1, x_dn)):
            rcopy(x_in.at[h, a], x_in.at[h, a], xb_s.at[h, a], xb_r.at[h, a], to).wait_recv()
        total = gwf[piece(x, h, 0, WIDE)] + x_in[h, 0].astype(F32) + x_in[h, 1].astype(F32)
        z_out[h] = total.astype(BF16)
        for t in Z_FAR_FIRST:
            zz = (z + t) % NZ
            begin(rcopy(z_out.at[h, zz], z_in.at[h, z], z_s.at[h, zz], z_r.at[h, z], at_z(zz)))
        z_in[h, z] = z_out[h, z]

    me_f = (2 * (y % 2) + c) * 2 + xh

    def f_copy(h, t):
        return rcopy(f_out.at[h], f_in.at[h, me_f], f_s.at[h, t], f_r.at[h, me_f], final_to(t))

    def g_fourth(h):
        for t in range(1, NZ):
            zz = (z + t) % NZ
            ref = z_in.at[h, zz]
            rcopy(ref, ref, z_s.at[h, zz], z_r.at[h, zz], partner).wait_recv()
        whole = z_in[h, 0].astype(F32)
        for zz in range(1, NZ):
            whole = whole + z_in[h, zz].astype(F32)
        f_out[h] = whole.astype(BF16)
        for t in range(8):
            to = final_to(t)

            @pl.when(jnp.logical_not(same(to)))
            def _(t=t):
                f_copy(h, t).start()

            @pl.when(same(to))
            def _():
                f_in[h, me_f] = f_out[h]

    def g_end(h):
        for t in range(8):
            source = final_from(t)

            @pl.when(jnp.logical_not(same(source)))
            def _(source=source, t=t):
                ref = f_in.at[h, t]
                rcopy(ref, ref, f_s.at[h, t], f_r.at[h, t], source).wait_recv()

            row, col = 16 * (t // 2), h * CHUNK + WIDE * (t % 2)
            gw_ref[row : row + 16, col : col + WIDE] = f_in[h, t].astype(F32) * loss_scale
        for t in range(8):
            to = final_to(t)

            @pl.when(jnp.logical_not(same(to)))
            def _(t=t):
                f_copy(h, t).wait_send()

    rows_at = lax.broadcasted_iota(jnp.int32, (HEAD, HEAD), 0)
    cols_at = lax.broadcasted_iota(jnp.int32, (HEAD, HEAD), 1)
    causal = rows_at >= cols_at

    def loop_b(h, _):
        cols = head(h)
        scores = dot(fq[:, cols], fk[:, cols], 1, 1)
        p = jnp.where(causal, scores, 0.0).astype(BF16)
        probs[h] = p
        att[:, cols] = dot(p, v_ref[:, cols], 1, 0)
        return 0

    def loop_c(h2, _):
        cols = pl.ds(pl.multiple_of(h2 * 256, 256), 256)
        rows = wfull[pl.ds(h2 * 4, 4)].reshape(256, 2048)
        dnorm[:, cols] = dot(cot_ref[...], rows, 1, 1) * gain_ref[:, cols]
        return 0

    def loop_n(h, _):
        cols = head(h)
        a = att[:, cols] + dot(fq[:, cols], prefix[h], 1, 0)
        inv = lax.rsqrt(jnp.mean(a * a, axis=-1, keepdims=True) + EPSILON)
        att[:, cols] = a
        inverse[h] = inv
        out = a * inv * gain_ref[:, cols]
        normed[:, cols] = out.astype(BF16)
        flipped[h] = jnp.transpose(out).astype(BF16).reshape(8, 16, HEAD)
        return 0

    def loop_d(h, _):
        cols = head(h)
        a = att[:, cols]
        inv = inverse[h]
        s = dnorm[:, cols]
        m = jnp.mean(s * a, axis=-1, keepdims=True)
        g = (inv * (s - a * inv * inv * m)).astype(BF16)
        datt[:, cols] = g
        local[h] = dot(fq[:, cols], g, 0, 0)
        return 0

    def loop_e(h, _):
        cols = head(h)
        g = datt[:, cols]
        fkh = fk[:, cols]
        dp = jnp.where(causal, dot(g, v_ref[:, cols], 1, 1), 0.0).astype(BF16)
        dfq = dot(dp, fkh, 1, 0) + dot(g, prefix[h], 1, 1)
        gq_ref[:, cols] = (dfq * slope(q_ref[:, cols])).astype(BF16)
        dfk[:, cols] = dot(dp, fq[:, cols], 0, 0)
        dgv[:, cols] = dot(probs[h], g, 0, 0)
        return 0

    def loop_m(n, _):
        cols = pl.ds(pl.multiple_of(n * 512, 512), 512)
        rows = wfull[:, :, cols].reshape(2048, 512)
        mixed_ref[:, cols] = dot(normed[...], rows, 1, 0).astype(BF16)
        return 0

    def loop_f(h, _):
        cols = head(h)
        s = suffix[h]
        gk = dfk[:, cols] + dot(v_ref[:, cols], s, 1, 1)
        gk_ref[:, cols] = (gk * slope(k_ref[:, cols])).astype(BF16)
        gv_ref[:, cols] = (dgv[:, cols] + dot(fk[:, cols], s, 1, 0)).astype(BF16)
        return 0

    def half(body, core):
        lax.fori_loop(0, 8, lambda h, _: body(h + 8 * core, 0), 0, unroll=8)

    def weights(side):
        lax.fori_loop(0, 4, lambda h, _: loop_c(h + 4 * side, 0), 0, unroll=4)

    scan_pair(0)
    w_first()
    c_first()
    scan_spread(0)
    wfull[i] = w_ref[...]
    cotg[cslot(0)] = cot_ref[...]
    w_step(1)
    lax.fori_loop(0, 16, loop_b, 0, unroll=8)
    scan_return(0)
    w_step(2)
    c_second()
    w_rest(1)
    w_rest(7)
    w_rest(2)
    w_rest(6)
    scan_share(0, prefix)
    w_step(3)
    half(loop_n, c)
    scan_wait(0, prefix)
    half(loop_n, o)
    n_send()
    c_third()
    w_last()
    for r in (0, 1, 7):
        w_other(r)
    for r in (3, 5):
        w_rest(r)
    for r in (2, 6):
        w_other(r)
    w_rest(4)
    c_wait()
    n_wait()
    for h in range(CHUNKS):
        g_tile(h)
        g_first(h)
    for r in (3, 5, 4):
        w_other(r)
    w_pair_wait(True)
    weights(xl)
    half(loop_d, xl)
    w_pair_wait(False)
    weights(1 - xl)
    half(loop_d, 1 - xl)
    scan_pair(1)
    g_second(0)
    scan_spread(1)
    for h in range(1, CHUNKS):
        g_second(h)
    lax.fori_loop(0, 8, loop_e, 0, unroll=8)
    g_third(0)
    lax.fori_loop(8, 16, loop_e, 0, unroll=8)
    for h in range(1, CHUNKS):
        g_third(h)
    scan_return(1)
    g_fourth(0)
    lax.fori_loop(0, 4, loop_m, 0)
    for h in range(1, CHUNKS):
        g_fourth(h)
    scan_share(1, suffix)
    half(loop_f, c)
    scan_wait(1, suffix)
    half(loop_f, o)
    for copy in pending:
        copy.wait_send()
    for h in range(CHUNKS):
        g_end(h)


def finish(*refs):
    copies = [pltpu.make_async_copy(refs[n], refs[5 + n], refs[10].at[n]) for n in range(5)]
    for copy in copies:
        copy.start()
    for copy in copies:
        copy.wait()


def on_device(loss_scale, query_rows, key_rows, value_rows, norm_gain, out_weight, cotangent):
    length, width = query_rows.shape[1:]
    rows = out_weight.shape[0]
    vmem = pl.BlockSpec(memory_space=pltpu.VMEM)
    hbm = pl.BlockSpec(memory_space=pltpu.HBM)
    block = jax.ShapeDtypeStruct((length, width), BF16)
    dma = pltpu.SemaphoreType.DMA
    states = (16, HEAD, HEAD)
    scratch = [
        pltpu.VMEM((length, width), BF16),
        pltpu.VMEM((length, width), BF16),
        pltpu.VMEM((length, width), BF16),
        pltpu.VMEM((1, width), F32),
        pltpu.VMEM((rows, width), BF16),
        pltpu.VMEM((length, width), BF16),
        dma((6,)),
        pltpu.VMEM((length, width), BF16),
        pltpu.VMEM((length, width), BF16),
        pltpu.VMEM(states, BF16),
        pltpu.VMEM((length, width), F32),
        pltpu.VMEM((length, width), F32),
        pltpu.VMEM((length, width), BF16),
        pltpu.VMEM((length, width), BF16),
        pltpu.VMEM((length, width), F32),
        pltpu.VMEM((length, width), F32),
        pltpu.VMEM(states, F32),
        pltpu.VMEM((16, length, 1), F32),
        pltpu.VMEM((2, 8, HEAD, HEAD), BF16),
        pltpu.VMEM((2, 8, HEAD, HEAD), BF16),
        pltpu.VMEM((2, CHIPS, 64, HEAD), BF16),
        pltpu.VMEM((2, CHIPS, 64, HEAD), BF16),
        pltpu.VMEM((2, CHIPS, 64, HEAD), BF16),
        pltpu.VMEM((2, CHIPS, 64, HEAD), BF16),
        pltpu.VMEM((2, 8, HEAD, HEAD), BF16),
        pltpu.VMEM(states, BF16),
        pltpu.VMEM(states, BF16),
        pltpu.VMEM((32, 64, width), BF16),
        pltpu.VMEM((8, length, width), BF16),
        pltpu.VMEM((16, 8, 16, length), BF16),
        pltpu.VMEM((16, 16, 8 * length), BF16),
        pltpu.VMEM((16, 16, width), F32),
        pltpu.VMEM((16, 16, width), BF16),
        pltpu.VMEM((CHUNKS, 2, 8, 16, WIDE // 2), BF16),
        pltpu.VMEM((CHUNKS, 2, 8, 16, WIDE), BF16),
        pltpu.VMEM((CHUNKS, 2, 8, 16, WIDE), BF16),
        pltpu.VMEM((CHUNKS, 8, 16, WIDE), BF16),
        pltpu.VMEM((CHUNKS, 8, 16, WIDE), BF16),
        pltpu.VMEM((CHUNKS, 16, WIDE), BF16),
        pltpu.VMEM((CHUNKS, 8, 16, WIDE), BF16),
        dma((2,)), dma((2,)), dma((2, 16)), dma((2, 16)), dma((2, 16)), dma((2, 16)), dma((2,)), dma((2,)),
        dma((4,)), dma((4,)), dma((4,)), dma((4,)), dma((8, 2)), dma((8, 2)), dma((8, 2)), dma((8, 2)), dma((16,)), dma((16,)),
        dma((2,)), dma((2,)), dma((2,)), dma((2,)), dma((4,)), dma((4,)),
        dma((8,)), dma((8,)),
        dma((CHUNKS, 2)), dma((CHUNKS, 2)), dma((CHUNKS, 2)), dma((CHUNKS, 2)),
        dma((CHUNKS, 8)), dma((CHUNKS, 8)), dma((CHUNKS, 8)), dma((CHUNKS, 8)),
    ]

    def body(*refs):
        kernel(loss_scale, *refs)

    shapes = (block, block, block, block, jax.ShapeDtypeStruct((rows, width), F32))
    results = pl.pallas_call(
        body,
        out_shape=shapes,
        in_specs=[hbm] * 6,
        out_specs=(vmem,) * 5,
        scratch_shapes=scratch,
        compiler_params=pltpu.CompilerParams(
            collective_id=0, has_side_effects=True, vmem_limit_bytes=44 * 1024 * 1024
        ),
        name="layer",
    )(
        *(pltpu.with_memory_space_constraint(a, pltpu.HBM) for a in (query_rows[0], key_rows[0], value_rows[0])),
        pltpu.with_memory_space_constraint(norm_gain.reshape(1, width), pltpu.HBM),
        *(pltpu.with_memory_space_constraint(a, pltpu.HBM) for a in (out_weight, cotangent[0])),
    )
    anywhere = pl.BlockSpec(memory_space=pl.ANY)
    mixed, gq, gk, gv, gw = pl.pallas_call(
        finish,
        out_shape=shapes,
        in_specs=[anywhere] * 5,
        out_specs=(hbm,) * 5,
        scratch_shapes=[dma((5,))],
        compiler_params=pltpu.CompilerParams(vmem_limit_bytes=8 * 1024 * 1024),
        name="finish",
    )(*results)
    return mixed[None], gq[None], gk[None], gv[None], gw


def solution(mesh):
    positions = mesh.shape["dp"] * mesh.shape["ctx"] * HEAD
    loss_scale = 1.0 / math.sqrt(positions)

    def run(*args):
        return on_device(loss_scale, *args)

    split = P("dp", "ctx", None)
    return jax.shard_map(
        run,
        mesh=mesh,
        in_specs=(split, split, split, P(), P("ctx", None), split),
        out_specs=(split, split, split, split, P("ctx", None)),
        check_vma=False,
    )
```
